32 devices in a mesh: dp: 4 (over z), mp: 8 (over y, x, core).
Axes of the slice: x: 2, y: 2, z: 4, core: 2. Of those that a mesh axis runs over, the one named last changes fastest.
Arguments:
- hidden_in: bfloat16 [64, 8192], P(None, 'dp'), may hold values from -25 to 25
- norm_gain: bfloat16 [8192], P('dp'), may hold values from 0.099609375 to 1.8984375
- w_query: bfloat16 [8192, 8192], P('dp', 'mp'), may hold values from -0.0625 to 0.0625
- w_keyval: bfloat16 [8192, 2048], P('dp', 'mp'), may hold values from -0.25 to 0.25
- w_out: bfloat16 [8192, 8192], P('mp', 'dp'), may hold values from -0.5 to 0.5
- cache_slots: bfloat16 [2, 64, 2, 8, 512, 128], P(None, ('dp', 'mp')), may hold values from -140 to 140
- lengths: int32 [64], replicated, may hold values from 1 to 512, 16384 in all
- positions: int32 [64], replicated, may hold values from 0 to 8191
- slot_order: int32 [64], replicated, may hold values from 0 to 63, each once
Outputs:
- result: bfloat16 [64, 8192], P(None, 'dp')
The draws below stay inside these ranges and needn't reach their ends.
Inputs may be any that keep to these rules, and one draw needn't show every extreme that they name: `lengths`: every request has at least one valid cache position; the longest has 512. `slot_order`: each request's cache sits in exactly one slot.
All inputs are finite; a program needn't handle non-finite values.
Results may differ from the reference program's by a relative error of at most 0.035.
Values may be sent and summed in bfloat16 or wider, within the bound.
A program may use at most 128 MiB of HBM per device.

```python
import math
import jax
import jax.numpy as jnp
import numpy as np
from jax import lax

D = 8192
HEADS = 64
KV_HEADS = 8
HEAD_DIM = 128
LAYERS = 2
CACHE = 512
REQUESTS = 64


def draw_hidden_in(key, part):
    first_key, second_key = jax.random.split(key)
    array_shape = (REQUESTS, D)
    columns = 1.0 + 0.8 * lax.broadcasted_iota(jnp.float32, (1, D), 1) / D
    base_draw = jnp.clip(jax.random.normal(first_key, array_shape, jnp.float32), -4.0, 4.0)
    row_scale = jnp.exp(jax.random.uniform(second_key, (REQUESTS, 1), jnp.float32, math.log(0.3), math.log(3.0)))
    return (base_draw * row_scale * columns).astype(jnp.bfloat16)


def draw_cache_slots(key, part):
    array_shape = (LAYERS, REQUESTS, 2, KV_HEADS, CACHE, HEAD_DIM)
    kind_index = lax.broadcasted_iota(jnp.int32, array_shape, 2)
    base_draw = jnp.clip(jax.random.normal(key, array_shape, jnp.float32), -6.0, 6.0)
    key_rows = 2.0 * base_draw
    return jnp.where(kind_index == 0, key_rows, base_draw).astype(jnp.bfloat16)


def touch_ends(entries, own_key, smallest, high):
    index_at = [jax.random.randint(jax.random.fold_in(own_key, axis), (), 0, length) for axis, length in enumerate(entries.shape)]
    main_axis = entries.shape.index(max(entries.shape))
    beside = index_at[:main_axis] + [(index_at[main_axis] + 1) % entries.shape[main_axis]] + index_at[main_axis + 1:]
    return entries.at[tuple(index_at)].set(smallest).at[tuple(beside)].set(high)


def level_of(rng, extent, cuts, smallest, largest):
    def one(position, blocks):
        steps = jax.random.uniform(jax.random.fold_in(jax.random.fold_in(rng, 6), position), (blocks,), jnp.float32, smallest / len(cuts), largest / len(cuts))
        return jnp.repeat(jnp.exp(steps), extent[position] // blocks).reshape((-1,) + (1,) * (len(extent) - position - 1))

    gain = one(*cuts[0])
    for cut in cuts[1:]:
        gain = gain * one(*cut)
    return gain


def length_profile(count, total, bound, lean):
    loads = [(1 << 20) // math.isqrt(grade ** lean) + 1 for grade in range(2, count + 1)]
    spare, given = total - bound - (count - 1), [1] * (count - 1)
    while spare > 0:
        free = [i for i in range(count - 1) if given[i] < bound]
        whole, left = sum([loads[i] for i in free]), spare
        for i in free:
            extra = min(bound - given[i], max(1, left * loads[i] // whole), spare)
            given[i] = given[i] + extra
            spare = spare - extra
    return np.array([bound] + given)


def uneven(rng, amount, total, limit, skew):
    if amount == 2:
        one = jax.random.randint(rng, (), max(1, total - limit), min(limit, total - 1) + 1)
        return jnp.stack([one, total - one])
    sizes = jnp.asarray(length_profile(amount, total, limit, skew), jnp.int32)
    couples = (amount - 1) // 2
    giver, receiver = sizes[1:1 + 2 * couples:2], sizes[2:2 + 2 * couples:2]
    room = jnp.minimum(giver - 1, limit - receiver)
    passed = jax.random.randint(jax.random.fold_in(rng, 1), (couples,), 0, 1 << 20) % (room + 1)
    sizes = sizes.at[1:1 + 2 * couples:2].set(giver - passed).at[2:2 + 2 * couples:2].set(receiver + passed)
    return sizes[jax.random.permutation(jax.random.fold_in(rng, 2), amount)]


def centred(rng, shape, deviation, limit, cuts=(), kind=jnp.bfloat16):
    drawn = jax.random.normal(rng, shape, jnp.float32) * deviation
    if len(cuts) > 0:
        drawn = level_of(rng, shape, cuts, -0.22, 0.18) * drawn
    return jnp.clip(drawn, min=-limit, max=limit).astype(kind)


def setup_inputs(seed: int = 0) -> dict:
    key_of = jax.random.split(jax.random.key(seed), 10)
    hidden_in = draw_hidden_in(jax.random.fold_in(key_of[9], 71), 0)
    norm_gain = jnp.clip(1.0 + 0.18 * jax.random.normal(key_of[1], (D,), jnp.float32), 0.099609375, 1.8984375).astype(jnp.bfloat16)
    w_query = centred(key_of[2], (D, HEADS * HEAD_DIM), D ** -0.5, 0.0625, ((0, 4), (1, 8)))
    w_keyval = centred(key_of[3], (D, 2 * KV_HEADS * HEAD_DIM), (D // 16) ** -0.5, 0.25, ((0, 4), (1, 8)))
    w_out = centred(key_of[4], (HEADS * HEAD_DIM, D), HEAD_DIM ** -0.5, 0.5, ((0, 8), (1, 4)))
    cache_slots = draw_cache_slots(jax.random.fold_in(key_of[9], 71), 0)
    lengths = uneven(key_of[6], REQUESTS, REQUESTS * CACHE // 2, CACHE, 2).astype(jnp.int32)
    positions = touch_ends(jax.random.randint(key_of[7], (REQUESTS,), 0, 8192), jax.random.fold_in(key_of[7], 1), 0, 8191).astype(jnp.int32)
    slot_order = jax.random.permutation(key_of[8], REQUESTS).astype(jnp.int32)
    return {"hidden_in": hidden_in, "norm_gain": norm_gain, "w_query": w_query, "w_keyval": w_keyval, "w_out": w_out, "cache_slots": cache_slots, "lengths": lengths, "positions": positions, "slot_order": slot_order}


norm_eps = 1e-05
rope_base = 500000.0

def rotate(values, at_positions):
    half_dim = values.shape[-1] // 2
    index_row = jnp.arange(half_dim, dtype=jnp.float32)
    frequency = jnp.exp(index_row * (-2.0 * math.log(rope_base) / values.shape[-1]))
    angles = at_positions.astype(jnp.float32)[:, None, None] * frequency
    cosines = jnp.cos(angles)
    sine_rows = jnp.sin(angles)
    first_half = values[..., :half_dim]
    second_half = values[..., half_dim:]
    return jnp.concatenate([first_half * cosines - second_half * sine_rows, second_half * cosines + first_half * sine_rows], axis=-1)

def attend_slot(pieces):
    query_row, key_fresh, value_fresh, length_one, slot_cache = pieces
    group_size = HEADS // KV_HEADS
    queries = query_row.reshape(KV_HEADS, group_size, HEAD_DIM).astype(jnp.float32)
    key_rows = slot_cache[0].astype(jnp.float32)
    values = slot_cache[1].astype(jnp.float32)
    score_scale = 1.0 / math.sqrt(HEAD_DIM)
    scores = jnp.einsum('kgd,ktd->kgt', queries, key_rows) * score_scale
    own_score = jnp.einsum('kgd,kd->kg', queries, key_fresh.astype(jnp.float32)) * score_scale
    valid_keys = jnp.arange(CACHE, dtype=jnp.int32) < length_one
    scores = jnp.where(valid_keys[None, None, :], scores, -jnp.inf)
    highest = jnp.maximum(lax.optimization_barrier(jnp.max(scores, axis=-1)), own_score)
    weights = jnp.exp(scores - highest[..., None])
    own_weight = jnp.exp(own_score - highest)
    denominator = lax.optimization_barrier(jnp.sum(weights, axis=-1)) + own_weight
    rounded = lax.optimization_barrier(weights.astype(jnp.bfloat16)).astype(jnp.float32)
    own_rounded = lax.optimization_barrier(own_weight.astype(jnp.bfloat16)).astype(jnp.float32)
    summed = jnp.einsum('kgt,ktd->kgd', rounded, values) + own_rounded[..., None] * value_fresh.astype(jnp.float32)[:, None, :]
    return (summed / denominator[..., None]).reshape(HEADS * HEAD_DIM).astype(jnp.bfloat16)

def reference(hidden_in, norm_gain, w_query, w_keyval, w_out, cache_slots, lengths, positions, slot_order):
    request_count = hidden_in.shape[0]
    inverse = jnp.zeros((request_count,), jnp.int32).at[slot_order].set(jnp.arange(request_count, dtype=jnp.int32))
    current = hidden_in
    half_width = KV_HEADS * HEAD_DIM
    for layer_index in range(LAYERS):
        floats = current.astype(jnp.float32)
        inverse_rms = lax.rsqrt(lax.optimization_barrier(jnp.sum(floats * floats, axis=1)) / D + norm_eps)
        scaled = (floats * norm_gain.astype(jnp.float32)).astype(jnp.bfloat16)
        query_raw = jnp.dot(scaled, w_query, preferred_element_type=jnp.float32) * inverse_rms[:, None]
        keyval_raw = jnp.dot(scaled, w_keyval, preferred_element_type=jnp.float32) * inverse_rms[:, None]
        queries = rotate(query_raw.reshape(request_count, HEADS, HEAD_DIM), positions).astype(jnp.bfloat16)
        fresh_keys = rotate(keyval_raw[:, :half_width].reshape(request_count, KV_HEADS, HEAD_DIM), positions).astype(jnp.bfloat16)
        fresh_values = keyval_raw[:, half_width:].reshape(request_count, KV_HEADS, HEAD_DIM).astype(jnp.bfloat16)
        slot_out = lax.map(attend_slot, (jnp.take(queries, slot_order, axis=0), jnp.take(fresh_keys, slot_order, axis=0), jnp.take(fresh_values, slot_order, axis=0), jnp.take(lengths, slot_order), cache_slots[layer_index]))
        attended = jnp.take(slot_out, inverse, axis=0)
        projected = jnp.dot(attended, w_out, preferred_element_type=jnp.float32)
        current = (floats + projected).astype(jnp.bfloat16)
    return current
```

```python
import functools
import math

import jax
import jax.numpy as jnp
import numpy as np
from jax import lax
from jax.experimental import pallas as pl
from jax.experimental.pallas import tpu as pltpu
from jax.sharding import PartitionSpec as P

LAYERS = 2


norm_eps = 1e-05
rope_base = 500000.0


def rotate(values, at_positions):
    half_dim = values.shape[-1] // 2
    index_row = jnp.arange(half_dim, dtype=jnp.float32)
    frequency = jnp.exp(index_row * (-2.0 * math.log(rope_base) / values.shape[-1]))
    angles = at_positions.astype(jnp.float32)[:, None, None] * frequency
    cosines = jnp.cos(angles)
    sine_rows = jnp.sin(angles)
    first_half = values[..., :half_dim]
    second_half = values[..., half_dim:]
    return jnp.concatenate(
        [
            first_half * cosines - second_half * sine_rows,
            second_half * cosines + first_half * sine_rows,
        ],
        axis=-1,
    )


def attend(queries, fresh_keys, fresh_values, key_rows, values, slot_lengths):
    score_scale = 1.0 / math.sqrt(queries.shape[-1])
    scores = (
        jnp.einsum("rkgd,rktd->rkgt", queries, key_rows, preferred_element_type=jnp.float32)
        * score_scale
    )
    own_score = (
        jnp.einsum("rkgd,rkd->rkg", queries, fresh_keys, preferred_element_type=jnp.float32)
        * score_scale
    )
    positions_row = lax.broadcasted_iota(jnp.int32, (1, 1, 1, key_rows.shape[2]), 3)
    valid_keys = positions_row < slot_lengths[:, None, None, None]
    scores = jnp.where(valid_keys, scores, -jnp.inf)
    highest = jnp.maximum(jnp.max(scores, axis=-1), own_score)
    weights = jnp.exp(scores - highest[..., None])
    own_weight = jnp.exp(own_score - highest)
    denominator = jnp.sum(weights, axis=-1) + own_weight
    rounded = weights.astype(jnp.bfloat16)
    own_rounded = lax.optimization_barrier(own_weight.astype(jnp.bfloat16)).astype(jnp.float32)
    summed = jnp.einsum("rkgt,rktd->rkgd", rounded, values, preferred_element_type=jnp.float32)
    summed = summed + own_rounded[..., None] * fresh_values.astype(jnp.float32)[:, :, None, :]
    return (summed / denominator[..., None]).astype(jnp.bfloat16)


def shards(
    hidden_in, norm_gain, w_query, w_keyval, w_out, cache_slots, lengths, positions, slot_order
):
    total_rows = hidden_in.shape[0]
    data_count = lax.axis_size("dp")
    model_count = lax.axis_size("mp")
    owned_rows = cache_slots.shape[1]
    key_heads = cache_slots.shape[3]
    head_dim = cache_slots.shape[5]
    query_cols = w_query.shape[1]
    head_count = query_cols * model_count // head_dim
    group_size = head_count // key_heads
    model_width = hidden_in.shape[1] * data_count
    half_width = key_heads * head_dim
    inverse = (
        jnp.zeros((total_rows,), jnp.int32)
        .at[slot_order]
        .set(jnp.arange(total_rows, dtype=jnp.int32))
    )
    device_index = lax.axis_index("dp") * model_count + lax.axis_index("mp")
    slot_lengths = lax.dynamic_slice_in_dim(
        jnp.take(lengths, slot_order), device_index * owned_rows, owned_rows
    )
    slot_positions = lax.dynamic_slice_in_dim(
        jnp.take(positions, slot_order), device_index * owned_rows, owned_rows
    )
    gain_float = norm_gain.astype(jnp.float32)
    current = jnp.take(hidden_in, slot_order, axis=0)
    for layer_index in range(LAYERS):
        floats = current.astype(jnp.float32)
        squares = jnp.sum(floats * floats, axis=1)
        scaled = (floats * gain_float).astype(jnp.bfloat16)
        partial_value = jnp.concatenate(
            [
                jnp.dot(scaled, w_query, preferred_element_type=jnp.float32),
                jnp.dot(scaled, w_keyval, preferred_element_type=jnp.float32),
            ],
            axis=1,
        )
        summed = lax.psum_scatter(partial_value, "dp", scatter_dimension=0, tiled=True)
        square_sum = lax.psum_scatter(squares, "dp", scatter_dimension=0, tiled=True)
        inverse_rms = lax.rsqrt(square_sum / model_width + norm_eps)
        projected = summed * inverse_rms[:, None]
        arrived = lax.all_to_all(projected, "mp", split_axis=0, concat_axis=1, tiled=True)
        arrived = arrived.reshape(owned_rows, model_count, projected.shape[1])
        query_part = arrived[:, :, :query_cols].reshape(owned_rows, head_count, head_dim)
        keyval_part = arrived[:, :, query_cols:].reshape(owned_rows, 2 * half_width)
        queries = (
            rotate(query_part, slot_positions)
            .astype(jnp.bfloat16)
            .reshape(owned_rows, key_heads, group_size, head_dim)
        )
        fresh_keys = rotate(
            keyval_part[:, :half_width].reshape(owned_rows, key_heads, head_dim), slot_positions
        ).astype(jnp.bfloat16)
        fresh_values = (
            keyval_part[:, half_width:]
            .reshape(owned_rows, key_heads, head_dim)
            .astype(jnp.bfloat16)
        )
        layer_cache = cache_slots[layer_index]
        attended = attend(
            queries, fresh_keys, fresh_values, layer_cache[:, 0], layer_cache[:, 1], slot_lengths
        )
        attended = attended.reshape(owned_rows, head_count * head_dim)
        returned = lax.all_to_all(attended, "mp", split_axis=1, concat_axis=0, tiled=True)
        partial_out = jnp.dot(
            lax.all_gather(returned, "dp", axis=0, tiled=True),
            w_out,
            preferred_element_type=jnp.float32,
        )
        totals = lax.psum(partial_out, "mp")
        current = (floats + totals).astype(jnp.bfloat16)
    return jnp.take(current, inverse, axis=0)


LINK = jnp.bfloat16


def flipped(at, mask, bits):
    turned_at = 0
    for b in range(bits):
        bit = (at // (1 << b)) % 2
        if (mask >> b) & 1:
            bit = 1 - bit
        turned_at = turned_at + bit * (1 << b)
    return turned_at


def fused_kernel(
    sizes,
    slot_hbm,
    length_hbm,
    position_hbm,
    slot_row_hbm,
    frequency_hbm,
    hidden_hbm,
    gain_hbm,
    wq_hbm,
    wkv_hbm,
    wo_hbm,
    cache_hbm,
    out_ref,
    slot_s,
    length_s,
    position_s,
    slot_row,
    frequency_ref,
    hidden_ref,
    gain_ref,
    wq,
    wkv,
    wo,
    cache,
    state,
    scaled,
    square_send,
    square_recv,
    kv_own,
    kv_send,
    kv_recv,
    row_send,
    row_recv,
    fresh_buf,
    stage,
    q_send,
    q_recv,
    att_send,
    gathered,
    att_stage,
    pair_send,
    pair_recv,
    first_send,
    first_recv,
    second_send,
    second_recv,
    small_sem,
    load_sem,
    sq_ssem,
    sq_rsem,
    kv_ssem,
    kv_rsem,
    rw_ssem,
    rw_rsem,
    qu_ssem,
    qu_rsem,
    at_ssem,
    at_rsem,
    pq_ssem,
    pq_rsem,
    fi_ssem,
    fi_rsem,
    se_ssem,
    se_rsem,
    st_ssem,
    st_rsem,
):
    n_dp, n_mp, rows, width, query_cols, keyval_cols, owned, key_heads, head_dim = sizes
    band = rows // n_dp
    chunk = width // n_mp
    group = query_cols // head_dim
    packed = owned * group
    half = n_mp // 2
    d_bits, m_bits = n_dp.bit_length() - 1, n_mp.bit_length() - 1
    f32, bf16 = jnp.float32, jnp.bfloat16
    d = lax.axis_index("dp")
    m = lax.axis_index("mp")
    model_width = width * n_dp
    core = lax.rem(m, 2)
    sibling = m + 1 - 2 * core
    score_scale = 1.0 / math.sqrt(head_dim)
    others = [
        (kd, km) for kd in reversed(range(n_dp)) for km in reversed(range(n_mp)) if kd or km
    ]
    place_of = {
        (kd, km): {"dp": flipped(d, kd, d_bits), "mp": flipped(m, km, m_bits)}
        for kd, km in others
    }

    barrier = pltpu.get_barrier_semaphore()
    for pair in others:
        pl.semaphore_signal(
            barrier, inc=1, device_id=place_of[pair], device_id_type=pl.DeviceIdType.MESH
        )

    small = [
        pltpu.make_async_copy(src, dst, small_sem.at[i])
        for i, (src, dst) in enumerate(
            [
                (slot_row_hbm, slot_row),
                (hidden_hbm, hidden_ref),
                (gain_hbm, gain_ref),
                (slot_hbm, slot_s),
                (length_hbm, length_s),
                (position_hbm, position_s),
                (frequency_hbm, frequency_ref),
            ]
        )
    ]
    loads = [
        pltpu.make_async_copy(wkv_hbm, wkv, load_sem.at[0]),
        pltpu.make_async_copy(wq_hbm, wq, load_sem.at[1]),
        pltpu.make_async_copy(cache_hbm.at[0], cache.at[0], load_sem.at[2]),
    ]
    for j in range(n_mp):
        loads.append(
            pltpu.make_async_copy(
                wo_hbm.at[:, pl.ds(j * chunk, chunk)], wo.at[j], load_sem.at[3 + j]
            )
        )
    for layer in range(1, LAYERS):
        loads.append(
            pltpu.make_async_copy(
                cache_hbm.at[layer], cache.at[layer], load_sem.at[2 + n_mp + layer]
            )
        )
    for one in small + loads:
        one.start()

    for one in small:
        one.wait()
    sublanes = lax.broadcasted_iota(jnp.int32, (rows, rows), 0)
    place = jnp.where(slot_row[...] == sublanes, 1.0, 0.0).astype(bf16)
    gains = gain_ref[...].astype(f32)
    for c in range(n_mp):
        state[0, c] = lax.dot_general(
            place,
            hidden_ref[:, c * chunk : (c + 1) * chunk],
            (((0,), (0,)), ((), ())),
            preferred_element_type=f32,
        ).astype(bf16)

    turns = []
    for r in range(owned):
        slot = slot_s[(d * n_mp + m) * owned + r]
        at = jnp.full((group, head_dim), position_s[slot], jnp.int32).astype(f32)
        angles = at * frequency_ref[...]
        lane = lax.broadcasted_iota(jnp.int32, (group, head_dim), 1)
        sines = jnp.sin(angles)
        turns.append(
            (jnp.cos(angles), jnp.where(lane < head_dim // 2, -sines, sines), length_s[slot])
        )

    sends = []

    def remote(src, dst, ssem, rsem, where):
        copy = pltpu.make_async_remote_copy(
            src_ref=src,
            dst_ref=dst,
            send_sem=ssem,
            recv_sem=rsem,
            device_id=where,
            device_id_type=pl.DeviceIdType.MESH,
        )
        copy.start()
        sends.append(copy)
        return copy

    def scale(layer):
        squares = jnp.zeros((rows, 128), f32)
        for c in range(n_mp):
            floats = state[layer, c].astype(f32)
            for t in range(chunk // 128):
                piece = floats[:, t * 128 : (t + 1) * 128]
                at = c * (chunk // 128) + t
                scaled[:, at * 128 : (at + 1) * 128] = (piece * gains[at : at + 1]).astype(bf16)
                squares = squares + piece * piece
        square_row = jnp.broadcast_to(jnp.sum(squares, axis=1, keepdims=True), (rows, 128))
        for i in range(n_dp):
            for j in range(n_mp):
                at = (i * n_mp + j) * owned
                square_send[layer, i, j] = square_row[at : at + owned]

    def project(layer):
        if layer == 0:
            loads[0].wait()
        product = jnp.dot(scaled[...], wkv[...], preferred_element_type=f32)
        product = product.reshape(n_dp, band, keyval_cols)
        kv_own[...] = product
        kv_send[layer] = product.astype(bf16)
        if layer == 0:
            loads[1].wait()
        wide = 256
        for b in range(query_cols // wide):
            product = jnp.dot(
                scaled[...], wq[:, b * wide : (b + 1) * wide], preferred_element_type=f32
            )
            for t in range(wide // head_dim):
                g = b * (wide // head_dim) + t
                stage[:, g, :] = product[:, t * head_dim : (t + 1) * head_dim]
        q_send[layer] = stage[...].reshape(n_dp, n_mp, packed, head_dim).astype(bf16)

    scale(0)
    project(0)
    pl.semaphore_wait(barrier, len(others))

    for layer in range(LAYERS):
        kv_copies, square_copies, q_copies = [], [], {}
        for kd in reversed(range(1, n_dp)):
            to = flipped(d, kd, d_bits)
            kv_copies.append(
                remote(
                    kv_send.at[layer, to],
                    kv_recv.at[layer, kd - 1],
                    kv_ssem.at[layer, kd - 1],
                    kv_rsem.at[layer, kd - 1],
                    {"dp": to},
                )
            )
        for kd in reversed(range(1, n_dp)):
            to = flipped(d, kd, d_bits)
            square_copies.append(
                remote(
                    square_send.at[layer, to, m],
                    square_recv.at[layer, kd - 1],
                    sq_ssem.at[layer, kd - 1],
                    sq_rsem.at[layer, kd - 1],
                    {"dp": to},
                )
            )
        for kd, km in others:
            where = place_of[kd, km]
            q_copies[kd, km] = remote(
                q_send.at[layer, where["dp"], where["mp"]],
                q_recv.at[layer, d, m],
                qu_ssem.at[layer, kd, km],
                qu_rsem.at[layer, kd, km],
                where,
            )
        q_recv[layer, d, m] = q_send[layer, d, m]
        for copy in kv_copies:
            copy.wait_recv()
        total = kv_own[d]
        for kd in range(1, n_dp):
            total = total + kv_recv[layer, kd - 1].astype(f32)
        for j in range(n_mp):
            row_send[layer, j] = total[j * owned : (j + 1) * owned]
        row_copies = []
        for km in reversed(range(1, n_mp)):
            to = flipped(m, km, m_bits)
            row_copies.append(
                remote(
                    row_send.at[layer, to],
                    row_recv.at[layer, m],
                    rw_ssem.at[layer, km - 1],
                    rw_rsem.at[layer, km - 1],
                    {"mp": to},
                )
            )
        row_recv[layer, m] = row_send[layer, m]
        for copy in square_copies:
            copy.wait_recv()
        square_sum = square_send[layer, d, m]
        for kd in range(1, n_dp):
            square_sum = square_sum + square_recv[layer, kd - 1]
        inverse_rms = lax.rsqrt(square_sum / model_width + norm_eps)

        def turned(x, r):
            cosines, sines, _ = turns[r]
            return x * cosines + pltpu.roll(x, head_dim // 2, 1) * sines

        if layer == 0:
            loads[2].wait()
        else:
            loads[2 + n_mp + layer].wait()
        for pair in others:
            q_copies[pair].wait_recv()
        for copy in row_copies:
            copy.wait_recv()
        per = keyval_cols // head_dim
        key_sources = key_heads // per
        for r in range(owned):
            for t in range(per):
                fresh = (
                    row_recv[layer, :, r, t * head_dim : (t + 1) * head_dim]
                    * inverse_rms[r : r + 1]
                )
                keys_fresh = turned(fresh, r)
                for source in range(n_mp):
                    kind = source // key_sources
                    head = (source % key_sources) * per + t
                    row = keys_fresh if kind == 0 else fresh
                    fresh_buf[r, kind, head] = row[source : source + 1]
        results = []
        for r in range(owned):
            length = turns[r][2]
            parts = []
            for h in range(key_heads):
                raw = q_recv[layer, 0, h].astype(f32)
                for i in range(1, n_dp):
                    raw = raw + q_recv[layer, i, h].astype(f32)
                raw = raw[r * group : (r + 1) * group] * inverse_rms[r : r + 1]
                parts.append(turned(raw, r)[None])
            queries = jnp.concatenate(parts, axis=0).astype(bf16)
            fresh_keys = fresh_buf[r, 0].astype(bf16).astype(f32)
            fresh_values = fresh_buf[r, 1].astype(bf16).astype(f32)
            key_rows = cache[layer, r, 0]
            value_rows = cache[layer, r, 1]
            scores = (
                lax.dot_general(
                    queries,
                    key_rows,
                    (((2,), (2,)), ((0,), (0,))),
                    preferred_element_type=f32,
                )
                * score_scale
            )
            own_score = (
                jnp.sum(queries.astype(f32) * fresh_keys, axis=2, keepdims=True) * score_scale
            )
            at = lax.broadcasted_iota(jnp.int32, scores.shape, 2)
            scores = jnp.where(at < length, scores, -jnp.inf)
            highest = jnp.maximum(jnp.max(scores, axis=2, keepdims=True), own_score)
            weights = jnp.exp(scores - highest)
            own_weight = jnp.exp(own_score - highest)
            denominator = jnp.sum(weights, axis=2, keepdims=True) + own_weight
            summed = lax.dot_general(
                weights.astype(bf16),
                value_rows,
                (((2,), (1,)), ((0,), (0,))),
                preferred_element_type=f32,
            )
            own_rounded = own_weight.astype(bf16).astype(f32)
            summed = summed + own_rounded * fresh_values
            results.append(summed / denominator)
        att_send[layer] = jnp.concatenate(results, axis=1).astype(bf16)
        att_copies = []
        for kd, km in others:
            where = place_of[kd, km]
            att_copies.append(
                remote(
                    att_send.at[layer, where["mp"]],
                    gathered.at[layer, d, m],
                    at_ssem.at[layer, kd, km],
                    at_rsem.at[layer, kd, km],
                    where,
                )
            )
        gathered[layer, d, m] = att_send[layer, m]
        if layer == 0:
            for j in range(n_mp):
                loads[3 + j].wait()
        for copy in att_copies:
            copy.wait_recv()
        att_stage[...] = gathered[layer].astype(f32).reshape(rows, group, head_dim)
        left = jnp.concatenate(
            [att_stage[:, g, :].astype(bf16) for g in range(group)], axis=1
        )
        pair_copies = []
        for q in range(half):
            pair_send[layer, q] = jnp.dot(
                left, wo[(1 - core) * half + q], preferred_element_type=f32
            )
            pair_copies.append(
                remote(
                    pair_send.at[layer, q],
                    pair_recv.at[layer, q],
                    pq_ssem.at[layer, q],
                    pq_rsem.at[layer, q],
                    {"mp": sibling},
                )
            )
        first_copies = []
        for q in range(half):
            product = jnp.dot(left, wo[core * half + q], preferred_element_type=f32)
            pair_copies[q].wait_recv()
            first_send[layer, q] = (product + pair_recv[layer, q]).astype(LINK)
            first_copies.append(
                remote(
                    first_send.at[layer, q],
                    first_recv.at[layer, q],
                    fi_ssem.at[layer, q],
                    fi_rsem.at[layer, q],
                    {"mp": flipped(m, 2 if q % 2 == 0 else 4, m_bits)},
                )
            )
        second_copies = []
        for q in range(half):
            first_copies[q].wait_recv()
            both = first_send[layer, q].astype(f32) + first_recv[layer, q].astype(f32)
            second_send[layer, q] = both.astype(LINK)
            second_copies.append(
                remote(
                    second_send.at[layer, q],
                    second_recv.at[layer, q],
                    se_ssem.at[layer, q],
                    se_rsem.at[layer, q],
                    {"mp": flipped(m, 4 if q % 2 == 0 else 2, m_bits)},
                )
            )
        arriving = []
        for q in range(half):
            second_copies[q].wait_recv()
            at = core * half + q
            total = second_send[layer, q].astype(f32) + second_recv[layer, q].astype(f32)
            state[layer + 1, at] = (state[layer, at].astype(f32) + total).astype(bf16)
            arriving.append(
                remote(
                    state.at[layer + 1, at],
                    state.at[layer + 1, at],
                    st_ssem.at[layer, q],
                    st_rsem.at[layer, q],
                    {"mp": sibling},
                )
            )
        for copy in arriving:
            copy.wait_recv()
        if layer + 1 < LAYERS:
            scale(layer + 1)
            project(layer + 1)
    for c in range(n_mp):
        out_ref[:, c * chunk : (c + 1) * chunk] = jnp.dot(
            place, state[LAYERS, c], preferred_element_type=f32
        ).astype(bf16)
    for copy in sends:
        copy.wait_send()


def fused(
    hidden_in, norm_gain, w_query, w_keyval, w_out, cache_slots, lengths, positions, slot_order
):
    n_dp = lax.axis_size("dp")
    n_mp = lax.axis_size("mp")
    rows, width = hidden_in.shape
    query_cols = w_query.shape[1]
    keyval_cols = w_keyval.shape[1]
    owned, key_heads, cache_rows, head_dim = (
        cache_slots.shape[1],
        cache_slots.shape[3],
        cache_slots.shape[4],
        cache_slots.shape[5],
    )
    group = query_cols // head_dim
    packed = owned * group
    band = rows // n_dp
    chunk = width // n_mp
    half = n_mp // 2
    index_row = np.arange(head_dim) % (head_dim // 2)
    frequency = np.exp(index_row * (-2.0 * math.log(rope_base) / head_dim))
    frequency = jnp.asarray(frequency[None].astype(np.float32))
    sizes = (n_dp, n_mp, rows, width, query_cols, keyval_cols, owned, key_heads, head_dim)
    vmem = pl.BlockSpec(memory_space=pltpu.VMEM)
    anywhere = pl.BlockSpec(memory_space=pl.ANY)
    f32, bf16 = jnp.float32, jnp.bfloat16
    dma = pltpu.SemaphoreType.DMA
    return pl.pallas_call(
        functools.partial(fused_kernel, sizes),
        out_shape=jax.ShapeDtypeStruct((rows, width), bf16),
        in_specs=[anywhere] * 11,
        out_specs=vmem,
        scratch_shapes=[
            pltpu.SMEM((rows,), jnp.int32),
            pltpu.SMEM((rows,), jnp.int32),
            pltpu.SMEM((rows,), jnp.int32),
            pltpu.VMEM((1, rows), jnp.int32),
            pltpu.VMEM((1, head_dim), f32),
            pltpu.VMEM((rows, width), bf16),
            pltpu.VMEM((width // 128, 128), bf16),
            pltpu.VMEM(w_query.shape, bf16),
            pltpu.VMEM(w_keyval.shape, bf16),
            pltpu.VMEM((n_mp, query_cols, chunk), bf16),
            pltpu.VMEM(cache_slots.shape, bf16),
            pltpu.VMEM((LAYERS + 1, n_mp, rows, chunk), bf16),
            pltpu.VMEM((rows, width), bf16),
            pltpu.VMEM((LAYERS, n_dp, n_mp, owned, 128), f32),
            pltpu.VMEM((LAYERS, n_dp - 1, owned, 128), f32),
            pltpu.VMEM((n_dp, band, keyval_cols), f32),
            pltpu.VMEM((LAYERS, n_dp, band, keyval_cols), LINK),
            pltpu.VMEM((LAYERS, n_dp - 1, band, keyval_cols), LINK),
            pltpu.VMEM((LAYERS, n_mp, owned, keyval_cols), f32),
            pltpu.VMEM((LAYERS, n_mp, owned, keyval_cols), f32),
            pltpu.VMEM((owned, 2, key_heads, 1, head_dim), f32),
            pltpu.VMEM((rows, group, head_dim), f32),
            pltpu.VMEM((LAYERS, n_dp, n_mp, packed, head_dim), LINK),
            pltpu.VMEM((LAYERS, n_dp, n_mp, packed, head_dim), LINK),
            pltpu.VMEM((LAYERS, n_mp, packed, head_dim), bf16),
            pltpu.VMEM((LAYERS, n_dp, n_mp, packed, head_dim), bf16),
            pltpu.VMEM((rows, group, head_dim), f32),
            pltpu.VMEM((LAYERS, half, rows, chunk), f32),
            pltpu.VMEM((LAYERS, half, rows, chunk), f32),
            pltpu.VMEM((LAYERS, half, rows, chunk), LINK),
            pltpu.VMEM((LAYERS, half, rows, chunk), LINK),
            pltpu.VMEM((LAYERS, half, rows, chunk), LINK),
            pltpu.VMEM((LAYERS, half, rows, chunk), LINK),
            dma((7,)),
            dma((2 + n_mp + LAYERS,)),
            dma((LAYERS, n_dp - 1)),
            dma((LAYERS, n_dp - 1)),
            dma((LAYERS, n_dp - 1)),
            dma((LAYERS, n_dp - 1)),
            dma((LAYERS, n_mp - 1)),
            dma((LAYERS, n_mp - 1)),
            dma((LAYERS, n_dp, n_mp)),
            dma((LAYERS, n_dp, n_mp)),
            dma((LAYERS, n_dp, n_mp)),
            dma((LAYERS, n_dp, n_mp)),
            dma((LAYERS, half)),
            dma((LAYERS, half)),
            dma((LAYERS, half)),
            dma((LAYERS, half)),
            dma((LAYERS, half)),
            dma((LAYERS, half)),
            dma((LAYERS, half)),
            dma((LAYERS, half)),
        ],
        compiler_params=pltpu.CompilerParams(
            collective_id=0, has_side_effects=True, vmem_limit_bytes=56 << 20
        ),
    )(
        slot_order,
        lengths,
        positions,
        slot_order.reshape(1, rows),
        frequency,
        hidden_in,
        norm_gain.reshape(width // 128, 128),
        w_query,
        w_keyval,
        w_out,
        cache_slots,
    )


def dispatch(
    hidden_in, norm_gain, w_query, w_keyval, w_out, cache_slots, lengths, positions, slot_order
):
    n_mp = lax.axis_size("mp")
    key_heads = cache_slots.shape[3]
    head_dim = cache_slots.shape[5]
    fits = (
        key_heads == n_mp
        and n_mp == 8
        and lax.axis_size("dp") == 4
        and cache_slots.shape[1] * (w_query.shape[1] // head_dim) % 16 == 0
        and (w_query.shape[1] // head_dim) == 8
        and w_keyval.shape[1] % head_dim == 0
        and w_query.shape[1] % w_keyval.shape[1] == 0
        and hidden_in.shape[1] % (128 * n_mp) == 0
        and hidden_in.shape[0] % (16 * lax.axis_size("dp")) == 0
    )
    chosen = fused if fits else shards
    return chosen(
        hidden_in, norm_gain, w_query, w_keyval, w_out, cache_slots, lengths, positions, slot_order
    )


def solution(mesh):
    placed = (
        P(None, "dp"),
        P("dp"),
        P("dp", "mp"),
        P("dp", "mp"),
        P("mp", "dp"),
        P(None, ("dp", "mp"), None, None, None, None),
        P(),
        P(),
        P(),
    )
    return jax.shard_map(
        dispatch, mesh=mesh, in_specs=placed, out_specs=P(None, "dp"), check_vma=False
    )
```

```python
import functools
import math

import jax
import jax.numpy as jnp
import numpy as np
from jax import lax
from jax.experimental import pallas as pl
from jax.experimental.pallas import tpu as pltpu
from jax.sharding import PartitionSpec as P

LAYERS = 2


norm_eps = 1e-05
rope_base = 500000.0


def rotate(values, at_positions):
    half_dim = values.shape[-1] // 2
    index_row = jnp.arange(half_dim, dtype=jnp.float32)
    frequency = jnp.exp(index_row * (-2.0 * math.log(rope_base) / values.shape[-1]))
    angles = at_positions.astype(jnp.float32)[:, None, None] * frequency
    cosines = jnp.cos(angles)
    sine_rows = jnp.sin(angles)
    first_half = values[..., :half_dim]
    second_half = values[..., half_dim:]
    return jnp.concatenate(
        [
            first_half * cosines - second_half * sine_rows,
            second_half * cosines + first_half * sine_rows,
        ],
        axis=-1,
    )


def attend(queries, fresh_keys, fresh_values, key_rows, values, slot_lengths):
    score_scale = 1.0 / math.sqrt(queries.shape[-1])
    scores = (
        jnp.einsum("rkgd,rktd->rkgt", queries, key_rows, preferred_element_type=jnp.float32)
        * score_scale
    )
    own_score = (
        jnp.einsum("rkgd,rkd->rkg", queries, fresh_keys, preferred_element_type=jnp.float32)
        * score_scale
    )
    positions_row = lax.broadcasted_iota(jnp.int32, (1, 1, 1, key_rows.shape[2]), 3)
    valid_keys = positions_row < slot_lengths[:, None, None, None]
    scores = jnp.where(valid_keys, scores, -jnp.inf)
    highest = jnp.maximum(jnp.max(scores, axis=-1), own_score)
    weights = jnp.exp(scores - highest[..., None])
    own_weight = jnp.exp(own_score - highest)
    denominator = jnp.sum(weights, axis=-1) + own_weight
    rounded = weights.astype(jnp.bfloat16)
    own_rounded = lax.optimization_barrier(own_weight.astype(jnp.bfloat16)).astype(jnp.float32)
    summed = jnp.einsum("rkgt,rktd->rkgd", rounded, values, preferred_element_type=jnp.float32)
    summed = summed + own_rounded[..., None] * fresh_values.astype(jnp.float32)[:, :, None, :]
    return (summed / denominator[..., None]).astype(jnp.bfloat16)


def shards(
    hidden_in, norm_gain, w_query, w_keyval, w_out, cache_slots, lengths, positions, slot_order
):
    total_rows = hidden_in.shape[0]
    data_count = lax.axis_size("dp")
    model_count = lax.axis_size("mp")
    owned_rows = cache_slots.shape[1]
    key_heads = cache_slots.shape[3]
    head_dim = cache_slots.shape[5]
    query_cols = w_query.shape[1]
    head_count = query_cols * model_count // head_dim
    group_size = head_count // key_heads
    model_width = hidden_in.shape[1] * data_count
    half_width = key_heads * head_dim
    inverse = (
        jnp.zeros((total_rows,), jnp.int32)
        .at[slot_order]
        .set(jnp.arange(total_rows, dtype=jnp.int32))
    )
    device_index = lax.axis_index("dp") * model_count + lax.axis_index("mp")
    slot_lengths = lax.dynamic_slice_in_dim(
        jnp.take(lengths, slot_order), device_index * owned_rows, owned_rows
    )
    slot_positions = lax.dynamic_slice_in_dim(
        jnp.take(positions, slot_order), device_index * owned_rows, owned_rows
    )
    gain_float = norm_gain.astype(jnp.float32)
    current = jnp.take(hidden_in, slot_order, axis=0)
    for layer_index in range(LAYERS):
        floats = current.astype(jnp.float32)
        squares = jnp.sum(floats * floats, axis=1)
        scaled = (floats * gain_float).astype(jnp.bfloat16)
        partial_value = jnp.concatenate(
            [
                jnp.dot(scaled, w_query, preferred_element_type=jnp.float32),
                jnp.dot(scaled, w_keyval, preferred_element_type=jnp.float32),
            ],
            axis=1,
        )
        summed = lax.psum_scatter(partial_value, "dp", scatter_dimension=0, tiled=True)
        square_sum = lax.psum_scatter(squares, "dp", scatter_dimension=0, tiled=True)
        inverse_rms = lax.rsqrt(square_sum / model_width + norm_eps)
        projected = summed * inverse_rms[:, None]
        arrived = lax.all_to_all(projected, "mp", split_axis=0, concat_axis=1, tiled=True)
        arrived = arrived.reshape(owned_rows, model_count, projected.shape[1])
        query_part = arrived[:, :, :query_cols].reshape(owned_rows, head_count, head_dim)
        keyval_part = arrived[:, :, query_cols:].reshape(owned_rows, 2 * half_width)
        queries = (
            rotate(query_part, slot_positions)
            .astype(jnp.bfloat16)
            .reshape(owned_rows, key_heads, group_size, head_dim)
        )
        fresh_keys = rotate(
            keyval_part[:, :half_width].reshape(owned_rows, key_heads, head_dim), slot_positions
        ).astype(jnp.bfloat16)
        fresh_values = (
            keyval_part[:, half_width:]
            .reshape(owned_rows, key_heads, head_dim)
            .astype(jnp.bfloat16)
        )
        layer_cache = cache_slots[layer_index]
        attended = attend(
            queries, fresh_keys, fresh_values, layer_cache[:, 0], layer_cache[:, 1], slot_lengths
        )
        attended = attended.reshape(owned_rows, head_count * head_dim)
        returned = lax.all_to_all(attended, "mp", split_axis=1, concat_axis=0, tiled=True)
        partial_out = jnp.dot(
            lax.all_gather(returned, "dp", axis=0, tiled=True),
            w_out,
            preferred_element_type=jnp.float32,
        )
        totals = lax.psum(partial_out, "mp")
        current = (floats + totals).astype(jnp.bfloat16)
    return jnp.take(current, inverse, axis=0)


LINK = jnp.bfloat16


def flipped(at, mask, bits):
    turned_at = 0
    for b in range(bits):
        bit = (at // (1 << b)) % 2
        if (mask >> b) & 1:
            bit = 1 - bit
        turned_at = turned_at + bit * (1 << b)
    return turned_at


def fused_kernel(
    sizes,
    slot_hbm,
    length_hbm,
    position_hbm,
    slot_row_hbm,
    frequency_hbm,
    hidden_hbm,
    gain_hbm,
    wq_hbm,
    wkv_hbm,
    wo_hbm,
    cache_hbm,
    out_ref,
    slot_s,
    length_s,
    position_s,
    slot_row,
    frequency_ref,
    hidden_ref,
    gain_ref,
    wq,
    wkv,
    wo,
    cache,
    state,
    square_send,
    square_recv,
    sums,
    square_sum_buf,
    gain_rows,
    kv_send,
    kv_recv,
    row_send,
    row_recv,
    fresh_buf,
    stage,
    q_send,
    q_recv,
    att_send,
    gathered,
    att_stage,
    pair_send,
    pair_recv,
    first_send,
    first_recv,
    second_send,
    second_recv,
    small_sem,
    load_sem,
    sq_ssem,
    sq_rsem,
    kv_ssem,
    kv_rsem,
    rw_ssem,
    rw_rsem,
    qu_ssem,
    qu_rsem,
    at_ssem,
    at_rsem,
    pq_ssem,
    pq_rsem,
    fi_ssem,
    fi_rsem,
    se_ssem,
    se_rsem,
    st_ssem,
    st_rsem,
):
    n_dp, n_mp, rows, width, query_cols, keyval_cols, owned, key_heads, head_dim = sizes
    band = rows // n_dp
    chunk = width // n_mp
    group = query_cols // head_dim
    packed = owned * group
    half = n_mp // 2
    d_bits, m_bits = n_dp.bit_length() - 1, n_mp.bit_length() - 1
    f32, bf16 = jnp.float32, jnp.bfloat16
    d = lax.axis_index("dp")
    m = lax.axis_index("mp")
    model_width = width * n_dp
    core = lax.rem(m, 2)
    sibling = m + 1 - 2 * core
    score_scale = 1.0 / math.sqrt(head_dim)
    others = [
        (kd, km) for kd in reversed(range(n_dp)) for km in reversed(range(n_mp)) if kd or km
    ]
    place_of = {
        (kd, km): {"dp": flipped(d, kd, d_bits), "mp": flipped(m, km, m_bits)}
        for kd, km in others
    }

    barrier = pltpu.get_barrier_semaphore()
    for pair in others:
        pl.semaphore_signal(
            barrier, inc=1, device_id=place_of[pair], device_id_type=pl.DeviceIdType.MESH
        )

    small = [
        pltpu.make_async_copy(src, dst, small_sem.at[i])
        for i, (src, dst) in enumerate(
            [
                (slot_row_hbm, slot_row),
                (hidden_hbm, hidden_ref),
                (gain_hbm, gain_ref),
                (slot_hbm, slot_s),
                (length_hbm, length_s),
                (position_hbm, position_s),
                (frequency_hbm, frequency_ref),
            ]
        )
    ]
    loads = [
        pltpu.make_async_copy(wkv_hbm, wkv, load_sem.at[0]),
        pltpu.make_async_copy(wq_hbm, wq, load_sem.at[1]),
        pltpu.make_async_copy(cache_hbm.at[0], cache.at[0], load_sem.at[2]),
    ]
    for j in range(n_mp):
        loads.append(
            pltpu.make_async_copy(
                wo_hbm.at[:, pl.ds(j * chunk, chunk)], wo.at[j], load_sem.at[3 + j]
            )
        )
    for layer in range(1, LAYERS):
        loads.append(
            pltpu.make_async_copy(
                cache_hbm.at[layer], cache.at[layer], load_sem.at[2 + n_mp + layer]
            )
        )
    for one in small + loads[:2]:
        one.start()

    for one in small:
        one.wait()
    sublanes = lax.broadcasted_iota(jnp.int32, (rows, rows), 0)
    place = jnp.where(slot_row[...] == sublanes, 1.0, 0.0).astype(bf16)
    gains = gain_ref[...].astype(f32)
    for c in range(n_mp):
        state[0, c] = lax.dot_general(
            place,
            hidden_ref[:, c * chunk : (c + 1) * chunk],
            (((0,), (0,)), ((), ())),
            preferred_element_type=f32,
        ).astype(bf16)

    turns = []
    for r in range(owned):
        slot = slot_s[(d * n_mp + m) * owned + r]
        at = jnp.full((group, head_dim), position_s[slot], jnp.int32).astype(f32)
        angles = at * frequency_ref[...]
        lane = lax.broadcasted_iota(jnp.int32, (group, head_dim), 1)
        sines = jnp.sin(angles)
        turns.append(
            (jnp.cos(angles), jnp.where(lane < head_dim // 2, -sines, sines), length_s[slot])
        )

    sends = []

    def remote(src, dst, ssem, rsem, where):
        copy = pltpu.make_async_remote_copy(
            src_ref=src,
            dst_ref=dst,
            send_sem=ssem,
            recv_sem=rsem,
            device_id=where,
            device_id_type=pl.DeviceIdType.MESH,
        )
        copy.start()
        sends.append(copy)
        return copy

    def gather_chunks(layer, places, fresh_start):
        squares = square_sum_buf[...]
        pieces = []
        for c in places:
            floats = state[layer, c].astype(f32)
            for t in range(chunk // 128):
                piece = floats[:, t * 128 : (t + 1) * 128]
                pieces.append((piece * gain_rows[c, t]).astype(bf16))
                squares = squares + piece * piece
        square_sum_buf[...] = squares
        depth = len(places) * chunk
        start = places[0] * chunk
        if not isinstance(start, int):
            start = pl.multiple_of(start, chunk)
        left = jnp.concatenate(pieces, axis=1)
        wide = 256
        for b in range(-1, query_cols // wide):
            if b < 0:
                weights = wkv[pl.ds(start, depth), :]
                at = query_cols
                span = keyval_cols
            else:
                weights = wq[pl.ds(start, depth), b * wide : (b + 1) * wide]
                at = b * wide
                span = wide
            product = jnp.dot(left, weights, preferred_element_type=f32)
            if fresh_start:
                sums[:, at : at + span] = product
            else:
                sums[:, at : at + span] += product

    def prepare(layer):
        square_row = jnp.broadcast_to(
            jnp.sum(square_sum_buf[...], axis=1, keepdims=True), (rows, 128)
        )
        product = sums[:, query_cols:].reshape(n_dp, band, keyval_cols)
        kv_send[layer] = product.astype(bf16)
        for g in range(group):
            stage[:, g, :] = sums[:, g * head_dim : (g + 1) * head_dim]
        q_send[layer] = stage[...].reshape(n_dp, n_mp, packed, head_dim).astype(bf16)
        for i in range(n_dp):
            for j in range(n_mp):
                at = (i * n_mp + j) * owned
                square_send[layer, i, j] = square_row[at : at + owned]

    for c in range(n_mp):
        for t in range(chunk // 128):
            at = c * (chunk // 128) + t
            gain_rows[c, t] = gains[at : at + 1]
    square_sum_buf[...] = jnp.zeros((rows, 128), f32)
    for one in loads[:2]:
        one.wait()
    for one in loads[2:]:
        one.start()
    gather_chunks(0, list(range(n_mp)), True)
    prepare(0)
    pl.semaphore_wait(barrier, len(others))

    for layer in range(LAYERS):
        kv_copies, square_copies, q_copies = [], [], {}
        for kd in reversed(range(1, n_dp)):
            to = flipped(d, kd, d_bits)
            kv_copies.append(
                remote(
                    kv_send.at[layer, to],
                    kv_recv.at[layer, kd - 1],
                    kv_ssem.at[layer, kd - 1],
                    kv_rsem.at[layer, kd - 1],
                    {"dp": to},
                )
            )
        for kd in reversed(range(1, n_dp)):
            to = flipped(d, kd, d_bits)
            square_copies.append(
                remote(
                    square_send.at[layer, to, m],
                    square_recv.at[layer, kd - 1],
                    sq_ssem.at[layer, kd - 1],
                    sq_rsem.at[layer, kd - 1],
                    {"dp": to},
                )
            )
        for kd, km in others:
            where = place_of[kd, km]
            q_copies[kd, km] = remote(
                q_send.at[layer, where["dp"], where["mp"]],
                q_recv.at[layer, d, m],
                qu_ssem.at[layer, kd, km],
                qu_rsem.at[layer, kd, km],
                where,
            )
        q_recv[layer, d, m] = q_send[layer, d, m]
        for copy in kv_copies:
            copy.wait_recv()
        total = sums[pl.ds(pl.multiple_of(d * band, band), band), query_cols:]
        for kd in range(1, n_dp):
            total = total + kv_recv[layer, kd - 1].astype(f32)
        for j in range(n_mp):
            row_send[layer, j] = total[j * owned : (j + 1) * owned]
        row_copies = []
        for km in reversed(range(1, n_mp)):
            to = flipped(m, km, m_bits)
            row_copies.append(
                remote(
                    row_send.at[layer, to],
                    row_recv.at[layer, m],
                    rw_ssem.at[layer, km - 1],
                    rw_rsem.at[layer, km - 1],
                    {"mp": to},
                )
            )
        row_recv[layer, m] = row_send[layer, m]
        for copy in square_copies:
            copy.wait_recv()
        square_sum = square_send[layer, d, m]
        for kd in range(1, n_dp):
            square_sum = square_sum + square_recv[layer, kd - 1]
        inverse_rms = lax.rsqrt(square_sum / model_width + norm_eps)

        def turned(x, r):
            cosines, sines, _ = turns[r]
            return x * cosines + pltpu.roll(x, head_dim // 2, 1) * sines

        if layer == 0:
            loads[2].wait()
        else:
            loads[2 + n_mp + layer].wait()
        per = keyval_cols // head_dim
        key_sources = key_heads // per
        part = key_heads // 2
        att_copies = []
        for step in range(2):
            base = (m // part) * part
            if step:
                base = part - base
            members = [
                (kd, km)
                for kd, km in others
                if km // part == step
            ]
            for pair in members:
                q_copies[pair].wait_recv()
            raw = q_recv[layer, 0, pl.ds(base, part)].astype(f32)
            for i in range(1, n_dp):
                raw = raw + q_recv[layer, i, pl.ds(base, part)].astype(f32)
            raw = raw.reshape(part, owned, group, head_dim)
            queries, scores = [], []
            for r in range(owned):
                asked = jnp.concatenate(
                    [turned(raw[j, r] * inverse_rms[r : r + 1], r)[None] for j in range(part)],
                    axis=0,
                ).astype(bf16)
                queries.append(asked)
                score = (
                    lax.dot_general(
                        asked,
                        cache[layer, r, 0, pl.ds(base, part)],
                        (((2,), (2,)), ((0,), (0,))),
                        preferred_element_type=f32,
                    )
                    * score_scale
                )
                at = lax.broadcasted_iota(jnp.int32, score.shape, 2)
                scores.append(jnp.where(at < turns[r][2], score, -jnp.inf))
            if step == 0:
                for copy in row_copies:
                    copy.wait_recv()
                for r in range(owned):
                    for t in range(per):
                        fresh = (
                            row_recv[layer, :, r, t * head_dim : (t + 1) * head_dim]
                            * inverse_rms[r : r + 1]
                        )
                        keys_fresh = turned(fresh, r)
                        for source in range(n_mp):
                            kind = source // key_sources
                            head = (source % key_sources) * per + t
                            row = keys_fresh if kind == 0 else fresh
                            fresh_buf[r, kind, head] = row[source : source + 1]
            results = []
            for r in range(owned):
                fresh_keys = fresh_buf[r, 0, pl.ds(base, part)].astype(bf16).astype(f32)
                fresh_values = fresh_buf[r, 1, pl.ds(base, part)].astype(bf16).astype(f32)
                own_score = (
                    jnp.sum(queries[r].astype(f32) * fresh_keys, axis=2, keepdims=True)
                    * score_scale
                )
                highest = jnp.maximum(jnp.max(scores[r], axis=2, keepdims=True), own_score)
                weights = jnp.exp(scores[r] - highest)
                own_weight = jnp.exp(own_score - highest)
                denominator = jnp.sum(weights, axis=2, keepdims=True) + own_weight
                summed = lax.dot_general(
                    weights.astype(bf16),
                    cache[layer, r, 1, pl.ds(base, part)],
                    (((2,), (1,)), ((0,), (0,))),
                    preferred_element_type=f32,
                )
                own_rounded = own_weight.astype(bf16).astype(f32)
                summed = summed + own_rounded * fresh_values
                results.append(summed / denominator)
            att_send[layer, pl.ds(base, part)] = jnp.concatenate(results, axis=1).astype(bf16)
            for kd, km in members:
                where = place_of[kd, km]
                att_copies.append(
                    remote(
                        att_send.at[layer, where["mp"]],
                        gathered.at[layer, d, m],
                        at_ssem.at[layer, kd, km],
                        at_rsem.at[layer, kd, km],
                        where,
                    )
                )
        gathered[layer, d, m] = att_send[layer, m]
        if layer == 0:
            for j in range(n_mp):
                loads[3 + j].wait()
        for copy in att_copies:
            copy.wait_recv()
        att_stage[...] = gathered[layer].astype(f32).reshape(rows, group, head_dim)
        left = jnp.concatenate(
            [att_stage[:, g, :].astype(bf16) for g in range(group)], axis=1
        )
        pair_copies = []
        for q in range(half):
            pair_send[layer, q] = jnp.dot(
                left, wo[(1 - core) * half + q], preferred_element_type=f32
            )
            pair_copies.append(
                remote(
                    pair_send.at[layer, q],
                    pair_recv.at[layer, q],
                    pq_ssem.at[layer, q],
                    pq_rsem.at[layer, q],
                    {"mp": sibling},
                )
            )
        first_copies = []
        for q in range(half):
            product = jnp.dot(left, wo[core * half + q], preferred_element_type=f32)
            pair_copies[q].wait_recv()
            first_send[layer, q] = (product + pair_recv[layer, q]).astype(LINK)
            first_copies.append(
                remote(
                    first_send.at[layer, q],
                    first_recv.at[layer, q],
                    fi_ssem.at[layer, q],
                    fi_rsem.at[layer, q],
                    {"mp": flipped(m, 2 if q % 2 == 0 else 4, m_bits)},
                )
            )
        second_copies = []
        for q in range(half):
            first_copies[q].wait_recv()
            both = first_send[layer, q].astype(f32) + first_recv[layer, q].astype(f32)
            second_send[layer, q] = both.astype(LINK)
            second_copies.append(
                remote(
                    second_send.at[layer, q],
                    second_recv.at[layer, q],
                    se_ssem.at[layer, q],
                    se_rsem.at[layer, q],
                    {"mp": flipped(m, 4 if q % 2 == 0 else 2, m_bits)},
                )
            )
        arriving = []
        for q in range(half):
            second_copies[q].wait_recv()
            at = core * half + q
            total = second_send[layer, q].astype(f32) + second_recv[layer, q].astype(f32)
            state[layer + 1, at] = (state[layer, at].astype(f32) + total).astype(bf16)
            arriving.append(
                remote(
                    state.at[layer + 1, at],
                    state.at[layer + 1, at],
                    st_ssem.at[layer, q],
                    st_rsem.at[layer, q],
                    {"mp": sibling},
                )
            )
            if layer + 1 < LAYERS and q % 2 == 1:
                if q == 1:
                    square_sum_buf[...] = jnp.zeros((rows, 128), f32)
                gather_chunks(layer + 1, [at - 1, at], q == 1)
        for q in range(half):
            arriving[q].wait_recv()
            if layer + 1 < LAYERS and q % 2 == 1:
                at = (1 - core) * half + q
                gather_chunks(layer + 1, [at - 1, at], False)
        if layer + 1 < LAYERS:
            prepare(layer + 1)
    for c in range(n_mp):
        out_ref[:, c * chunk : (c + 1) * chunk] = jnp.dot(
            place, state[LAYERS, c], preferred_element_type=f32
        ).astype(bf16)
    for copy in sends:
        copy.wait_send()


def fused(
    hidden_in, norm_gain, w_query, w_keyval, w_out, cache_slots, lengths, positions, slot_order
):
    n_dp = lax.axis_size("dp")
    n_mp = lax.axis_size("mp")
    rows, width = hidden_in.shape
    query_cols = w_query.shape[1]
    keyval_cols = w_keyval.shape[1]
    owned, key_heads, cache_rows, head_dim = (
        cache_slots.shape[1],
        cache_slots.shape[3],
        cache_slots.shape[4],
        cache_slots.shape[5],
    )
    group = query_cols // head_dim
    packed = owned * group
    band = rows // n_dp
    chunk = width // n_mp
    half = n_mp // 2
    index_row = np.arange(head_dim) % (head_dim // 2)
    frequency = np.exp(index_row * (-2.0 * math.log(rope_base) / head_dim))
    frequency = jnp.asarray(frequency[None].astype(np.float32))
    sizes = (n_dp, n_mp, rows, width, query_cols, keyval_cols, owned, key_heads, head_dim)
    vmem = pl.BlockSpec(memory_space=pltpu.VMEM)
    anywhere = pl.BlockSpec(memory_space=pl.ANY)
    f32, bf16 = jnp.float32, jnp.bfloat16
    dma = pltpu.SemaphoreType.DMA
    return pl.pallas_call(
        functools.partial(fused_kernel, sizes),
        out_shape=jax.ShapeDtypeStruct((rows, width), bf16),
        in_specs=[anywhere] * 11,
        out_specs=vmem,
        scratch_shapes=[
            pltpu.SMEM((rows,), jnp.int32),
            pltpu.SMEM((rows,), jnp.int32),
            pltpu.SMEM((rows,), jnp.int32),
            pltpu.VMEM((1, rows), jnp.int32),
            pltpu.VMEM((1, head_dim), f32),
            pltpu.VMEM((rows, width), bf16),
            pltpu.VMEM((width // 128, 128), bf16),
            pltpu.VMEM(w_query.shape, bf16),
            pltpu.VMEM(w_keyval.shape, bf16),
            pltpu.VMEM((n_mp, query_cols, chunk), bf16),
            pltpu.VMEM(cache_slots.shape, bf16),
            pltpu.VMEM((LAYERS + 1, n_mp, rows, chunk), bf16),
            pltpu.VMEM((LAYERS, n_dp, n_mp, owned, 128), f32),
            pltpu.VMEM((LAYERS, n_dp - 1, owned, 128), f32),
            pltpu.VMEM((rows, query_cols + keyval_cols), f32),
            pltpu.VMEM((rows, 128), f32),
            pltpu.VMEM((n_mp, chunk // 128, 1, 128), f32),
            pltpu.VMEM((LAYERS, n_dp, band, keyval_cols), LINK),
            pltpu.VMEM((LAYERS, n_dp - 1, band, keyval_cols), LINK),
            pltpu.VMEM((LAYERS, n_mp, owned, keyval_cols), f32),
            pltpu.VMEM((LAYERS, n_mp, owned, keyval_cols), f32),
            pltpu.VMEM((owned, 2, key_heads, 1, head_dim), f32),
            pltpu.VMEM((rows, group, head_dim), f32),
            pltpu.VMEM((LAYERS, n_dp, n_mp, packed, head_dim), LINK),
            pltpu.VMEM((LAYERS, n_dp, n_mp, packed, head_dim), LINK),
            pltpu.VMEM((LAYERS, n_mp, packed, head_dim), bf16),
            pltpu.VMEM((LAYERS, n_dp, n_mp, packed, head_dim), bf16),
            pltpu.VMEM((rows, group, head_dim), f32),
            pltpu.VMEM((LAYERS, half, rows, chunk), f32),
            pltpu.VMEM((LAYERS, half, rows, chunk), f32),
            pltpu.VMEM((LAYERS, half, rows, chunk), LINK),
            pltpu.VMEM((LAYERS, half, rows, chunk), LINK),
            pltpu.VMEM((LAYERS, half, rows, chunk), LINK),
            pltpu.VMEM((LAYERS, half, rows, chunk), LINK),
            dma((7,)),
            dma((2 + n_mp + LAYERS,)),
            dma((LAYERS, n_dp - 1)),
            dma((LAYERS, n_dp - 1)),
            dma((LAYERS, n_dp - 1)),
            dma((LAYERS, n_dp - 1)),
            dma((LAYERS, n_mp - 1)),
            dma((LAYERS, n_mp - 1)),
            dma((LAYERS, n_dp, n_mp)),
            dma((LAYERS, n_dp, n_mp)),
            dma((LAYERS, n_dp, n_mp)),
            dma((LAYERS, n_dp, n_mp)),
            dma((LAYERS, half)),
            dma((LAYERS, half)),
            dma((LAYERS, half)),
            dma((LAYERS, half)),
            dma((LAYERS, half)),
            dma((LAYERS, half)),
            dma((LAYERS, half)),
            dma((LAYERS, half)),
        ],
        compiler_params=pltpu.CompilerParams(
            collective_id=0, has_side_effects=True, vmem_limit_bytes=56 << 20
        ),
    )(
        slot_order,
        lengths,
        positions,
        slot_order.reshape(1, rows),
        frequency,
        hidden_in,
        norm_gain.reshape(width // 128, 128),
        w_query,
        w_keyval,
        w_out,
        cache_slots,
    )


def dispatch(
    hidden_in, norm_gain, w_query, w_keyval, w_out, cache_slots, lengths, positions, slot_order
):
    n_mp = lax.axis_size("mp")
    key_heads = cache_slots.shape[3]
    head_dim = cache_slots.shape[5]
    fits = (
        key_heads == n_mp
        and n_mp == 8
        and lax.axis_size("dp") == 4
        and cache_slots.shape[1] * (w_query.shape[1] // head_dim) % 16 == 0
        and (w_query.shape[1] // head_dim) == 8
        and w_keyval.shape[1] % head_dim == 0
        and w_query.shape[1] % w_keyval.shape[1] == 0
        and hidden_in.shape[1] % (128 * n_mp) == 0
        and hidden_in.shape[0] % (16 * lax.axis_size("dp")) == 0
    )
    chosen = fused if fits else shards
    return chosen(
        hidden_in, norm_gain, w_query, w_keyval, w_out, cache_slots, lengths, positions, slot_order
    )


def solution(mesh):
    placed = (
        P(None, "dp"),
        P("dp"),
        P("dp", "mp"),
        P("dp", "mp"),
        P("mp", "dp"),
        P(None, ("dp", "mp"), None, None, None, None),
        P(),
        P(),
        P(),
    )
    return jax.shard_map(
        dispatch, mesh=mesh, in_specs=placed, out_specs=P(None, "dp"), check_vma=False
    )
```

```python
import functools
import math

import jax
import jax.numpy as jnp
import numpy as np
from jax import lax
from jax.experimental import pallas as pl
from jax.experimental.pallas import tpu as pltpu
from jax.sharding import PartitionSpec as P

LAYERS = 2


norm_eps = 1e-05
rope_base = 500000.0


def rotate(values, at_positions):
    half_dim = values.shape[-1] // 2
    index_row = jnp.arange(half_dim, dtype=jnp.float32)
    frequency = jnp.exp(index_row * (-2.0 * math.log(rope_base) / values.shape[-1]))
    angles = at_positions.astype(jnp.float32)[:, None, None] * frequency
    cosines = jnp.cos(angles)
    sine_rows = jnp.sin(angles)
    first_half = values[..., :half_dim]
    second_half = values[..., half_dim:]
    return jnp.concatenate(
        [
            first_half * cosines - second_half * sine_rows,
            second_half * cosines + first_half * sine_rows,
        ],
        axis=-1,
    )


def attend(queries, fresh_keys, fresh_values, key_rows, values, slot_lengths):
    score_scale = 1.0 / math.sqrt(queries.shape[-1])
    scores = (
        jnp.einsum("rkgd,rktd->rkgt", queries, key_rows, preferred_element_type=jnp.float32)
        * score_scale
    )
    own_score = (
        jnp.einsum("rkgd,rkd->rkg", queries, fresh_keys, preferred_element_type=jnp.float32)
        * score_scale
    )
    positions_row = lax.broadcasted_iota(jnp.int32, (1, 1, 1, key_rows.shape[2]), 3)
    valid_keys = positions_row < slot_lengths[:, None, None, None]
    scores = jnp.where(valid_keys, scores, -jnp.inf)
    highest = jnp.maximum(jnp.max(scores, axis=-1), own_score)
    weights = jnp.exp(scores - highest[..., None])
    own_weight = jnp.exp(own_score - highest)
    denominator = jnp.sum(weights, axis=-1) + own_weight
    rounded = weights.astype(jnp.bfloat16)
    own_rounded = lax.optimization_barrier(own_weight.astype(jnp.bfloat16)).astype(jnp.float32)
    summed = jnp.einsum("rkgt,rktd->rkgd", rounded, values, preferred_element_type=jnp.float32)
    summed = summed + own_rounded[..., None] * fresh_values.astype(jnp.float32)[:, :, None, :]
    return (summed / denominator[..., None]).astype(jnp.bfloat16)


def shards(
    hidden_in, norm_gain, w_query, w_keyval, w_out, cache_slots, lengths, positions, slot_order
):
    total_rows = hidden_in.shape[0]
    data_count = lax.axis_size("dp")
    model_count = lax.axis_size("mp")
    owned_rows = cache_slots.shape[1]
    key_heads = cache_slots.shape[3]
    head_dim = cache_slots.shape[5]
    query_cols = w_query.shape[1]
    head_count = query_cols * model_count // head_dim
    group_size = head_count // key_heads
    model_width = hidden_in.shape[1] * data_count
    half_width = key_heads * head_dim
    inverse = (
        jnp.zeros((total_rows,), jnp.int32)
        .at[slot_order]
        .set(jnp.arange(total_rows, dtype=jnp.int32))
    )
    device_index = lax.axis_index("dp") * model_count + lax.axis_index("mp")
    slot_lengths = lax.dynamic_slice_in_dim(
        jnp.take(lengths, slot_order), device_index * owned_rows, owned_rows
    )
    slot_positions = lax.dynamic_slice_in_dim(
        jnp.take(positions, slot_order), device_index * owned_rows, owned_rows
    )
    gain_float = norm_gain.astype(jnp.float32)
    current = jnp.take(hidden_in, slot_order, axis=0)
    for layer_index in range(LAYERS):
        floats = current.astype(jnp.float32)
        squares = jnp.sum(floats * floats, axis=1)
        scaled = (floats * gain_float).astype(jnp.bfloat16)
        partial_value = jnp.concatenate(
            [
                jnp.dot(scaled, w_query, preferred_element_type=jnp.float32),
                jnp.dot(scaled, w_keyval, preferred_element_type=jnp.float32),
            ],
            axis=1,
        )
        summed = lax.psum_scatter(partial_value, "dp", scatter_dimension=0, tiled=True)
        square_sum = lax.psum_scatter(squares, "dp", scatter_dimension=0, tiled=True)
        inverse_rms = lax.rsqrt(square_sum / model_width + norm_eps)
        projected = summed * inverse_rms[:, None]
        arrived = lax.all_to_all(projected, "mp", split_axis=0, concat_axis=1, tiled=True)
        arrived = arrived.reshape(owned_rows, model_count, projected.shape[1])
        query_part = arrived[:, :, :query_cols].reshape(owned_rows, head_count, head_dim)
        keyval_part = arrived[:, :, query_cols:].reshape(owned_rows, 2 * half_width)
        queries = (
            rotate(query_part, slot_positions)
            .astype(jnp.bfloat16)
            .reshape(owned_rows, key_heads, group_size, head_dim)
        )
        fresh_keys = rotate(
            keyval_part[:, :half_width].reshape(owned_rows, key_heads, head_dim), slot_positions
        ).astype(jnp.bfloat16)
        fresh_values = (
            keyval_part[:, half_width:]
            .reshape(owned_rows, key_heads, head_dim)
            .astype(jnp.bfloat16)
        )
        layer_cache = cache_slots[layer_index]
        attended = attend(
            queries, fresh_keys, fresh_values, layer_cache[:, 0], layer_cache[:, 1], slot_lengths
        )
        attended = attended.reshape(owned_rows, head_count * head_dim)
        returned = lax.all_to_all(attended, "mp", split_axis=1, concat_axis=0, tiled=True)
        partial_out = jnp.dot(
            lax.all_gather(returned, "dp", axis=0, tiled=True),
            w_out,
            preferred_element_type=jnp.float32,
        )
        totals = lax.psum(partial_out, "mp")
        current = (floats + totals).astype(jnp.bfloat16)
    return jnp.take(current, inverse, axis=0)


LINK = jnp.bfloat16


def flipped(at, mask, bits):
    turned_at = 0
    for b in range(bits):
        bit = (at // (1 << b)) % 2
        if (mask >> b) & 1:
            bit = 1 - bit
        turned_at = turned_at + bit * (1 << b)
    return turned_at


def fused_kernel(
    sizes,
    slot_hbm,
    length_hbm,
    position_hbm,
    slot_row_hbm,
    frequency_hbm,
    hidden_hbm,
    gain_hbm,
    wq_hbm,
    wkv_hbm,
    wo_hbm,
    cache_hbm,
    out_ref,
    slot_s,
    length_s,
    position_s,
    slot_row,
    frequency_ref,
    hidden_ref,
    gain_ref,
    wq,
    wkv,
    wo,
    cache,
    state,
    square_send,
    square_recv,
    sums,
    square_sum_buf,
    gain_rows,
    kv_send,
    kv_recv,
    fresh_buf,
    stage,
    q_send,
    q_recv,
    att_send,
    gathered,
    att_stage,
    pair_send,
    pair_recv,
    first_send,
    first_recv,
    second_send,
    second_recv,
    direct_all,
    small_sem,
    weight_sem,
    load_sem,
    sq_ssem,
    sq_rsem,
    kv_ssem,
    kv_rsem,
    qu_ssem,
    qu_rsem,
    at_ssem,
    at_rsem,
    pq_ssem,
    pq_rsem,
    fi_ssem,
    fi_rsem,
    se_ssem,
    se_rsem,
    di_ssem,
    di_rsem,
    st_ssem,
    st_rsem,
):
    n_dp, n_mp, rows, width, query_cols, keyval_cols, owned, key_heads, head_dim = sizes
    band = rows // n_dp
    chunk = width // n_mp
    group = query_cols // head_dim
    packed = owned * group
    half = n_mp // 2
    d_bits, m_bits = n_dp.bit_length() - 1, n_mp.bit_length() - 1
    f32, bf16 = jnp.float32, jnp.bfloat16
    d = lax.axis_index("dp")
    m = lax.axis_index("mp")
    model_width = width * n_dp
    core = lax.rem(m, 2)
    sibling = m + 1 - 2 * core
    score_scale = 1.0 / math.sqrt(head_dim)
    others = [
        (kd, km) for kd in reversed(range(n_dp)) for km in reversed(range(n_mp)) if kd or km
    ]
    place_of = {
        (kd, km): {"dp": flipped(d, kd, d_bits), "mp": flipped(m, km, m_bits)}
        for kd, km in others
    }

    shallow = width // 4
    small = [
        pltpu.make_async_copy(src, dst, small_sem.at[i])
        for i, (src, dst) in enumerate(
            [
                (slot_row_hbm, slot_row),
                (hidden_hbm, hidden_ref),
                (gain_hbm, gain_ref),
                (slot_hbm, slot_s),
                (length_hbm, length_s),
                (position_hbm, position_s),
                (frequency_hbm, frequency_ref),
            ]
        )
    ]
    weight_loads = [
        [
            pltpu.make_async_copy(
                src.at[pl.ds(k * shallow, shallow)],
                dst.at[pl.ds(k * shallow, shallow)],
                weight_sem.at[k, i],
            )
            for i, (src, dst) in enumerate([(wkv_hbm, wkv), (wq_hbm, wq)])
        ]
        for k in range(4)
    ]
    loads = []
    for layer in range(LAYERS):
        loads.append(
            pltpu.make_async_copy(cache_hbm.at[layer], cache.at[layer], load_sem.at[layer])
        )
    for j in range(n_mp):
        loads.insert(
            1 + j,
            pltpu.make_async_copy(
                wo_hbm.at[:, pl.ds(j * chunk, chunk)], wo.at[j], load_sem.at[LAYERS + j]
            ),
        )
    for one in small[:3]:
        one.start()
    for both in weight_loads:
        for one in both:
            one.start()

    barrier = pltpu.get_barrier_semaphore()
    for pair in others:
        pl.semaphore_signal(
            barrier, inc=1, device_id=place_of[pair], device_id_type=pl.DeviceIdType.MESH
        )
    for one in small[3:]:
        one.start()

    for one in small[:3]:
        one.wait()
    sublanes = lax.broadcasted_iota(jnp.int32, (rows, rows), 0)
    place = jnp.where(slot_row[...] == sublanes, 1.0, 0.0).astype(bf16)
    gains = gain_ref[...].astype(f32)
    for c in range(n_mp):
        state[0, c] = lax.dot_general(
            place,
            hidden_ref[:, c * chunk : (c + 1) * chunk],
            (((0,), (0,)), ((), ())),
            preferred_element_type=f32,
        ).astype(bf16)

    sends = []

    def remote(src, dst, ssem, rsem, where):
        copy = pltpu.make_async_remote_copy(
            src_ref=src,
            dst_ref=dst,
            send_sem=ssem,
            recv_sem=rsem,
            device_id=where,
            device_id_type=pl.DeviceIdType.MESH,
        )
        copy.start()
        sends.append(copy)
        return copy

    def gather_chunks(layer, places, fresh_start):
        squares = square_sum_buf[...]
        pieces = []
        for c in places:
            floats = state[layer, c].astype(f32)
            for t in range(chunk // 128):
                piece = floats[:, t * 128 : (t + 1) * 128]
                pieces.append((piece * gain_rows[c, t]).astype(bf16))
                squares = squares + piece * piece
        square_sum_buf[...] = squares
        depth = len(places) * chunk
        start = places[0] * chunk
        if not isinstance(start, int):
            start = pl.multiple_of(start, chunk)
        left = jnp.concatenate(pieces, axis=1)
        wide = 256
        for b in range(-1, query_cols // wide):
            if b < 0:
                weights = wkv[pl.ds(start, depth), :]
                at = query_cols
                span = keyval_cols
            else:
                weights = wq[pl.ds(start, depth), b * wide : (b + 1) * wide]
                at = b * wide
                span = wide
            product = jnp.dot(left, weights, preferred_element_type=f32)
            if fresh_start:
                sums[:, at : at + span] = product
            else:
                sums[:, at : at + span] += product

    def prepare(layer):
        square_row = jnp.broadcast_to(
            jnp.sum(square_sum_buf[...], axis=1, keepdims=True), (rows, 128)
        )
        product = sums[:, query_cols:]
        for g in range(group):
            stage[:, g, :] = sums[:, g * head_dim : (g + 1) * head_dim]
        q_send[layer] = stage[...].reshape(n_dp, n_mp, packed, head_dim).astype(bf16)
        for i in range(n_dp):
            for j in range(n_mp):
                at = (i * n_mp + j) * owned
                square_send[layer, i, j] = square_row[at : at + owned]
                kv_send[layer, i, j] = product[at : at + owned]

    for c in range(n_mp):
        for t in range(chunk // 128):
            at = c * (chunk // 128) + t
            gain_rows[c, t] = gains[at : at + 1]
    square_sum_buf[...] = jnp.zeros((rows, 128), f32)
    for k, both in enumerate(weight_loads):
        for one in both:
            one.wait()
        if k == 3:
            for one in loads:
                one.start()
        per_load = n_mp // 4
        gather_chunks(0, [k * per_load + i for i in range(per_load)], k == 0)
    prepare(0)
    turns = []
    pl.semaphore_wait(barrier, len(others))

    for layer in range(LAYERS):
        square_copies, kv_copies, q_copies = [], [], {}
        for kd in reversed(range(1, n_dp)):
            to = flipped(d, kd, d_bits)
            square_copies.append(
                remote(
                    square_send.at[layer, to, m],
                    square_recv.at[layer, kd - 1],
                    sq_ssem.at[layer, kd - 1],
                    sq_rsem.at[layer, kd - 1],
                    {"dp": to},
                )
            )
        for kd, km in others:
            where = place_of[kd, km]
            q_copies[kd, km] = remote(
                q_send.at[layer, where["dp"], where["mp"]],
                q_recv.at[layer, d, m],
                qu_ssem.at[layer, kd, km],
                qu_rsem.at[layer, kd, km],
                where,
            )
        q_recv[layer, d, m] = q_send[layer, d, m]
        for kd, km in others:
            where = place_of[kd, km]
            kv_copies.append(
                remote(
                    kv_send.at[layer, where["dp"], where["mp"]],
                    kv_recv.at[layer, d, m],
                    kv_ssem.at[layer, kd, km],
                    kv_rsem.at[layer, kd, km],
                    where,
                )
            )
        kv_recv[layer, d, m] = kv_send[layer, d, m]
        if layer == 0:
            for one in small[3:]:
                one.wait()
            for r in range(owned):
                slot = slot_s[(d * n_mp + m) * owned + r]
                at = jnp.full((group, head_dim), position_s[slot], jnp.int32).astype(f32)
                angles = at * frequency_ref[...]
                lane = lax.broadcasted_iota(jnp.int32, (group, head_dim), 1)
                sines = jnp.sin(angles)
                turns.append(
                    (
                        jnp.cos(angles),
                        jnp.where(lane < head_dim // 2, -sines, sines),
                        length_s[slot],
                    )
                )
        for copy in square_copies:
            copy.wait_recv()
        square_sum = square_send[layer, d, m]
        for kd in range(1, n_dp):
            square_sum = square_sum + square_recv[layer, kd - 1]
        inverse_rms = lax.rsqrt(square_sum / model_width + norm_eps)

        def turned(x, r):
            cosines, sines, _ = turns[r]
            return x * cosines + pltpu.roll(x, head_dim // 2, 1) * sines

        loads[layer * (n_mp + 1)].wait()
        per = keyval_cols // head_dim
        key_sources = key_heads // per
        part = key_heads // 2
        att_copies = []
        for step in range(2):
            base = (m // part) * part
            if step:
                base = part - base
            members = [
                (kd, km)
                for kd, km in others
                if km // part == step
            ]
            for pair in members:
                q_copies[pair].wait_recv()
            raw = q_recv[layer, 0, pl.ds(base, part)].astype(f32)
            for i in range(1, n_dp):
                raw = raw + q_recv[layer, i, pl.ds(base, part)].astype(f32)
            raw = raw.reshape(part, owned, group, head_dim)
            queries, scores = [], []
            for r in range(owned):
                asked = jnp.concatenate(
                    [turned(raw[j, r] * inverse_rms[r : r + 1], r)[None] for j in range(part)],
                    axis=0,
                ).astype(bf16)
                queries.append(asked)
                score = (
                    lax.dot_general(
                        asked,
                        cache[layer, r, 0, pl.ds(base, part)],
                        (((2,), (2,)), ((0,), (0,))),
                        preferred_element_type=f32,
                    )
                    * score_scale
                )
                at = lax.broadcasted_iota(jnp.int32, score.shape, 2)
                scores.append(jnp.where(at < turns[r][2], score, -jnp.inf))
            if step == 0:
                for copy in kv_copies:
                    copy.wait_recv()
                for r in range(owned):
                    for t in range(per):
                        fresh = kv_recv[layer, 0, :, r, t * head_dim : (t + 1) * head_dim]
                        for i in range(1, n_dp):
                            fresh = (
                                fresh
                                + kv_recv[layer, i, :, r, t * head_dim : (t + 1) * head_dim]
                            )
                        fresh = fresh * inverse_rms[r : r + 1]
                        keys_fresh = turned(fresh, r)
                        for source in range(n_mp):
                            kind = source // key_sources
                            head = (source % key_sources) * per + t
                            row = keys_fresh if kind == 0 else fresh
                            fresh_buf[r, kind, head] = row[source : source + 1]
            results = []
            for r in range(owned):
                fresh_keys = fresh_buf[r, 0, pl.ds(base, part)].astype(bf16).astype(f32)
                fresh_values = fresh_buf[r, 1, pl.ds(base, part)].astype(bf16).astype(f32)
                own_score = (
                    jnp.sum(queries[r].astype(f32) * fresh_keys, axis=2, keepdims=True)
                    * score_scale
                )
                highest = jnp.maximum(jnp.max(scores[r], axis=2, keepdims=True), own_score)
                weights = jnp.exp(scores[r] - highest)
                own_weight = jnp.exp(own_score - highest)
                denominator = jnp.sum(weights, axis=2, keepdims=True) + own_weight
                summed = lax.dot_general(
                    weights.astype(bf16),
                    cache[layer, r, 1, pl.ds(base, part)],
                    (((2,), (1,)), ((0,), (0,))),
                    preferred_element_type=f32,
                )
                own_rounded = own_weight.astype(bf16).astype(f32)
                summed = summed + own_rounded * fresh_values
                results.append(summed / denominator)
            att_send[layer, pl.ds(base, part)] = jnp.concatenate(results, axis=1).astype(bf16)
            for kd, km in members:
                where = place_of[kd, km]
                att_copies.append(
                    remote(
                        att_send.at[layer, where["mp"]],
                        gathered.at[layer, d, m],
                        at_ssem.at[layer, kd, km],
                        at_rsem.at[layer, kd, km],
                        where,
                    )
                )
        gathered[layer, d, m] = att_send[layer, m]
        if layer == 0:
            for j in range(n_mp):
                loads[1 + j].wait()
        for copy in att_copies:
            copy.wait_recv()
        att_stage[...] = gathered[layer].astype(f32).reshape(rows, group, head_dim)
        left = jnp.concatenate(
            [att_stage[:, g, :].astype(bf16) for g in range(group)], axis=1
        )
        pair_copies = []
        for q in range(half):
            pair_send[layer, q] = jnp.dot(
                left, wo[(1 - core) * half + q], preferred_element_type=f32
            )
            pair_copies.append(
                remote(
                    pair_send.at[layer, q],
                    pair_recv.at[layer, q],
                    pq_ssem.at[layer, q],
                    pq_rsem.at[layer, q],
                    {"mp": sibling},
                )
            )
        staged = half // 2
        chip = m // 2
        first_copies, second_copies, direct_copies = [], [], []
        for q in range(half):
            product = jnp.dot(left, wo[core * half + q], preferred_element_type=f32)
            pair_copies[q].wait_recv()
            chip_sum = (product + pair_recv[layer, q]).astype(LINK)
            if q < staged:
                first_send[layer, q] = chip_sum
                first_copies.append(
                    remote(
                        first_send.at[layer, q],
                        first_recv.at[layer, q],
                        fi_ssem.at[layer, q],
                        fi_rsem.at[layer, q],
                        {"mp": flipped(m, 2 if q % 2 == 0 else 4, m_bits)},
                    )
                )
            else:
                direct_all[layer, q - staged, chip] = chip_sum
                for k in (3, 1, 2):
                    direct_copies.append(
                        remote(
                            direct_all.at[layer, q - staged, chip],
                            direct_all.at[layer, q - staged, chip],
                            di_ssem.at[layer, q - staged, k - 1],
                            di_rsem.at[layer, q - staged, k - 1],
                            {"mp": flipped(m, 2 * k, m_bits)},
                        )
                    )
        for q in range(staged):
            first_copies[q].wait_recv()
            both = first_send[layer, q].astype(f32) + first_recv[layer, q].astype(f32)
            second_send[layer, q] = both.astype(LINK)
            second_copies.append(
                remote(
                    second_send.at[layer, q],
                    second_recv.at[layer, q],
                    se_ssem.at[layer, q],
                    se_rsem.at[layer, q],
                    {"mp": flipped(m, 4 if q % 2 == 0 else 2, m_bits)},
                )
            )
        arriving = {}
        order = list(range(staged, half)) + list(range(staged))
        if layer + 1 < LAYERS:
            square_sum_buf[...] = jnp.zeros((rows, 128), f32)
        for i, q in enumerate(order):
            at = core * half + q
            if q < staged:
                second_copies[q].wait_recv()
                total = second_send[layer, q].astype(f32) + second_recv[layer, q].astype(f32)
            else:
                for copy in direct_copies[(q - staged) * 3 : (q - staged) * 3 + 3]:
                    copy.wait_recv()
                total = direct_all[layer, q - staged, 0].astype(f32)
                for c in range(1, n_mp // 2):
                    total = total + direct_all[layer, q - staged, c].astype(f32)
            state[layer + 1, at] = (state[layer, at].astype(f32) + total).astype(bf16)
            arriving[q] = remote(
                state.at[layer + 1, at],
                state.at[layer + 1, at],
                st_ssem.at[layer, q],
                st_rsem.at[layer, q],
                {"mp": sibling},
            )
            if layer + 1 < LAYERS and i % 2 == 1:
                gather_chunks(layer + 1, [at - 1, at], i == 1)
        for i, q in enumerate(order):
            arriving[q].wait_recv()
            if layer + 1 < LAYERS and i % 2 == 1:
                at = (1 - core) * half + q
                gather_chunks(layer + 1, [at - 1, at], False)
        if layer + 1 < LAYERS:
            prepare(layer + 1)
    for c in range(n_mp):
        out_ref[:, c * chunk : (c + 1) * chunk] = jnp.dot(
            place, state[LAYERS, c], preferred_element_type=f32
        ).astype(bf16)
    for copy in sends:
        copy.wait_send()


def fused(
    hidden_in, norm_gain, w_query, w_keyval, w_out, cache_slots, lengths, positions, slot_order
):
    n_dp = lax.axis_size("dp")
    n_mp = lax.axis_size("mp")
    rows, width = hidden_in.shape
    query_cols = w_query.shape[1]
    keyval_cols = w_keyval.shape[1]
    owned, key_heads, cache_rows, head_dim = (
        cache_slots.shape[1],
        cache_slots.shape[3],
        cache_slots.shape[4],
        cache_slots.shape[5],
    )
    group = query_cols // head_dim
    packed = owned * group
    band = rows // n_dp
    chunk = width // n_mp
    half = n_mp // 2
    index_row = np.arange(head_dim) % (head_dim // 2)
    frequency = np.exp(index_row * (-2.0 * math.log(rope_base) / head_dim))
    frequency = jnp.asarray(frequency[None].astype(np.float32))
    sizes = (n_dp, n_mp, rows, width, query_cols, keyval_cols, owned, key_heads, head_dim)
    vmem = pl.BlockSpec(memory_space=pltpu.VMEM)
    anywhere = pl.BlockSpec(memory_space=pl.ANY)
    f32, bf16 = jnp.float32, jnp.bfloat16
    dma = pltpu.SemaphoreType.DMA
    return pl.pallas_call(
        functools.partial(fused_kernel, sizes),
        out_shape=jax.ShapeDtypeStruct((rows, width), bf16),
        in_specs=[anywhere] * 11,
        out_specs=vmem,
        scratch_shapes=[
            pltpu.SMEM((rows,), jnp.int32),
            pltpu.SMEM((rows,), jnp.int32),
            pltpu.SMEM((rows,), jnp.int32),
            pltpu.VMEM((1, rows), jnp.int32),
            pltpu.VMEM((1, head_dim), f32),
            pltpu.VMEM((rows, width), bf16),
            pltpu.VMEM((width // 128, 128), bf16),
            pltpu.VMEM(w_query.shape, bf16),
            pltpu.VMEM(w_keyval.shape, bf16),
            pltpu.VMEM((n_mp, query_cols, chunk), bf16),
            pltpu.VMEM(cache_slots.shape, bf16),
            pltpu.VMEM((LAYERS + 1, n_mp, rows, chunk), bf16),
            pltpu.VMEM((LAYERS, n_dp, n_mp, owned, 128), f32),
            pltpu.VMEM((LAYERS, n_dp - 1, owned, 128), f32),
            pltpu.VMEM((rows, query_cols + keyval_cols), f32),
            pltpu.VMEM((rows, 128), f32),
            pltpu.VMEM((n_mp, chunk // 128, 1, 128), f32),
            pltpu.VMEM((LAYERS, n_dp, n_mp, owned, keyval_cols), f32),
            pltpu.VMEM((LAYERS, n_dp, n_mp, owned, keyval_cols), f32),
            pltpu.VMEM((owned, 2, key_heads, 1, head_dim), f32),
            pltpu.VMEM((rows, group, head_dim), f32),
            pltpu.VMEM((LAYERS, n_dp, n_mp, packed, head_dim), LINK),
            pltpu.VMEM((LAYERS, n_dp, n_mp, packed, head_dim), LINK),
            pltpu.VMEM((LAYERS, n_mp, packed, head_dim), bf16),
            pltpu.VMEM((LAYERS, n_dp, n_mp, packed, head_dim), bf16),
            pltpu.VMEM((rows, group, head_dim), f32),
            pltpu.VMEM((LAYERS, half, rows, chunk), f32),
            pltpu.VMEM((LAYERS, half, rows, chunk), f32),
            pltpu.VMEM((LAYERS, half // 2, rows, chunk), LINK),
            pltpu.VMEM((LAYERS, half // 2, rows, chunk), LINK),
            pltpu.VMEM((LAYERS, half // 2, rows, chunk), LINK),
            pltpu.VMEM((LAYERS, half // 2, rows, chunk), LINK),
            pltpu.VMEM((LAYERS, half // 2, half, rows, chunk), LINK),
            dma((7,)),
            dma((4, 2)),
            dma((n_mp + LAYERS,)),
            dma((LAYERS, n_dp - 1)),
            dma((LAYERS, n_dp - 1)),
            dma((LAYERS, n_dp, n_mp)),
            dma((LAYERS, n_dp, n_mp)),
            dma((LAYERS, n_dp, n_mp)),
            dma((LAYERS, n_dp, n_mp)),
            dma((LAYERS, n_dp, n_mp)),
            dma((LAYERS, n_dp, n_mp)),
            dma((LAYERS, half)),
            dma((LAYERS, half)),
            dma((LAYERS, half // 2)),
            dma((LAYERS, half // 2)),
            dma((LAYERS, half // 2)),
            dma((LAYERS, half // 2)),
            dma((LAYERS, half // 2, half - 1)),
            dma((LAYERS, half // 2, half - 1)),
            dma((LAYERS, half)),
            dma((LAYERS, half)),
        ],
        compiler_params=pltpu.CompilerParams(
            collective_id=0, has_side_effects=True, vmem_limit_bytes=56 << 20
        ),
    )(
        slot_order,
        lengths,
        positions,
        slot_order.reshape(1, rows),
        frequency,
        hidden_in,
        norm_gain.reshape(width // 128, 128),
        w_query,
        w_keyval,
        w_out,
        cache_slots,
    )


def dispatch(
    hidden_in, norm_gain, w_query, w_keyval, w_out, cache_slots, lengths, positions, slot_order
):
    n_mp = lax.axis_size("mp")
    key_heads = cache_slots.shape[3]
    head_dim = cache_slots.shape[5]
    fits = (
        key_heads == n_mp
        and n_mp == 8
        and lax.axis_size("dp") == 4
        and cache_slots.shape[1] * (w_query.shape[1] // head_dim) % 16 == 0
        and (w_query.shape[1] // head_dim) == 8
        and w_keyval.shape[1] % head_dim == 0
        and w_query.shape[1] % w_keyval.shape[1] == 0
        and hidden_in.shape[1] % (128 * n_mp) == 0
        and hidden_in.shape[0] % (16 * lax.axis_size("dp")) == 0
    )
    chosen = fused if fits else shards
    return chosen(
        hidden_in, norm_gain, w_query, w_keyval, w_out, cache_slots, lengths, positions, slot_order
    )


def solution(mesh):
    placed = (
        P(None, "dp"),
        P("dp"),
        P("dp", "mp"),
        P("dp", "mp"),
        P("mp", "dp"),
        P(None, ("dp", "mp"), None, None, None, None),
        P(),
        P(),
        P(),
    )
    return jax.shard_map(
        dispatch, mesh=mesh, in_specs=placed, out_specs=P(None, "dp"), check_vma=False
    )
```

```python
import functools
import math

import jax
import jax.numpy as jnp
import numpy as np
from jax import lax
from jax.experimental import pallas as pl
from jax.experimental.pallas import tpu as pltpu
from jax.sharding import PartitionSpec as P

LAYERS = 2


norm_eps = 1e-05
rope_base = 500000.0


def rotate(values, at_positions):
    half_dim = values.shape[-1] // 2
    index_row = jnp.arange(half_dim, dtype=jnp.float32)
    frequency = jnp.exp(index_row * (-2.0 * math.log(rope_base) / values.shape[-1]))
    angles = at_positions.astype(jnp.float32)[:, None, None] * frequency
    cosines = jnp.cos(angles)
    sine_rows = jnp.sin(angles)
    first_half = values[..., :half_dim]
    second_half = values[..., half_dim:]
    return jnp.concatenate(
        [
            first_half * cosines - second_half * sine_rows,
            second_half * cosines + first_half * sine_rows,
        ],
        axis=-1,
    )


def attend(queries, fresh_keys, fresh_values, key_rows, values, slot_lengths):
    score_scale = 1.0 / math.sqrt(queries.shape[-1])
    scores = (
        jnp.einsum("rkgd,rktd->rkgt", queries, key_rows, preferred_element_type=jnp.float32)
        * score_scale
    )
    own_score = (
        jnp.einsum("rkgd,rkd->rkg", queries, fresh_keys, preferred_element_type=jnp.float32)
        * score_scale
    )
    positions_row = lax.broadcasted_iota(jnp.int32, (1, 1, 1, key_rows.shape[2]), 3)
    valid_keys = positions_row < slot_lengths[:, None, None, None]
    scores = jnp.where(valid_keys, scores, -jnp.inf)
    highest = jnp.maximum(jnp.max(scores, axis=-1), own_score)
    weights = jnp.exp(scores - highest[..., None])
    own_weight = jnp.exp(own_score - highest)
    denominator = jnp.sum(weights, axis=-1) + own_weight
    rounded = weights.astype(jnp.bfloat16)
    own_rounded = lax.optimization_barrier(own_weight.astype(jnp.bfloat16)).astype(jnp.float32)
    summed = jnp.einsum("rkgt,rktd->rkgd", rounded, values, preferred_element_type=jnp.float32)
    summed = summed + own_rounded[..., None] * fresh_values.astype(jnp.float32)[:, :, None, :]
    return (summed / denominator[..., None]).astype(jnp.bfloat16)


def shards(
    hidden_in, norm_gain, w_query, w_keyval, w_out, cache_slots, lengths, positions, slot_order
):
    total_rows = hidden_in.shape[0]
    data_count = lax.axis_size("dp")
    model_count = lax.axis_size("mp")
    owned_rows = cache_slots.shape[1]
    key_heads = cache_slots.shape[3]
    head_dim = cache_slots.shape[5]
    query_cols = w_query.shape[1]
    head_count = query_cols * model_count // head_dim
    group_size = head_count // key_heads
    model_width = hidden_in.shape[1] * data_count
    half_width = key_heads * head_dim
    inverse = (
        jnp.zeros((total_rows,), jnp.int32)
        .at[slot_order]
        .set(jnp.arange(total_rows, dtype=jnp.int32))
    )
    device_index = lax.axis_index("dp") * model_count + lax.axis_index("mp")
    slot_lengths = lax.dynamic_slice_in_dim(
        jnp.take(lengths, slot_order), device_index * owned_rows, owned_rows
    )
    slot_positions = lax.dynamic_slice_in_dim(
        jnp.take(positions, slot_order), device_index * owned_rows, owned_rows
    )
    gain_float = norm_gain.astype(jnp.float32)
    current = jnp.take(hidden_in, slot_order, axis=0)
    for layer_index in range(LAYERS):
        floats = current.astype(jnp.float32)
        squares = jnp.sum(floats * floats, axis=1)
        scaled = (floats * gain_float).astype(jnp.bfloat16)
        partial_value = jnp.concatenate(
            [
                jnp.dot(scaled, w_query, preferred_element_type=jnp.float32),
                jnp.dot(scaled, w_keyval, preferred_element_type=jnp.float32),
            ],
            axis=1,
        )
        summed = lax.psum_scatter(partial_value, "dp", scatter_dimension=0, tiled=True)
        square_sum = lax.psum_scatter(squares, "dp", scatter_dimension=0, tiled=True)
        inverse_rms = lax.rsqrt(square_sum / model_width + norm_eps)
        projected = summed * inverse_rms[:, None]
        arrived = lax.all_to_all(projected, "mp", split_axis=0, concat_axis=1, tiled=True)
        arrived = arrived.reshape(owned_rows, model_count, projected.shape[1])
        query_part = arrived[:, :, :query_cols].reshape(owned_rows, head_count, head_dim)
        keyval_part = arrived[:, :, query_cols:].reshape(owned_rows, 2 * half_width)
        queries = (
            rotate(query_part, slot_positions)
            .astype(jnp.bfloat16)
            .reshape(owned_rows, key_heads, group_size, head_dim)
        )
        fresh_keys = rotate(
            keyval_part[:, :half_width].reshape(owned_rows, key_heads, head_dim), slot_positions
        ).astype(jnp.bfloat16)
        fresh_values = (
            keyval_part[:, half_width:]
            .reshape(owned_rows, key_heads, head_dim)
            .astype(jnp.bfloat16)
        )
        layer_cache = cache_slots[layer_index]
        attended = attend(
            queries, fresh_keys, fresh_values, layer_cache[:, 0], layer_cache[:, 1], slot_lengths
        )
        attended = attended.reshape(owned_rows, head_count * head_dim)
        returned = lax.all_to_all(attended, "mp", split_axis=1, concat_axis=0, tiled=True)
        partial_out = jnp.dot(
            lax.all_gather(returned, "dp", axis=0, tiled=True),
            w_out,
            preferred_element_type=jnp.float32,
        )
        totals = lax.psum(partial_out, "mp")
        current = (floats + totals).astype(jnp.bfloat16)
    return jnp.take(current, inverse, axis=0)


LINK = jnp.bfloat16


def flipped(at, mask, bits):
    turned_at = 0
    for b in range(bits):
        bit = (at // (1 << b)) % 2
        if (mask >> b) & 1:
            bit = 1 - bit
        turned_at = turned_at + bit * (1 << b)
    return turned_at


def fused_kernel(
    sizes,
    slot_hbm,
    length_hbm,
    position_hbm,
    slot_row_hbm,
    frequency_hbm,
    hidden_hbm,
    gain_hbm,
    wq_hbm,
    wkv_hbm,
    wo_hbm,
    cache_hbm,
    out_ref,
    slot_s,
    length_s,
    position_s,
    slot_row,
    frequency_ref,
    hidden_ref,
    gain_ref,
    wq,
    wkv,
    wo,
    wo_other,
    cache,
    state,
    square_send,
    square_recv,
    sums,
    square_sum_buf,
    gain_rows,
    kv_send,
    kv_recv,
    row_send,
    row_recv,
    fresh_buf,
    stage,
    q_send,
    q_recv,
    att_send,
    gathered,
    att_stage,
    left_send,
    left_recv,
    out_acc,
    first_send,
    first_recv,
    second_send,
    second_recv,
    direct_all,
    sems,
):
    n_dp, n_mp, rows, width, query_cols, keyval_cols, owned, key_heads, head_dim = sizes
    band = rows // n_dp
    chunk = width // n_mp
    group = query_cols // head_dim
    packed = owned * group
    half = n_mp // 2
    d_bits, m_bits = n_dp.bit_length() - 1, n_mp.bit_length() - 1
    f32, bf16 = jnp.float32, jnp.bfloat16
    d = lax.axis_index("dp")
    m = lax.axis_index("mp")
    model_width = width * n_dp
    core = lax.rem(m, 2)
    sibling = m + 1 - 2 * core
    score_scale = 1.0 / math.sqrt(head_dim)
    others = [
        (kd, km) for kd in reversed(range(n_dp)) for km in reversed(range(n_mp)) if kd or km
    ]
    place_of = {
        (kd, km): {"dp": flipped(d, kd, d_bits), "mp": flipped(m, km, m_bits)}
        for kd, km in others
    }

    taken = []

    def fresh_sem():
        taken.append(0)
        return sems.at[len(taken) - 1]

    shallow = width // 4
    small = [
        pltpu.make_async_copy(src, dst, fresh_sem())
        for src, dst in (
            [
                (slot_row_hbm, slot_row),
                (hidden_hbm, hidden_ref),
                (gain_hbm, gain_ref),
                (slot_hbm, slot_s),
                (length_hbm, length_s),
                (position_hbm, position_s),
                (frequency_hbm, frequency_ref),
            ]
        )
    ]
    weight_loads = [
        [
            pltpu.make_async_copy(
                src.at[pl.ds(k * shallow, shallow)],
                dst.at[pl.ds(k * shallow, shallow)],
                fresh_sem(),
            )
            for src, dst in [(wkv_hbm, wkv), (wq_hbm, wq)]
        ]
        for k in range(4)
    ]
    cache_loads = [
        pltpu.make_async_copy(cache_hbm.at[layer], cache.at[layer], fresh_sem())
        for layer in range(LAYERS)
    ]
    wo_sem = fresh_sem()
    wo_loads = [
        pltpu.make_async_copy(wo_hbm.at[:, pl.ds(j * chunk, chunk)], wo.at[j], wo_sem)
        for j in range(n_mp)
    ]
    wo_arrival = pltpu.make_async_copy(wo, wo, wo_sem)
    loads = [cache_loads[0]] + wo_loads + cache_loads[1:]
    for one in small[:3]:
        one.start()
    for both in weight_loads:
        for one in both:
            one.start()

    barrier = pltpu.get_barrier_semaphore()
    for pair in others:
        pl.semaphore_signal(
            barrier, inc=1, device_id=place_of[pair], device_id_type=pl.DeviceIdType.MESH
        )
    for one in small[3:]:
        one.start()

    for one in small[:3]:
        one.wait()
    sublanes = lax.broadcasted_iota(jnp.int32, (rows, rows), 0)
    place = jnp.where(slot_row[...] == sublanes, 1.0, 0.0).astype(bf16)
    gains = gain_ref[...].astype(f32)
    for c in range(n_mp):
        state[0, c] = lax.dot_general(
            place,
            hidden_ref[:, c * chunk : (c + 1) * chunk],
            (((0,), (0,)), ((), ())),
            preferred_element_type=f32,
        ).astype(bf16)

    unsent = []

    def remote(src, dst, ssem, rsem, where):
        copy = pltpu.make_async_remote_copy(
            src_ref=src,
            dst_ref=dst,
            send_sem=ssem,
            recv_sem=rsem,
            device_id=where,
            device_id_type=pl.DeviceIdType.MESH,
        )
        copy.start()
        return copy

    def single(src, dst, where):
        copy = remote(src, dst, fresh_sem(), fresh_sem(), where)
        unsent.append(copy.wait_send)
        return copy

    def whole(ref, sem):
        return pltpu.make_async_copy(ref, ref, sem).wait

    def gather_chunks(layer, places, fresh_start):
        squares = square_sum_buf[...]
        pieces = []
        for c in places:
            floats = state[layer, c].astype(f32)
            for t in range(chunk // 128):
                piece = floats[:, t * 128 : (t + 1) * 128]
                pieces.append((piece * gain_rows[c, t]).astype(bf16))
                squares = squares + piece * piece
        square_sum_buf[...] = squares
        depth = len(places) * chunk
        start = places[0] * chunk
        if not isinstance(start, int):
            start = pl.multiple_of(start, chunk)
        left = jnp.concatenate(pieces, axis=1)
        wide = 256
        for b in range(-1, query_cols // wide):
            if b < 0:
                weights = wkv[pl.ds(start, depth), :]
                at = query_cols
                span = keyval_cols
            else:
                weights = wq[pl.ds(start, depth), b * wide : (b + 1) * wide]
                at = b * wide
                span = wide
            product = jnp.dot(left, weights, preferred_element_type=f32)
            if fresh_start:
                sums[:, at : at + span] = product
            else:
                sums[:, at : at + span] += product

    def prepare(layer):
        square_row = jnp.broadcast_to(
            jnp.sum(square_sum_buf[...], axis=1, keepdims=True), (rows, 128)
        )
        product = sums[:, query_cols:].reshape(n_dp, band, keyval_cols)
        kv_send[layer] = product.astype(LINK)
        for g in range(group):
            stage[:, g, :] = sums[:, g * head_dim : (g + 1) * head_dim]
        q_send[layer] = stage[...].reshape(n_dp * n_mp, packed, head_dim).astype(bf16)
        for i in range(n_dp):
            for j in range(n_mp):
                at = (i * n_mp + j) * owned
                square_send[layer, i, j] = square_row[at : at + owned]

    for c in range(n_mp):
        for t in range(chunk // 128):
            at = c * (chunk // 128) + t
            gain_rows[c, t] = gains[at : at + 1]
    square_sum_buf[...] = jnp.zeros((rows, 128), f32)
    for k, both in enumerate(weight_loads):
        for one in both:
            one.wait()
        if k == 3:
            for one in loads:
                one.start()
        per_load = n_mp // 4
        gather_chunks(0, [k * per_load + i for i in range(per_load)], k == 0)
    prepare(0)
    turns = []
    pl.semaphore_wait(barrier, len(others))

    for layer in range(LAYERS):
        kv_out, kv_in, sq_out, sq_in = fresh_sem(), fresh_sem(), fresh_sem(), fresh_sem()
        for kd in reversed(range(1, n_dp)):
            to = flipped(d, kd, d_bits)
            remote(
                kv_send.at[layer, to], kv_recv.at[layer, kd - 1], kv_out, kv_in, {"dp": to}
            )
        for kd in reversed(range(1, n_dp)):
            to = flipped(d, kd, d_bits)
            remote(
                square_send.at[layer, to, m],
                square_recv.at[layer, kd - 1],
                sq_out,
                sq_in,
                {"dp": to},
            )
        unsent.append(whole(kv_recv.at[layer], kv_out))
        unsent.append(whole(square_recv.at[layer], sq_out))
        part = key_heads // 2
        mine = d * n_mp + m
        q_out, q_in = fresh_sem(), [fresh_sem(), fresh_sem()]
        for kd, km in others:
            where = place_of[kd, km]
            remote(
                q_send.at[layer, where["dp"] * n_mp + where["mp"]],
                q_recv.at[layer, mine],
                q_out,
                q_in[km // part],
                where,
            )
        unsent.append(whole(q_recv.at[layer, pl.ds(0, len(others))], q_out))
        q_recv[layer, mine] = q_send[layer, mine]
        if layer == 0:
            for one in small[3:]:
                one.wait()
            for r in range(owned):
                slot = slot_s[(d * n_mp + m) * owned + r]
                at = jnp.full((group, head_dim), position_s[slot], jnp.int32).astype(f32)
                angles = at * frequency_ref[...]
                lane = lax.broadcasted_iota(jnp.int32, (group, head_dim), 1)
                sines = jnp.sin(angles)
                turns.append(
                    (
                        jnp.cos(angles),
                        jnp.where(lane < head_dim // 2, -sines, sines),
                        length_s[slot],
                    )
                )
        whole(kv_recv.at[layer], kv_in)()
        total = sums[pl.ds(pl.multiple_of(d * band, band), band), query_cols:]
        for kd in range(1, n_dp):
            total = total + kv_recv[layer, kd - 1].astype(f32)
        for j in range(n_mp):
            row_send[layer, j] = total[j * owned : (j + 1) * owned]
        row_out, row_in = fresh_sem(), fresh_sem()
        for km in reversed(range(1, n_mp)):
            to = flipped(m, km, m_bits)
            remote(row_send.at[layer, to], row_recv.at[layer, m], row_out, row_in, {"mp": to})
        unsent.append(whole(row_recv.at[layer, pl.ds(0, n_mp - 1)], row_out))
        row_recv[layer, m] = row_send[layer, m]
        if layer == 0:
            wo_arrival.wait()
            swap_out, swap_in = fresh_sem(), fresh_sem()
            for q in range(half):
                remote(
                    wo.at[(1 - core) * half + q],
                    wo_other.at[q],
                    swap_out,
                    swap_in,
                    {"mp": sibling},
                )
            unsent.append(whole(wo_other, swap_out))
        whole(square_recv.at[layer], sq_in)()
        square_sum = square_send[layer, d, m]
        for kd in range(1, n_dp):
            square_sum = square_sum + square_recv[layer, kd - 1]
        inverse_rms = lax.rsqrt(square_sum / model_width + norm_eps)

        def turned(x, r):
            cosines, sines, _ = turns[r]
            return x * cosines + pltpu.roll(x, head_dim // 2, 1) * sines

        cache_loads[layer].wait()
        per = keyval_cols // head_dim
        key_sources = key_heads // per
        first_base = (m // part) * part
        bases = [first_base, part - first_base]
        rests = {}
        for step, base in enumerate(bases):
            count = n_dp * part - (1 if step == 0 else 0)
            whole(q_recv.at[layer, pl.ds(0, count)], q_in[step])()
            raw = q_recv[layer, pl.ds(base, part)].astype(f32)
            for i in range(1, n_dp):
                raw = raw + q_recv[layer, pl.ds(i * n_mp + base, part)].astype(f32)
            raw = raw.reshape(part, owned, group, head_dim)
            for r in range(owned):
                asked = jnp.concatenate(
                    [turned(raw[j, r] * inverse_rms[r : r + 1], r)[None] for j in range(part)],
                    axis=0,
                ).astype(bf16)
                score = (
                    lax.dot_general(
                        asked,
                        cache[layer, r, 0, pl.ds(base, part)],
                        (((2,), (2,)), ((0,), (0,))),
                        preferred_element_type=f32,
                    )
                    * score_scale
                )
                at = lax.broadcasted_iota(jnp.int32, score.shape, 2)
                score = jnp.where(at < turns[r][2], score, -jnp.inf)
                peak = jnp.max(score, axis=2, keepdims=True)
                weights = jnp.exp(score - peak)
                summed = lax.dot_general(
                    weights.astype(bf16),
                    cache[layer, r, 1, pl.ds(base, part)],
                    (((2,), (1,)), ((0,), (0,))),
                    preferred_element_type=f32,
                )
                rests[step, r] = (
                    asked.astype(f32),
                    peak,
                    jnp.sum(weights, axis=2, keepdims=True),
                    summed,
                )
        whole(row_recv.at[layer, pl.ds(0, n_mp - 1)], row_in)()
        for r in range(owned):
            for t in range(per):
                fresh = (
                    row_recv[layer, :, r, t * head_dim : (t + 1) * head_dim]
                    * inverse_rms[r : r + 1]
                )
                keys_fresh = turned(fresh, r)
                for source in range(n_mp):
                    kind = source // key_sources
                    head = (source % key_sources) * per + t
                    row = keys_fresh if kind == 0 else fresh
                    fresh_buf[r, kind, head] = row[source : source + 1]
        at_out, at_in = fresh_sem(), fresh_sem()
        for step, base in enumerate(bases):
            results = []
            for r in range(owned):
                asked, peak, denominator, summed = rests[step, r]
                fresh_keys = fresh_buf[r, 0, pl.ds(base, part)].astype(bf16).astype(f32)
                fresh_values = fresh_buf[r, 1, pl.ds(base, part)].astype(bf16).astype(f32)
                own_score = jnp.sum(asked * fresh_keys, axis=2, keepdims=True) * score_scale
                highest = jnp.maximum(peak, own_score)
                shrink = jnp.exp(peak - highest)
                own_weight = jnp.exp(own_score - highest)
                own_rounded = own_weight.astype(bf16).astype(f32)
                results.append(
                    (summed * shrink + own_rounded * fresh_values)
                    / (denominator * shrink + own_weight)
                )
            att_send[layer, pl.ds(base, part)] = jnp.concatenate(results, axis=1).astype(bf16)
            for kd, km in others:
                if km // part == step:
                    where = place_of[kd, km]
                    remote(
                        att_send.at[layer, where["mp"]],
                        gathered.at[layer, mine],
                        at_out,
                        at_in,
                        where,
                    )
        unsent.append(whole(gathered.at[layer, pl.ds(0, len(others))], at_out))
        gathered[layer, mine] = att_send[layer, m]
        whole(gathered.at[layer, pl.ds(0, len(others))], at_in)()
        att_stage[...] = gathered[layer].astype(f32).reshape(rows, group, head_dim)
        left = jnp.concatenate(
            [att_stage[:, g, :].astype(bf16) for g in range(group)], axis=1
        )
        left_send[layer] = left
        left_copy = single(left_send.at[layer], left_recv.at[layer], {"mp": sibling})
        for q in range(half):
            out_acc[q] = jnp.dot(left, wo[core * half + q], preferred_element_type=f32)
        if layer == 0:
            whole(wo_other, swap_in)()
        left_copy.wait_recv()
        other_left = left_recv[layer]
        staged = half // 2
        chip = m // 2
        first_copies, second_copies, direct_in = [], [], []
        for q in range(half):
            product = jnp.dot(other_left, wo_other[q], preferred_element_type=f32)
            chip_sum = (product + out_acc[q]).astype(LINK)
            if q < staged:
                first_send[layer, q] = chip_sum
                first_copies.append(
                    single(
                        first_send.at[layer, q],
                        first_recv.at[layer, q],
                        {"mp": flipped(m, 2 if q % 2 == 0 else 4, m_bits)},
                    )
                )
            else:
                direct_all[layer, q - staged, chip] = chip_sum
                di_out, di_in = fresh_sem(), fresh_sem()
                for k in (3, 1, 2):
                    remote(
                        direct_all.at[layer, q - staged, chip],
                        direct_all.at[layer, q - staged, chip],
                        di_out,
                        di_in,
                        {"mp": flipped(m, 2 * k, m_bits)},
                    )
                three = direct_all.at[layer, q - staged, pl.ds(0, half - 1)]
                unsent.append(whole(three, di_out))
                direct_in.append(whole(three, di_in))
        for q in range(staged):
            first_copies[q].wait_recv()
            both = first_send[layer, q].astype(f32) + first_recv[layer, q].astype(f32)
            second_send[layer, q] = both.astype(LINK)
            second_copies.append(
                single(
                    second_send.at[layer, q],
                    second_recv.at[layer, q],
                    {"mp": flipped(m, 4 if q % 2 == 0 else 2, m_bits)},
                )
            )
        arriving = {}
        order = list(range(staged, half)) + list(range(staged))
        if layer + 1 < LAYERS:
            square_sum_buf[...] = jnp.zeros((rows, 128), f32)
        for i, q in enumerate(order):
            at = core * half + q
            if q < staged:
                second_copies[q].wait_recv()
                total = second_send[layer, q].astype(f32) + second_recv[layer, q].astype(f32)
            else:
                direct_in[q - staged]()
                total = direct_all[layer, q - staged, 0].astype(f32)
                for c in range(1, n_mp // 2):
                    total = total + direct_all[layer, q - staged, c].astype(f32)
            state[layer + 1, at] = (state[layer, at].astype(f32) + total).astype(bf16)
            arriving[q] = single(
                state.at[layer + 1, at], state.at[layer + 1, at], {"mp": sibling}
            )
            if layer + 1 < LAYERS and i % 2 == 1:
                gather_chunks(layer + 1, [at - 1, at], i == 1)
        for i, q in enumerate(order):
            arriving[q].wait_recv()
            if layer + 1 < LAYERS and i % 2 == 1:
                at = (1 - core) * half + q
                gather_chunks(layer + 1, [at - 1, at], False)
        if layer + 1 < LAYERS:
            prepare(layer + 1)
    for c in range(n_mp):
        out_ref[:, c * chunk : (c + 1) * chunk] = jnp.dot(
            place, state[LAYERS, c], preferred_element_type=f32
        ).astype(bf16)
    for wait in unsent:
        wait()


def fused(
    hidden_in, norm_gain, w_query, w_keyval, w_out, cache_slots, lengths, positions, slot_order
):
    n_dp = lax.axis_size("dp")
    n_mp = lax.axis_size("mp")
    rows, width = hidden_in.shape
    query_cols = w_query.shape[1]
    keyval_cols = w_keyval.shape[1]
    owned, key_heads, cache_rows, head_dim = (
        cache_slots.shape[1],
        cache_slots.shape[3],
        cache_slots.shape[4],
        cache_slots.shape[5],
    )
    group = query_cols // head_dim
    packed = owned * group
    band = rows // n_dp
    chunk = width // n_mp
    half = n_mp // 2
    index_row = np.arange(head_dim) % (head_dim // 2)
    frequency = np.exp(index_row * (-2.0 * math.log(rope_base) / head_dim))
    frequency = jnp.asarray(frequency[None].astype(np.float32))
    sizes = (n_dp, n_mp, rows, width, query_cols, keyval_cols, owned, key_heads, head_dim)
    vmem = pl.BlockSpec(memory_space=pltpu.VMEM)
    anywhere = pl.BlockSpec(memory_space=pl.ANY)
    f32, bf16 = jnp.float32, jnp.bfloat16
    dma = pltpu.SemaphoreType.DMA
    return pl.pallas_call(
        functools.partial(fused_kernel, sizes),
        out_shape=jax.ShapeDtypeStruct((rows, width), bf16),
        in_specs=[anywhere] * 11,
        out_specs=vmem,
        scratch_shapes=[
            pltpu.SMEM((rows,), jnp.int32),
            pltpu.SMEM((rows,), jnp.int32),
            pltpu.SMEM((rows,), jnp.int32),
            pltpu.VMEM((1, rows), jnp.int32),
            pltpu.VMEM((1, head_dim), f32),
            pltpu.VMEM((rows, width), bf16),
            pltpu.VMEM((width // 128, 128), bf16),
            pltpu.VMEM(w_query.shape, bf16),
            pltpu.VMEM(w_keyval.shape, bf16),
            pltpu.VMEM((n_mp, query_cols, chunk), bf16),
            pltpu.VMEM((half, query_cols, chunk), bf16),
            pltpu.VMEM(cache_slots.shape, bf16),
            pltpu.VMEM((LAYERS + 1, n_mp, rows, chunk), bf16),
            pltpu.VMEM((LAYERS, n_dp, n_mp, owned, 128), f32),
            pltpu.VMEM((LAYERS, n_dp - 1, owned, 128), f32),
            pltpu.VMEM((rows, query_cols + keyval_cols), f32),
            pltpu.VMEM((rows, 128), f32),
            pltpu.VMEM((n_mp, chunk // 128, 1, 128), f32),
            pltpu.VMEM((LAYERS, n_dp, band, keyval_cols), LINK),
            pltpu.VMEM((LAYERS, n_dp - 1, band, keyval_cols), LINK),
            pltpu.VMEM((LAYERS, n_mp, owned, keyval_cols), f32),
            pltpu.VMEM((LAYERS, n_mp, owned, keyval_cols), f32),
            pltpu.VMEM((owned, 2, key_heads, 1, head_dim), f32),
            pltpu.VMEM((rows, group, head_dim), f32),
            pltpu.VMEM((LAYERS, n_dp * n_mp, packed, head_dim), LINK),
            pltpu.VMEM((LAYERS, n_dp * n_mp, packed, head_dim), LINK),
            pltpu.VMEM((LAYERS, n_mp, packed, head_dim), bf16),
            pltpu.VMEM((LAYERS, n_dp * n_mp, packed, head_dim), bf16),
            pltpu.VMEM((rows, group, head_dim), f32),
            pltpu.VMEM((LAYERS, rows, query_cols), bf16),
            pltpu.VMEM((LAYERS, rows, query_cols), bf16),
            pltpu.VMEM((half, rows, chunk), f32),
            pltpu.VMEM((LAYERS, half // 2, rows, chunk), LINK),
            pltpu.VMEM((LAYERS, half // 2, rows, chunk), LINK),
            pltpu.VMEM((LAYERS, half // 2, rows, chunk), LINK),
            pltpu.VMEM((LAYERS, half // 2, rows, chunk), LINK),
            pltpu.VMEM((LAYERS, half // 2, half, rows, chunk), LINK),
            dma((20 + LAYERS * 34,)),
        ],
        compiler_params=pltpu.CompilerParams(
            collective_id=0, has_side_effects=True, vmem_limit_bytes=56 << 20
        ),
    )(
        slot_order,
        lengths,
        positions,
        slot_order.reshape(1, rows),
        frequency,
        hidden_in,
        norm_gain.reshape(width // 128, 128),
        w_query,
        w_keyval,
        w_out,
        cache_slots,
    )


def dispatch(
    hidden_in, norm_gain, w_query, w_keyval, w_out, cache_slots, lengths, positions, slot_order
):
    n_mp = lax.axis_size("mp")
    key_heads = cache_slots.shape[3]
    head_dim = cache_slots.shape[5]
    fits = (
        key_heads == n_mp
        and n_mp == 8
        and lax.axis_size("dp") == 4
        and cache_slots.shape[1] * (w_query.shape[1] // head_dim) % 16 == 0
        and (w_query.shape[1] // head_dim) == 8
        and w_keyval.shape[1] % head_dim == 0
        and w_query.shape[1] % w_keyval.shape[1] == 0
        and hidden_in.shape[1] % (128 * n_mp) == 0
        and hidden_in.shape[0] % (16 * lax.axis_size("dp")) == 0
    )
    chosen = fused if fits else shards
    return chosen(
        hidden_in, norm_gain, w_query, w_keyval, w_out, cache_slots, lengths, positions, slot_order
    )


def solution(mesh):
    placed = (
        P(None, "dp"),
        P("dp"),
        P("dp", "mp"),
        P("dp", "mp"),
        P("mp", "dp"),
        P(None, ("dp", "mp"), None, None, None, None),
        P(),
        P(),
        P(),
    )
    return jax.shard_map(
        dispatch, mesh=mesh, in_specs=placed, out_specs=P(None, "dp"), check_vma=False
    )
```

```python
import functools
import math

import jax
import jax.numpy as jnp
import numpy as np
from jax import lax
from jax.experimental import pallas as pl
from jax.experimental.pallas import tpu as pltpu
from jax.sharding import PartitionSpec as P

LAYERS = 2


norm_eps = 1e-05
rope_base = 500000.0


def rotate(values, at_positions):
    half_dim = values.shape[-1] // 2
    index_row = jnp.arange(half_dim, dtype=jnp.float32)
    frequency = jnp.exp(index_row * (-2.0 * math.log(rope_base) / values.shape[-1]))
    angles = at_positions.astype(jnp.float32)[:, None, None] * frequency
    cosines = jnp.cos(angles)
    sine_rows = jnp.sin(angles)
    first_half = values[..., :half_dim]
    second_half = values[..., half_dim:]
    return jnp.concatenate(
        [
            first_half * cosines - second_half * sine_rows,
            second_half * cosines + first_half * sine_rows,
        ],
        axis=-1,
    )


def attend(queries, fresh_keys, fresh_values, key_rows, values, slot_lengths):
    score_scale = 1.0 / math.sqrt(queries.shape[-1])
    scores = (
        jnp.einsum("rkgd,rktd->rkgt", queries, key_rows, preferred_element_type=jnp.float32)
        * score_scale
    )
    own_score = (
        jnp.einsum("rkgd,rkd->rkg", queries, fresh_keys, preferred_element_type=jnp.float32)
        * score_scale
    )
    positions_row = lax.broadcasted_iota(jnp.int32, (1, 1, 1, key_rows.shape[2]), 3)
    valid_keys = positions_row < slot_lengths[:, None, None, None]
    scores = jnp.where(valid_keys, scores, -jnp.inf)
    highest = jnp.maximum(jnp.max(scores, axis=-1), own_score)
    weights = jnp.exp(scores - highest[..., None])
    own_weight = jnp.exp(own_score - highest)
    denominator = jnp.sum(weights, axis=-1) + own_weight
    rounded = weights.astype(jnp.bfloat16)
    own_rounded = lax.optimization_barrier(own_weight.astype(jnp.bfloat16)).astype(jnp.float32)
    summed = jnp.einsum("rkgt,rktd->rkgd", rounded, values, preferred_element_type=jnp.float32)
    summed = summed + own_rounded[..., None] * fresh_values.astype(jnp.float32)[:, :, None, :]
    return (summed / denominator[..., None]).astype(jnp.bfloat16)


def shards(
    hidden_in, norm_gain, w_query, w_keyval, w_out, cache_slots, lengths, positions, slot_order
):
    total_rows = hidden_in.shape[0]
    data_count = lax.axis_size("dp")
    model_count = lax.axis_size("mp")
    owned_rows = cache_slots.shape[1]
    key_heads = cache_slots.shape[3]
    head_dim = cache_slots.shape[5]
    query_cols = w_query.shape[1]
    head_count = query_cols * model_count // head_dim
    group_size = head_count // key_heads
    model_width = hidden_in.shape[1] * data_count
    half_width = key_heads * head_dim
    inverse = (
        jnp.zeros((total_rows,), jnp.int32)
        .at[slot_order]
        .set(jnp.arange(total_rows, dtype=jnp.int32))
    )
    device_index = lax.axis_index("dp") * model_count + lax.axis_index("mp")
    slot_lengths = lax.dynamic_slice_in_dim(
        jnp.take(lengths, slot_order), device_index * owned_rows, owned_rows
    )
    slot_positions = lax.dynamic_slice_in_dim(
        jnp.take(positions, slot_order), device_index * owned_rows, owned_rows
    )
    gain_float = norm_gain.astype(jnp.float32)
    current = jnp.take(hidden_in, slot_order, axis=0)
    for layer_index in range(LAYERS):
        floats = current.astype(jnp.float32)
        squares = jnp.sum(floats * floats, axis=1)
        scaled = (floats * gain_float).astype(jnp.bfloat16)
        partial_value = jnp.concatenate(
            [
                jnp.dot(scaled, w_query, preferred_element_type=jnp.float32),
                jnp.dot(scaled, w_keyval, preferred_element_type=jnp.float32),
            ],
            axis=1,
        )
        summed = lax.psum_scatter(partial_value, "dp", scatter_dimension=0, tiled=True)
        square_sum = lax.psum_scatter(squares, "dp", scatter_dimension=0, tiled=True)
        inverse_rms = lax.rsqrt(square_sum / model_width + norm_eps)
        projected = summed * inverse_rms[:, None]
        arrived = lax.all_to_all(projected, "mp", split_axis=0, concat_axis=1, tiled=True)
        arrived = arrived.reshape(owned_rows, model_count, projected.shape[1])
        query_part = arrived[:, :, :query_cols].reshape(owned_rows, head_count, head_dim)
        keyval_part = arrived[:, :, query_cols:].reshape(owned_rows, 2 * half_width)
        queries = (
            rotate(query_part, slot_positions)
            .astype(jnp.bfloat16)
            .reshape(owned_rows, key_heads, group_size, head_dim)
        )
        fresh_keys = rotate(
            keyval_part[:, :half_width].reshape(owned_rows, key_heads, head_dim), slot_positions
        ).astype(jnp.bfloat16)
        fresh_values = (
            keyval_part[:, half_width:]
            .reshape(owned_rows, key_heads, head_dim)
            .astype(jnp.bfloat16)
        )
        layer_cache = cache_slots[layer_index]
        attended = attend(
            queries, fresh_keys, fresh_values, layer_cache[:, 0], layer_cache[:, 1], slot_lengths
        )
        attended = attended.reshape(owned_rows, head_count * head_dim)
        returned = lax.all_to_all(attended, "mp", split_axis=1, concat_axis=0, tiled=True)
        partial_out = jnp.dot(
            lax.all_gather(returned, "dp", axis=0, tiled=True),
            w_out,
            preferred_element_type=jnp.float32,
        )
        totals = lax.psum(partial_out, "mp")
        current = (floats + totals).astype(jnp.bfloat16)
    return jnp.take(current, inverse, axis=0)


LINK = jnp.bfloat16


def flipped(at, mask, bits):
    turned_at = 0
    for b in range(bits):
        bit = (at // (1 << b)) % 2
        if (mask >> b) & 1:
            bit = 1 - bit
        turned_at = turned_at + bit * (1 << b)
    return turned_at


def fused_kernel(
    sizes,
    slot_hbm,
    length_hbm,
    position_hbm,
    slot_row_hbm,
    frequency_hbm,
    hidden_hbm,
    gain_hbm,
    wq_hbm,
    wkv_hbm,
    wo_hbm,
    cache_hbm,
    out_ref,
    slot_s,
    length_s,
    position_s,
    slot_row,
    frequency_ref,
    hidden_ref,
    gain_ref,
    wq,
    wkv,
    wo,
    wo_other,
    cache,
    state,
    square_send,
    square_recv,
    sums,
    square_sum_buf,
    gain_rows,
    kv_send,
    kv_recv,
    row_send,
    row_recv,
    fresh_buf,
    stage,
    q_send,
    q_recv,
    att_send,
    gathered,
    att_stage,
    left_send,
    left_recv,
    out_acc,
    first_send,
    first_recv,
    second_send,
    second_recv,
    direct_all,
    sems,
):
    n_dp, n_mp, rows, width, query_cols, keyval_cols, owned, key_heads, head_dim = sizes
    band = rows // n_dp
    chunk = width // n_mp
    group = query_cols // head_dim
    packed = owned * group
    half = n_mp // 2
    side = rows // 2
    d_bits, m_bits = n_dp.bit_length() - 1, n_mp.bit_length() - 1
    f32, bf16 = jnp.float32, jnp.bfloat16
    d = lax.axis_index("dp")
    m = lax.axis_index("mp")
    model_width = width * n_dp
    core = lax.rem(m, 2)
    sibling = m + 1 - 2 * core
    score_scale = 1.0 / math.sqrt(head_dim)
    others = [
        (kd, km) for kd in reversed(range(n_dp)) for km in reversed(range(n_mp)) if kd or km
    ]
    place_of = {
        (kd, km): {"dp": flipped(d, kd, d_bits), "mp": flipped(m, km, m_bits)}
        for kd, km in others
    }

    taken = []

    def fresh_sem():
        taken.append(0)
        return sems.at[len(taken) - 1]

    shallow = width // 4
    small = [
        pltpu.make_async_copy(src, dst, fresh_sem())
        for src, dst in (
            [
                (slot_row_hbm, slot_row),
                (hidden_hbm, hidden_ref),
                (gain_hbm, gain_ref),
                (slot_hbm, slot_s),
                (length_hbm, length_s),
                (position_hbm, position_s),
                (frequency_hbm, frequency_ref),
            ]
        )
    ]
    weight_loads = [
        [
            pltpu.make_async_copy(
                src.at[pl.ds(k * shallow, shallow)],
                dst.at[pl.ds(k * shallow, shallow)],
                fresh_sem(),
            )
            for src, dst in [(wkv_hbm, wkv), (wq_hbm, wq)]
        ]
        for k in range(4)
    ]
    cache_loads = [
        pltpu.make_async_copy(cache_hbm.at[layer], cache.at[layer], fresh_sem())
        for layer in range(LAYERS)
    ]
    wo_sem = fresh_sem()
    wo_loads = [
        pltpu.make_async_copy(wo_hbm.at[:, pl.ds(j * chunk, chunk)], wo.at[j], wo_sem)
        for j in range(n_mp)
    ]
    wo_arrival = pltpu.make_async_copy(wo, wo, wo_sem)
    loads = [cache_loads[0]] + wo_loads + cache_loads[1:]
    for one in small[:3]:
        one.start()
    for both in weight_loads:
        for one in both:
            one.start()

    barrier = pltpu.get_barrier_semaphore()
    for pair in others:
        pl.semaphore_signal(
            barrier, inc=1, device_id=place_of[pair], device_id_type=pl.DeviceIdType.MESH
        )
    for one in small[3:]:
        one.start()

    for one in small[:3]:
        one.wait()
    sublanes = lax.broadcasted_iota(jnp.int32, (rows, rows), 0)
    place = jnp.where(slot_row[...] == sublanes, 1.0, 0.0).astype(bf16)
    gains = gain_ref[...].astype(f32)
    for c in range(n_mp):
        state[0, c] = (
            lax.dot_general(
                place,
                hidden_ref[:, c * chunk : (c + 1) * chunk],
                (((0,), (0,)), ((), ())),
                preferred_element_type=f32,
            )
            .astype(bf16)
            .reshape(2, side, chunk)
        )

    unsent = []

    def remote(src, dst, ssem, rsem, where):
        copy = pltpu.make_async_remote_copy(
            src_ref=src,
            dst_ref=dst,
            send_sem=ssem,
            recv_sem=rsem,
            device_id=where,
            device_id_type=pl.DeviceIdType.MESH,
        )
        copy.start()
        return copy

    def single(src, dst, where):
        copy = remote(src, dst, fresh_sem(), fresh_sem(), where)
        unsent.append(copy.wait_send)
        return copy

    def whole(ref, sem):
        return pltpu.make_async_copy(ref, ref, sem).wait

    def gather_chunks(layer, places, fresh_start):
        squares = square_sum_buf[...]
        pieces = []
        for c in places:
            floats = state[layer, c].reshape(rows, chunk).astype(f32)
            for t in range(chunk // 128):
                piece = floats[:, t * 128 : (t + 1) * 128]
                pieces.append((piece * gain_rows[c, t]).astype(bf16))
                squares = squares + piece * piece
        square_sum_buf[...] = squares
        depth = len(places) * chunk
        start = places[0] * chunk
        if not isinstance(start, int):
            start = pl.multiple_of(start, chunk)
        left = jnp.concatenate(pieces, axis=1)
        wide = 256
        for b in range(-1, query_cols // wide):
            if b < 0:
                weights = wkv[pl.ds(start, depth), :]
                at = query_cols
                span = keyval_cols
            else:
                weights = wq[pl.ds(start, depth), b * wide : (b + 1) * wide]
                at = b * wide
                span = wide
            product = jnp.dot(left, weights, preferred_element_type=f32)
            if fresh_start:
                sums[:, at : at + span] = product
            else:
                sums[:, at : at + span] += product

    def prepare(layer):
        square_row = jnp.broadcast_to(
            jnp.sum(square_sum_buf[...], axis=1, keepdims=True), (rows, 128)
        )
        product = sums[:, query_cols:].reshape(n_dp, band, keyval_cols)
        kv_send[layer] = product.astype(LINK)
        for g in range(group):
            stage[:, g, :] = sums[:, g * head_dim : (g + 1) * head_dim]
        q_send[layer] = stage[...].reshape(n_dp * n_mp, packed, head_dim).astype(bf16)
        for i in range(n_dp):
            for j in range(n_mp):
                at = (i * n_mp + j) * owned
                square_send[layer, i, j] = square_row[at : at + owned]

    for c in range(n_mp):
        for t in range(chunk // 128):
            at = c * (chunk // 128) + t
            gain_rows[c, t] = gains[at : at + 1]
    square_sum_buf[...] = jnp.zeros((rows, 128), f32)
    for k, both in enumerate(weight_loads):
        for one in both:
            one.wait()
        if k == 3:
            for one in loads:
                one.start()
        per_load = n_mp // 4
        gather_chunks(0, [k * per_load + i for i in range(per_load)], k == 0)
    prepare(0)
    turns = []
    pl.semaphore_wait(barrier, len(others))

    for layer in range(LAYERS):
        kv_out, kv_in, sq_out, sq_in = fresh_sem(), fresh_sem(), fresh_sem(), fresh_sem()
        for kd in reversed(range(1, n_dp)):
            to = flipped(d, kd, d_bits)
            remote(
                kv_send.at[layer, to], kv_recv.at[layer, kd - 1], kv_out, kv_in, {"dp": to}
            )
        for kd in reversed(range(1, n_dp)):
            to = flipped(d, kd, d_bits)
            remote(
                square_send.at[layer, to, m],
                square_recv.at[layer, kd - 1],
                sq_out,
                sq_in,
                {"dp": to},
            )
        unsent.append(whole(kv_recv.at[layer], kv_out))
        unsent.append(whole(square_recv.at[layer], sq_out))
        part = key_heads // 2
        mine = d * n_mp + m
        q_out, q_in = fresh_sem(), [fresh_sem(), fresh_sem()]
        for kd, km in others:
            where = place_of[kd, km]
            remote(
                q_send.at[layer, where["dp"] * n_mp + where["mp"]],
                q_recv.at[layer, mine],
                q_out,
                q_in[km // part],
                where,
            )
        unsent.append(whole(q_recv.at[layer, pl.ds(0, len(others))], q_out))
        q_recv[layer, mine] = q_send[layer, mine]
        if layer == 0:
            for one in small[3:]:
                one.wait()
            for r in range(owned):
                slot = slot_s[(d * n_mp + m) * owned + r]
                at = jnp.full((group, head_dim), position_s[slot], jnp.int32).astype(f32)
                angles = at * frequency_ref[...]
                lane = lax.broadcasted_iota(jnp.int32, (group, head_dim), 1)
                sines = jnp.sin(angles)
                turns.append(
                    (
                        jnp.cos(angles),
                        jnp.where(lane < head_dim // 2, -sines, sines),
                        length_s[slot],
                    )
                )
        whole(kv_recv.at[layer], kv_in)()
        total = sums[pl.ds(pl.multiple_of(d * band, band), band), query_cols:]
        for kd in range(1, n_dp):
            total = total + kv_recv[layer, kd - 1].astype(f32)
        for j in range(n_mp):
            row_send[layer, j] = total[j * owned : (j + 1) * owned]
        row_out, row_in = fresh_sem(), fresh_sem()
        for km in reversed(range(1, n_mp)):
            to = flipped(m, km, m_bits)
            remote(row_send.at[layer, to], row_recv.at[layer, m], row_out, row_in, {"mp": to})
        unsent.append(whole(row_recv.at[layer, pl.ds(0, n_mp - 1)], row_out))
        row_recv[layer, m] = row_send[layer, m]
        if layer == 0:
            wo_arrival.wait()
            swap_out, swap_in = fresh_sem(), fresh_sem()
            for q in range(half):
                remote(
                    wo.at[(1 - core) * half + q],
                    wo_other.at[q],
                    swap_out,
                    swap_in,
                    {"mp": sibling},
                )
            unsent.append(whole(wo_other, swap_out))
        whole(square_recv.at[layer], sq_in)()
        square_sum = square_send[layer, d, m]
        for kd in range(1, n_dp):
            square_sum = square_sum + square_recv[layer, kd - 1]
        inverse_rms = lax.rsqrt(square_sum / model_width + norm_eps)

        def turned(x, r):
            cosines, sines, _ = turns[r]
            return x * cosines + pltpu.roll(x, head_dim // 2, 1) * sines

        cache_loads[layer].wait()
        per = keyval_cols // head_dim
        key_sources = key_heads // per
        first_base = (m // part) * part
        bases = [first_base, part - first_base]
        rests = {}
        for step, base in enumerate(bases):
            count = n_dp * part - (1 if step == 0 else 0)
            whole(q_recv.at[layer, pl.ds(0, count)], q_in[step])()
            raw = q_recv[layer, pl.ds(base, part)].astype(f32)
            for i in range(1, n_dp):
                raw = raw + q_recv[layer, pl.ds(i * n_mp + base, part)].astype(f32)
            raw = raw.reshape(part, owned, group, head_dim)
            for r in range(owned):
                asked = jnp.concatenate(
                    [turned(raw[j, r] * inverse_rms[r : r + 1], r)[None] for j in range(part)],
                    axis=0,
                ).astype(bf16)
                score = (
                    lax.dot_general(
                        asked,
                        cache[layer, r, 0, pl.ds(base, part)],
                        (((2,), (2,)), ((0,), (0,))),
                        preferred_element_type=f32,
                    )
                    * score_scale
                )
                at = lax.broadcasted_iota(jnp.int32, score.shape, 2)
                score = jnp.where(at < turns[r][2], score, -jnp.inf)
                peak = jnp.max(score, axis=2, keepdims=True)
                weights = jnp.exp(score - peak)
                summed = lax.dot_general(
                    weights.astype(bf16),
                    cache[layer, r, 1, pl.ds(base, part)],
                    (((2,), (1,)), ((0,), (0,))),
                    preferred_element_type=f32,
                )
                rests[step, r] = (
                    asked.astype(f32),
                    peak,
                    jnp.sum(weights, axis=2, keepdims=True),
                    summed,
                )
        whole(row_recv.at[layer, pl.ds(0, n_mp - 1)], row_in)()
        for r in range(owned):
            for t in range(per):
                fresh = (
                    row_recv[layer, :, r, t * head_dim : (t + 1) * head_dim]
                    * inverse_rms[r : r + 1]
                )
                keys_fresh = turned(fresh, r)
                for source in range(n_mp):
                    kind = source // key_sources
                    head = (source % key_sources) * per + t
                    row = keys_fresh if kind == 0 else fresh
                    fresh_buf[r, kind, head] = row[source : source + 1]
        at_out, at_in = fresh_sem(), [fresh_sem(), fresh_sem()]
        for step, base in enumerate(bases):
            results = []
            for r in range(owned):
                asked, peak, denominator, summed = rests[step, r]
                fresh_keys = fresh_buf[r, 0, pl.ds(base, part)].astype(bf16).astype(f32)
                fresh_values = fresh_buf[r, 1, pl.ds(base, part)].astype(bf16).astype(f32)
                own_score = jnp.sum(asked * fresh_keys, axis=2, keepdims=True) * score_scale
                highest = jnp.maximum(peak, own_score)
                shrink = jnp.exp(peak - highest)
                own_weight = jnp.exp(own_score - highest)
                own_rounded = own_weight.astype(bf16).astype(f32)
                results.append(
                    (summed * shrink + own_rounded * fresh_values)
                    / (denominator * shrink + own_weight)
                )
            att_send[layer, pl.ds(base, part)] = jnp.concatenate(results, axis=1).astype(bf16)
            for kd, km in sorted(others, key=lambda one: (1, 0, 3, 2).index(one[0])):
                if km // part == step:
                    where = place_of[kd, km]
                    remote(
                        att_send.at[layer, where["mp"]],
                        gathered.at[layer, mine],
                        at_out,
                        at_in[kd // 2],
                        where,
                    )
        unsent.append(whole(gathered.at[layer, pl.ds(0, len(others))], at_out))
        gathered[layer, mine] = att_send[layer, m]
        chip = m // 2
        sides = [d // 2, 1 - d // 2]
        sources = n_dp * n_mp // 2
        first_copies, second_copies, direct_in = [], [], []
        for h, at_side in enumerate(sides):
            whole(gathered.at[layer, pl.ds(0, sources - 1 + h)], at_in[h])()
            att_stage[...] = (
                gathered[layer, pl.ds(at_side * sources, sources)]
                .astype(f32)
                .reshape(side, group, head_dim)
            )
            left = jnp.concatenate(
                [att_stage[:, g, :].astype(bf16) for g in range(group)], axis=1
            )
            left_send[layer, h] = left
            left_copy = single(left_send.at[layer, h], left_recv.at[layer, h], {"mp": sibling})
            for q in range(half):
                out_acc[q] = jnp.dot(left, wo[core * half + q], preferred_element_type=f32)
            if layer == 0 and h == 0:
                whole(wo_other, swap_in)()
            left_copy.wait_recv()
            other_left = left_recv[layer, h]
            for q in range(half):
                product = jnp.dot(other_left, wo_other[q], preferred_element_type=f32)
                chip_sum = (product + out_acc[q]).astype(LINK)
                if h == 0:
                    first_send[layer, q] = chip_sum
                    first_copies.append(
                        single(
                            first_send.at[layer, q],
                            first_recv.at[layer, q],
                            {"mp": flipped(m, 2 if q % 2 == 0 else 4, m_bits)},
                        )
                    )
                else:
                    direct_all[layer, q, chip] = chip_sum
                    di_out, di_in = fresh_sem(), fresh_sem()
                    for k in (3, 1, 2):
                        remote(
                            direct_all.at[layer, q, chip],
                            direct_all.at[layer, q, chip],
                            di_out,
                            di_in,
                            {"mp": flipped(m, 2 * k, m_bits)},
                        )
                    three = direct_all.at[layer, q, pl.ds(0, half - 1)]
                    unsent.append(whole(three, di_out))
                    direct_in.append(whole(three, di_in))
        for q in range(half):
            first_copies[q].wait_recv()
            both = first_send[layer, q].astype(f32) + first_recv[layer, q].astype(f32)
            second_send[layer, q] = both.astype(LINK)
            second_copies.append(
                single(
                    second_send.at[layer, q],
                    second_recv.at[layer, q],
                    {"mp": flipped(m, 4 if q % 2 == 0 else 2, m_bits)},
                )
            )
        arriving = {}
        if layer + 1 < LAYERS:
            square_sum_buf[...] = jnp.zeros((rows, 128), f32)
        for h, at_side in enumerate(sides):
            for q in range(half):
                at = core * half + q
                if h == 0:
                    second_copies[q].wait_recv()
                    total = second_send[layer, q].astype(f32) + second_recv[layer, q].astype(f32)
                else:
                    direct_in[q]()
                    total = direct_all[layer, q, 0].astype(f32)
                    for c in range(1, n_mp // 2):
                        total = total + direct_all[layer, q, c].astype(f32)
                state[layer + 1, at, at_side] = (
                    state[layer, at, at_side].astype(f32) + total
                ).astype(bf16)
                arriving[h, q] = single(
                    state.at[layer + 1, at, at_side],
                    state.at[layer + 1, at, at_side],
                    {"mp": sibling},
                )
        if layer + 1 < LAYERS:
            for q in range(1, half, 2):
                at = core * half + q
                gather_chunks(layer + 1, [at - 1, at], q == 1)
        for q in range(half):
            arriving[0, q].wait_recv()
            arriving[1, q].wait_recv()
            if layer + 1 < LAYERS and q % 2 == 1:
                at = (1 - core) * half + q
                gather_chunks(layer + 1, [at - 1, at], False)
        if layer + 1 < LAYERS:
            prepare(layer + 1)
    for c in range(n_mp):
        out_ref[:, c * chunk : (c + 1) * chunk] = jnp.dot(
            place, state[LAYERS, c].reshape(rows, chunk), preferred_element_type=f32
        ).astype(bf16)
    for wait in unsent:
        wait()


def fused(
    hidden_in, norm_gain, w_query, w_keyval, w_out, cache_slots, lengths, positions, slot_order
):
    n_dp = lax.axis_size("dp")
    n_mp = lax.axis_size("mp")
    rows, width = hidden_in.shape
    query_cols = w_query.shape[1]
    keyval_cols = w_keyval.shape[1]
    owned, key_heads, cache_rows, head_dim = (
        cache_slots.shape[1],
        cache_slots.shape[3],
        cache_slots.shape[4],
        cache_slots.shape[5],
    )
    group = query_cols // head_dim
    packed = owned * group
    band = rows // n_dp
    chunk = width // n_mp
    half = n_mp // 2
    index_row = np.arange(head_dim) % (head_dim // 2)
    frequency = np.exp(index_row * (-2.0 * math.log(rope_base) / head_dim))
    frequency = jnp.asarray(frequency[None].astype(np.float32))
    sizes = (n_dp, n_mp, rows, width, query_cols, keyval_cols, owned, key_heads, head_dim)
    vmem = pl.BlockSpec(memory_space=pltpu.VMEM)
    anywhere = pl.BlockSpec(memory_space=pl.ANY)
    f32, bf16 = jnp.float32, jnp.bfloat16
    dma = pltpu.SemaphoreType.DMA
    return pl.pallas_call(
        functools.partial(fused_kernel, sizes),
        out_shape=jax.ShapeDtypeStruct((rows, width), bf16),
        in_specs=[anywhere] * 11,
        out_specs=vmem,
        scratch_shapes=[
            pltpu.SMEM((rows,), jnp.int32),
            pltpu.SMEM((rows,), jnp.int32),
            pltpu.SMEM((rows,), jnp.int32),
            pltpu.VMEM((1, rows), jnp.int32),
            pltpu.VMEM((1, head_dim), f32),
            pltpu.VMEM((rows, width), bf16),
            pltpu.VMEM((width // 128, 128), bf16),
            pltpu.VMEM(w_query.shape, bf16),
            pltpu.VMEM(w_keyval.shape, bf16),
            pltpu.VMEM((n_mp, query_cols, chunk), bf16),
            pltpu.VMEM((half, query_cols, chunk), bf16),
            pltpu.VMEM(cache_slots.shape, bf16),
            pltpu.VMEM((LAYERS + 1, n_mp, 2, rows // 2, chunk), bf16),
            pltpu.VMEM((LAYERS, n_dp, n_mp, owned, 128), f32),
            pltpu.VMEM((LAYERS, n_dp - 1, owned, 128), f32),
            pltpu.VMEM((rows, query_cols + keyval_cols), f32),
            pltpu.VMEM((rows, 128), f32),
            pltpu.VMEM((n_mp, chunk // 128, 1, 128), f32),
            pltpu.VMEM((LAYERS, n_dp, band, keyval_cols), LINK),
            pltpu.VMEM((LAYERS, n_dp - 1, band, keyval_cols), LINK),
            pltpu.VMEM((LAYERS, n_mp, owned, keyval_cols), f32),
            pltpu.VMEM((LAYERS, n_mp, owned, keyval_cols), f32),
            pltpu.VMEM((owned, 2, key_heads, 1, head_dim), f32),
            pltpu.VMEM((rows, group, head_dim), f32),
            pltpu.VMEM((LAYERS, n_dp * n_mp, packed, head_dim), LINK),
            pltpu.VMEM((LAYERS, n_dp * n_mp, packed, head_dim), LINK),
            pltpu.VMEM((LAYERS, n_mp, packed, head_dim), bf16),
            pltpu.VMEM((LAYERS, n_dp * n_mp, packed, head_dim), bf16),
            pltpu.VMEM((rows // 2, group, head_dim), f32),
            pltpu.VMEM((LAYERS, 2, rows // 2, query_cols), bf16),
            pltpu.VMEM((LAYERS, 2, rows // 2, query_cols), bf16),
            pltpu.VMEM((half, rows // 2, chunk), f32),
            pltpu.VMEM((LAYERS, half, rows // 2, chunk), LINK),
            pltpu.VMEM((LAYERS, half, rows // 2, chunk), LINK),
            pltpu.VMEM((LAYERS, half, rows // 2, chunk), LINK),
            pltpu.VMEM((LAYERS, half, rows // 2, chunk), LINK),
            pltpu.VMEM((LAYERS, half, half, rows // 2, chunk), LINK),
            dma((20 + LAYERS * 56,)),
        ],
        compiler_params=pltpu.CompilerParams(
            collective_id=0, has_side_effects=True, vmem_limit_bytes=56 << 20
        ),
    )(
        slot_order,
        lengths,
        positions,
        slot_order.reshape(1, rows),
        frequency,
        hidden_in,
        norm_gain.reshape(width // 128, 128),
        w_query,
        w_keyval,
        w_out,
        cache_slots,
    )


def dispatch(
    hidden_in, norm_gain, w_query, w_keyval, w_out, cache_slots, lengths, positions, slot_order
):
    n_mp = lax.axis_size("mp")
    key_heads = cache_slots.shape[3]
    head_dim = cache_slots.shape[5]
    fits = (
        key_heads == n_mp
        and n_mp == 8
        and lax.axis_size("dp") == 4
        and cache_slots.shape[1] * (w_query.shape[1] // head_dim) % 16 == 0
        and (w_query.shape[1] // head_dim) == 8
        and w_keyval.shape[1] % head_dim == 0
        and w_query.shape[1] % w_keyval.shape[1] == 0
        and hidden_in.shape[1] % (128 * n_mp) == 0
        and hidden_in.shape[0] % (16 * lax.axis_size("dp")) == 0
    )
    chosen = fused if fits else shards
    return chosen(
        hidden_in, norm_gain, w_query, w_keyval, w_out, cache_slots, lengths, positions, slot_order
    )


def solution(mesh):
    placed = (
        P(None, "dp"),
        P("dp"),
        P("dp", "mp"),
        P("dp", "mp"),
        P("mp", "dp"),
        P(None, ("dp", "mp"), None, None, None, None),
        P(),
        P(),
        P(),
    )
    return jax.shard_map(
        dispatch, mesh=mesh, in_specs=placed, out_specs=P(None, "dp"), check_vma=False
    )
```

```python
import functools
import math

import jax
import jax.numpy as jnp
import numpy as np
from jax import lax
from jax.experimental import pallas as pl
from jax.experimental.pallas import tpu as pltpu
from jax.sharding import PartitionSpec as P

LAYERS = 2


norm_eps = 1e-05
rope_base = 500000.0


def rotate(values, at_positions):
    half_dim = values.shape[-1] // 2
    index_row = jnp.arange(half_dim, dtype=jnp.float32)
    frequency = jnp.exp(index_row * (-2.0 * math.log(rope_base) / values.shape[-1]))
    angles = at_positions.astype(jnp.float32)[:, None, None] * frequency
    cosines = jnp.cos(angles)
    sine_rows = jnp.sin(angles)
    first_half = values[..., :half_dim]
    second_half = values[..., half_dim:]
    return jnp.concatenate(
        [
            first_half * cosines - second_half * sine_rows,
            second_half * cosines + first_half * sine_rows,
        ],
        axis=-1,
    )


def attend(queries, fresh_keys, fresh_values, key_rows, values, slot_lengths):
    score_scale = 1.0 / math.sqrt(queries.shape[-1])
    scores = (
        jnp.einsum("rkgd,rktd->rkgt", queries, key_rows, preferred_element_type=jnp.float32)
        * score_scale
    )
    own_score = (
        jnp.einsum("rkgd,rkd->rkg", queries, fresh_keys, preferred_element_type=jnp.float32)
        * score_scale
    )
    positions_row = lax.broadcasted_iota(jnp.int32, (1, 1, 1, key_rows.shape[2]), 3)
    valid_keys = positions_row < slot_lengths[:, None, None, None]
    scores = jnp.where(valid_keys, scores, -jnp.inf)
    highest = jnp.maximum(jnp.max(scores, axis=-1), own_score)
    weights = jnp.exp(scores - highest[..., None])
    own_weight = jnp.exp(own_score - highest)
    denominator = jnp.sum(weights, axis=-1) + own_weight
    rounded = weights.astype(jnp.bfloat16)
    own_rounded = lax.optimization_barrier(own_weight.astype(jnp.bfloat16)).astype(jnp.float32)
    summed = jnp.einsum("rkgt,rktd->rkgd", rounded, values, preferred_element_type=jnp.float32)
    summed = summed + own_rounded[..., None] * fresh_values.astype(jnp.float32)[:, :, None, :]
    return (summed / denominator[..., None]).astype(jnp.bfloat16)


def shards(
    hidden_in, norm_gain, w_query, w_keyval, w_out, cache_slots, lengths, positions, slot_order
):
    total_rows = hidden_in.shape[0]
    data_count = lax.axis_size("dp")
    model_count = lax.axis_size("mp")
    owned_rows = cache_slots.shape[1]
    key_heads = cache_slots.shape[3]
    head_dim = cache_slots.shape[5]
    query_cols = w_query.shape[1]
    head_count = query_cols * model_count // head_dim
    group_size = head_count // key_heads
    model_width = hidden_in.shape[1] * data_count
    half_width = key_heads * head_dim
    inverse = (
        jnp.zeros((total_rows,), jnp.int32)
        .at[slot_order]
        .set(jnp.arange(total_rows, dtype=jnp.int32))
    )
    device_index = lax.axis_index("dp") * model_count + lax.axis_index("mp")
    slot_lengths = lax.dynamic_slice_in_dim(
        jnp.take(lengths, slot_order), device_index * owned_rows, owned_rows
    )
    slot_positions = lax.dynamic_slice_in_dim(
        jnp.take(positions, slot_order), device_index * owned_rows, owned_rows
    )
    gain_float = norm_gain.astype(jnp.float32)
    current = jnp.take(hidden_in, slot_order, axis=0)
    for layer_index in range(LAYERS):
        floats = current.astype(jnp.float32)
        squares = jnp.sum(floats * floats, axis=1)
        scaled = (floats * gain_float).astype(jnp.bfloat16)
        partial_value = jnp.concatenate(
            [
                jnp.dot(scaled, w_query, preferred_element_type=jnp.float32),
                jnp.dot(scaled, w_keyval, preferred_element_type=jnp.float32),
            ],
            axis=1,
        )
        summed = lax.psum_scatter(partial_value, "dp", scatter_dimension=0, tiled=True)
        square_sum = lax.psum_scatter(squares, "dp", scatter_dimension=0, tiled=True)
        inverse_rms = lax.rsqrt(square_sum / model_width + norm_eps)
        projected = summed * inverse_rms[:, None]
        arrived = lax.all_to_all(projected, "mp", split_axis=0, concat_axis=1, tiled=True)
        arrived = arrived.reshape(owned_rows, model_count, projected.shape[1])
        query_part = arrived[:, :, :query_cols].reshape(owned_rows, head_count, head_dim)
        keyval_part = arrived[:, :, query_cols:].reshape(owned_rows, 2 * half_width)
        queries = (
            rotate(query_part, slot_positions)
            .astype(jnp.bfloat16)
            .reshape(owned_rows, key_heads, group_size, head_dim)
        )
        fresh_keys = rotate(
            keyval_part[:, :half_width].reshape(owned_rows, key_heads, head_dim), slot_positions
        ).astype(jnp.bfloat16)
        fresh_values = (
            keyval_part[:, half_width:]
            .reshape(owned_rows, key_heads, head_dim)
            .astype(jnp.bfloat16)
        )
        layer_cache = cache_slots[layer_index]
        attended = attend(
            queries, fresh_keys, fresh_values, layer_cache[:, 0], layer_cache[:, 1], slot_lengths
        )
        attended = attended.reshape(owned_rows, head_count * head_dim)
        returned = lax.all_to_all(attended, "mp", split_axis=1, concat_axis=0, tiled=True)
        partial_out = jnp.dot(
            lax.all_gather(returned, "dp", axis=0, tiled=True),
            w_out,
            preferred_element_type=jnp.float32,
        )
        totals = lax.psum(partial_out, "mp")
        current = (floats + totals).astype(jnp.bfloat16)
    return jnp.take(current, inverse, axis=0)


LINK = jnp.bfloat16


def flipped(at, mask, bits):
    turned_at = 0
    for b in range(bits):
        bit = (at // (1 << b)) % 2
        if (mask >> b) & 1:
            bit = 1 - bit
        turned_at = turned_at + bit * (1 << b)
    return turned_at


def fused_kernel(
    sizes,
    slot_hbm,
    length_hbm,
    position_hbm,
    slot_row_hbm,
    frequency_hbm,
    hidden_hbm,
    gain_hbm,
    wq_hbm,
    wkv_hbm,
    wo_hbm,
    cache_hbm,
    out_ref,
    slot_s,
    length_s,
    position_s,
    slot_row,
    frequency_ref,
    hidden_ref,
    gain_ref,
    wq,
    wkv,
    wo,
    wo_other,
    cache,
    state,
    scaled,
    square_send,
    square_recv,
    sums,
    square_sum_buf,
    gain_rows,
    kv_send,
    kv_recv,
    row_send,
    row_recv,
    fresh_buf,
    stage,
    q_send,
    q_recv,
    att_send,
    gathered,
    att_stage,
    left_send,
    left_recv,
    out_acc,
    first_send,
    first_recv,
    second_send,
    second_recv,
    direct_all,
    sems,
):
    n_dp, n_mp, rows, width, query_cols, keyval_cols, owned, key_heads, head_dim = sizes
    band = rows // n_dp
    chunk = width // n_mp
    group = query_cols // head_dim
    packed = owned * group
    half = n_mp // 2
    side = rows // 2
    d_bits, m_bits = n_dp.bit_length() - 1, n_mp.bit_length() - 1
    f32, bf16 = jnp.float32, jnp.bfloat16
    d = lax.axis_index("dp")
    m = lax.axis_index("mp")
    model_width = width * n_dp
    core = lax.rem(m, 2)
    sibling = m + 1 - 2 * core
    score_scale = 1.0 / math.sqrt(head_dim)
    others = [
        (kd, km) for kd in reversed(range(n_dp)) for km in reversed(range(n_mp)) if kd or km
    ]
    place_of = {
        (kd, km): {"dp": flipped(d, kd, d_bits), "mp": flipped(m, km, m_bits)}
        for kd, km in others
    }

    taken = []

    def fresh_sem():
        taken.append(0)
        return sems.at[len(taken) - 1]

    shallow = width // 4
    small = [
        pltpu.make_async_copy(src, dst, fresh_sem())
        for src, dst in (
            [
                (slot_row_hbm, slot_row),
                (hidden_hbm, hidden_ref),
                (gain_hbm, gain_ref),
                (slot_hbm, slot_s),
                (length_hbm, length_s),
                (position_hbm, position_s),
                (frequency_hbm, frequency_ref),
            ]
        )
    ]
    wkv_load = pltpu.make_async_copy(wkv_hbm, wkv, fresh_sem())
    wq_loads = [
        pltpu.make_async_copy(
            wq_hbm.at[pl.ds(k * shallow, shallow)],
            wq.at[pl.ds(k * shallow, shallow)],
            fresh_sem(),
        )
        for k in range(4)
    ]
    cache_loads = [
        pltpu.make_async_copy(cache_hbm.at[layer], cache.at[layer], fresh_sem())
        for layer in range(LAYERS)
    ]
    wo_sem = fresh_sem()
    wo_loads = [
        pltpu.make_async_copy(wo_hbm.at[:, pl.ds(j * chunk, chunk)], wo.at[j], wo_sem)
        for j in range(n_mp)
    ]
    wo_arrival = pltpu.make_async_copy(wo, wo, wo_sem)
    loads = [cache_loads[0]] + wo_loads + cache_loads[1:]
    for one in small[:3]:
        one.start()
    for one in [wkv_load] + wq_loads:
        one.start()

    barrier = pltpu.get_barrier_semaphore()
    for pair in others:
        pl.semaphore_signal(
            barrier, inc=1, device_id=place_of[pair], device_id_type=pl.DeviceIdType.MESH
        )
    for one in small[3:]:
        one.start()

    for one in small[:3]:
        one.wait()
    sublanes = lax.broadcasted_iota(jnp.int32, (rows, rows), 0)
    place = jnp.where(slot_row[...] == sublanes, 1.0, 0.0).astype(bf16)
    gains = gain_ref[...].astype(f32)
    for c in range(n_mp):
        state[0, c] = (
            lax.dot_general(
                place,
                hidden_ref[:, c * chunk : (c + 1) * chunk],
                (((0,), (0,)), ((), ())),
                preferred_element_type=f32,
            )
            .astype(bf16)
            .reshape(2, side, chunk)
        )

    unsent = []

    def remote(src, dst, ssem, rsem, where):
        copy = pltpu.make_async_remote_copy(
            src_ref=src,
            dst_ref=dst,
            send_sem=ssem,
            recv_sem=rsem,
            device_id=where,
            device_id_type=pl.DeviceIdType.MESH,
        )
        copy.start()
        return copy

    def single(src, dst, where):
        copy = remote(src, dst, fresh_sem(), fresh_sem(), where)
        unsent.append(copy.wait_send)
        return copy

    def whole(ref, sem):
        return pltpu.make_async_copy(ref, ref, sem).wait

    def gather_chunks(layer, places, fresh_start):
        squares = square_sum_buf[...]
        pieces = []
        for c in places:
            floats = state[layer, c].reshape(rows, chunk).astype(f32)
            for t in range(chunk // 128):
                piece = floats[:, t * 128 : (t + 1) * 128]
                pieces.append((piece * gain_rows[c, t]).astype(bf16))
                squares = squares + piece * piece
        square_sum_buf[...] = squares
        depth = len(places) * chunk
        start = places[0] * chunk
        if not isinstance(start, int):
            start = pl.multiple_of(start, chunk)
        left = jnp.concatenate(pieces, axis=1)
        wide = 256
        for b in range(-1, query_cols // wide):
            if b < 0:
                weights = wkv[pl.ds(start, depth), :]
                at = query_cols
                span = keyval_cols
            else:
                weights = wq[pl.ds(start, depth), b * wide : (b + 1) * wide]
                at = b * wide
                span = wide
            product = jnp.dot(left, weights, preferred_element_type=f32)
            if fresh_start:
                sums[:, at : at + span] = product
            else:
                sums[:, at : at + span] += product

    def prepare_rows(layer):
        square_row = jnp.broadcast_to(
            jnp.sum(square_sum_buf[...], axis=1, keepdims=True), (rows, 128)
        )
        product = sums[:, query_cols:].reshape(n_dp, band, keyval_cols)
        kv_send[layer] = product.astype(LINK)
        for i in range(n_dp):
            for j in range(n_mp):
                at = (i * n_mp + j) * owned
                square_send[layer, i, j] = square_row[at : at + owned]

    def prepare_queries(layer):
        for g in range(group):
            stage[:, g, :] = sums[:, g * head_dim : (g + 1) * head_dim]
        q_send[layer] = stage[...].reshape(n_dp * n_mp, packed, head_dim).astype(bf16)

    for c in range(n_mp):
        for t in range(chunk // 128):
            at = c * (chunk // 128) + t
            gain_rows[c, t] = gains[at : at + 1]
    squares = jnp.zeros((rows, 128), f32)
    for c in range(n_mp):
        floats = state[0, c].reshape(rows, chunk).astype(f32)
        for t in range(chunk // 128):
            piece = floats[:, t * 128 : (t + 1) * 128]
            at = c * (chunk // 128) + t
            scaled[:, at * 128 : (at + 1) * 128] = (piece * gain_rows[c, t]).astype(bf16)
            squares = squares + piece * piece
    square_sum_buf[...] = squares
    wkv_load.wait()
    sums[:, query_cols:] = jnp.dot(scaled[...], wkv[...], preferred_element_type=f32)
    prepare_rows(0)
    turns = []
    pl.semaphore_wait(barrier, len(others))

    swap_out, swap_in = fresh_sem(), fresh_sem()
    layer_base = len(taken)
    for layer in range(LAYERS):
        kv_out, kv_in, sq_out, sq_in = fresh_sem(), fresh_sem(), fresh_sem(), fresh_sem()
        for kd in reversed(range(1, n_dp)):
            to = flipped(d, kd, d_bits)
            remote(
                kv_send.at[layer, to], kv_recv.at[layer, kd - 1], kv_out, kv_in, {"dp": to}
            )
        for kd in reversed(range(1, n_dp)):
            to = flipped(d, kd, d_bits)
            remote(
                square_send.at[layer, to, m],
                square_recv.at[layer, kd - 1],
                sq_out,
                sq_in,
                {"dp": to},
            )
        unsent.append(whole(kv_recv.at[layer], kv_out))
        unsent.append(whole(square_recv.at[layer], sq_out))
        if layer == 0:
            for k, one in enumerate(wq_loads):
                one.wait()
                if k == 3:
                    for late in loads:
                        late.start()
                left = scaled[:, k * shallow : (k + 1) * shallow]
                for b in range(query_cols // 256):
                    product = jnp.dot(
                        left,
                        wq[k * shallow : (k + 1) * shallow, b * 256 : (b + 1) * 256],
                        preferred_element_type=f32,
                    )
                    if k == 0:
                        sums[:, b * 256 : (b + 1) * 256] = product
                    else:
                        sums[:, b * 256 : (b + 1) * 256] += product
            prepare_queries(0)
        part = key_heads // 2
        mine = d * n_mp + m
        q_out, q_in = fresh_sem(), [fresh_sem(), fresh_sem()]
        for kd, km in others:
            where = place_of[kd, km]
            remote(
                q_send.at[layer, where["dp"] * n_mp + where["mp"]],
                q_recv.at[layer, mine],
                q_out,
                q_in[km // part],
                where,
            )
        unsent.append(whole(q_recv.at[layer, pl.ds(0, len(others))], q_out))
        q_recv[layer, mine] = q_send[layer, mine]
        if layer == 0:
            for one in small[3:]:
                one.wait()
            for r in range(owned):
                slot = slot_s[(d * n_mp + m) * owned + r]
                at = jnp.full((group, head_dim), position_s[slot], jnp.int32).astype(f32)
                angles = at * frequency_ref[...]
                lane = lax.broadcasted_iota(jnp.int32, (group, head_dim), 1)
                sines = jnp.sin(angles)
                turns.append(
                    (
                        jnp.cos(angles),
                        jnp.where(lane < head_dim // 2, -sines, sines),
                        length_s[slot],
                    )
                )
        whole(kv_recv.at[layer], kv_in)()
        total = sums[pl.ds(pl.multiple_of(d * band, band), band), query_cols:]
        for kd in range(1, n_dp):
            total = total + kv_recv[layer, kd - 1].astype(f32)
        for j in range(n_mp):
            row_send[layer, j] = total[j * owned : (j + 1) * owned]
        row_out, row_in = fresh_sem(), fresh_sem()
        for km in reversed(range(1, n_mp)):
            to = flipped(m, km, m_bits)
            remote(row_send.at[layer, to], row_recv.at[layer, m], row_out, row_in, {"mp": to})
        unsent.append(whole(row_recv.at[layer, pl.ds(0, n_mp - 1)], row_out))
        row_recv[layer, m] = row_send[layer, m]
        if layer == 0:
            wo_arrival.wait()
            for q in range(half):
                remote(
                    wo.at[(1 - core) * half + q],
                    wo_other.at[q],
                    swap_out,
                    swap_in,
                    {"mp": sibling},
                )
            unsent.append(whole(wo_other, swap_out))
        whole(square_recv.at[layer], sq_in)()
        square_sum = square_send[layer, d, m]
        for kd in range(1, n_dp):
            square_sum = square_sum + square_recv[layer, kd - 1]
        inverse_rms = lax.rsqrt(square_sum / model_width + norm_eps)

        def turned(x, r):
            cosines, sines, _ = turns[r]
            return x * cosines + pltpu.roll(x, head_dim // 2, 1) * sines

        cache_loads[layer].wait()
        per = keyval_cols // head_dim
        key_sources = key_heads // per
        first_base = (m // part) * part
        bases = [first_base, part - first_base]
        rests = {}
        for step, base in enumerate(bases):
            count = n_dp * part - (1 if step == 0 else 0)
            whole(q_recv.at[layer, pl.ds(0, count)], q_in[step])()
            raw = q_recv[layer, pl.ds(base, part)].astype(f32)
            for i in range(1, n_dp):
                raw = raw + q_recv[layer, pl.ds(i * n_mp + base, part)].astype(f32)
            raw = raw.reshape(part, owned, group, head_dim)
            for r in range(owned):
                asked = jnp.concatenate(
                    [turned(raw[j, r] * inverse_rms[r : r + 1], r)[None] for j in range(part)],
                    axis=0,
                ).astype(bf16)
                score = (
                    lax.dot_general(
                        asked,
                        cache[layer, r, 0, pl.ds(base, part)],
                        (((2,), (2,)), ((0,), (0,))),
                        preferred_element_type=f32,
                    )
                    * score_scale
                )
                at = lax.broadcasted_iota(jnp.int32, score.shape, 2)
                score = jnp.where(at < turns[r][2], score, -jnp.inf)
                peak = jnp.max(score, axis=2, keepdims=True)
                weights = jnp.exp(score - peak)
                summed = lax.dot_general(
                    weights.astype(bf16),
                    cache[layer, r, 1, pl.ds(base, part)],
                    (((2,), (1,)), ((0,), (0,))),
                    preferred_element_type=f32,
                )
                rests[step, r] = (
                    asked.astype(f32),
                    peak,
                    jnp.sum(weights, axis=2, keepdims=True),
                    summed,
                )
        whole(row_recv.at[layer, pl.ds(0, n_mp - 1)], row_in)()
        for r in range(owned):
            for t in range(per):
                fresh = (
                    row_recv[layer, :, r, t * head_dim : (t + 1) * head_dim]
                    * inverse_rms[r : r + 1]
                )
                keys_fresh = turned(fresh, r)
                for source in range(n_mp):
                    kind = source // key_sources
                    head = (source % key_sources) * per + t
                    row = keys_fresh if kind == 0 else fresh
                    fresh_buf[r, kind, head] = row[source : source + 1]
        at_out, at_in = fresh_sem(), [fresh_sem(), fresh_sem()]
        for step, base in enumerate(bases):
            results = []
            for r in range(owned):
                asked, peak, denominator, summed = rests[step, r]
                fresh_keys = fresh_buf[r, 0, pl.ds(base, part)].astype(bf16).astype(f32)
                fresh_values = fresh_buf[r, 1, pl.ds(base, part)].astype(bf16).astype(f32)
                own_score = jnp.sum(asked * fresh_keys, axis=2, keepdims=True) * score_scale
                highest = jnp.maximum(peak, own_score)
                shrink = jnp.exp(peak - highest)
                own_weight = jnp.exp(own_score - highest)
                own_rounded = own_weight.astype(bf16).astype(f32)
                results.append(
                    (summed * shrink + own_rounded * fresh_values)
                    / (denominator * shrink + own_weight)
                )
            att_send[layer, pl.ds(base, part)] = jnp.concatenate(results, axis=1).astype(bf16)
            for kd, km in sorted(others, key=lambda one: (1, 0, 3, 2).index(one[0])):
                if km // part == step:
                    where = place_of[kd, km]
                    remote(
                        att_send.at[layer, where["mp"]],
                        gathered.at[layer, mine],
                        at_out,
                        at_in[kd // 2],
                        where,
                    )
        unsent.append(whole(gathered.at[layer, pl.ds(0, len(others))], at_out))
        gathered[layer, mine] = att_send[layer, m]
        chip = m // 2
        sides = [d // 2, 1 - d // 2]
        sources = n_dp * n_mp // 2
        first_copies, second_copies, direct_in = [], [], []
        fi_out, se_out, di_out, st_out = fresh_sem(), fresh_sem(), fresh_sem(), fresh_sem()
        unsent.append(whole(first_recv.at[layer], fi_out))
        unsent.append(whole(second_recv.at[layer], se_out))
        unsent.append(whole(direct_all.at[layer, :, pl.ds(0, half - 1)], di_out))
        unsent.append(whole(state.at[layer + 1, pl.ds(0, half)], st_out))
        for h, at_side in enumerate(sides):
            whole(gathered.at[layer, pl.ds(0, sources - 1 + h)], at_in[h])()
            att_stage[...] = (
                gathered[layer, pl.ds(at_side * sources, sources)]
                .astype(f32)
                .reshape(side, group, head_dim)
            )
            left = jnp.concatenate(
                [att_stage[:, g, :].astype(bf16) for g in range(group)], axis=1
            )
            left_send[layer, h] = left
            left_copy = single(left_send.at[layer, h], left_recv.at[layer, h], {"mp": sibling})
            for q in range(half):
                out_acc[q] = jnp.dot(left, wo[core * half + q], preferred_element_type=f32)
            if layer == 0 and h == 0:
                whole(wo_other, swap_in)()
            left_copy.wait_recv()
            other_left = left_recv[layer, h]
            for q in range(half):
                product = jnp.dot(other_left, wo_other[q], preferred_element_type=f32)
                chip_sum = (product + out_acc[q]).astype(LINK)
                if h == 0:
                    first_send[layer, q] = chip_sum
                    first_copies.append(
                        remote(
                            first_send.at[layer, q],
                            first_recv.at[layer, q],
                            fi_out,
                            fresh_sem(),
                            {"mp": flipped(m, 2 if q % 2 == 0 else 4, m_bits)},
                        )
                    )
                else:
                    direct_all[layer, q, chip] = chip_sum
                    di_in = fresh_sem()
                    for k in (3, 1, 2):
                        remote(
                            direct_all.at[layer, q, chip],
                            direct_all.at[layer, q, chip],
                            di_out,
                            di_in,
                            {"mp": flipped(m, 2 * k, m_bits)},
                        )
                    three = direct_all.at[layer, q, pl.ds(0, half - 1)]
                    direct_in.append(whole(three, di_in))
        for q in range(half):
            first_copies[q].wait_recv()
            both = first_send[layer, q].astype(f32) + first_recv[layer, q].astype(f32)
            second_send[layer, q] = both.astype(LINK)
            second_copies.append(
                remote(
                    second_send.at[layer, q],
                    second_recv.at[layer, q],
                    se_out,
                    fresh_sem(),
                    {"mp": flipped(m, 4 if q % 2 == 0 else 2, m_bits)},
                )
            )
        st_in = [fresh_sem() for _ in range(half)]
        if layer + 1 < LAYERS:
            square_sum_buf[...] = jnp.zeros((rows, 128), f32)
        for h, at_side in enumerate(sides):
            for q in range(half):
                at = core * half + q
                if h == 0:
                    second_copies[q].wait_recv()
                    total = second_send[layer, q].astype(f32) + second_recv[layer, q].astype(f32)
                else:
                    direct_in[q]()
                    total = direct_all[layer, q, 0].astype(f32)
                    for c in range(1, n_mp // 2):
                        total = total + direct_all[layer, q, c].astype(f32)
                state[layer + 1, at, at_side] = (
                    state[layer, at, at_side].astype(f32) + total
                ).astype(bf16)
                remote(
                    state.at[layer + 1, at, at_side],
                    state.at[layer + 1, at, at_side],
                    st_out,
                    st_in[q],
                    {"mp": sibling},
                )
        if layer + 1 < LAYERS:
            for q in range(1, half, 2):
                at = core * half + q
                gather_chunks(layer + 1, [at - 1, at], q == 1)
        for q in range(half):
            at = (1 - core) * half + q
            whole(state.at[layer + 1, at], st_in[q])()
            if layer + 1 < LAYERS and q % 2 == 1:
                gather_chunks(layer + 1, [at - 1, at], False)
        if layer + 1 < LAYERS:
            prepare_rows(layer + 1)
            prepare_queries(layer + 1)
            for wait in unsent:
                wait()
            unsent.clear()
            del taken[layer_base:]
    for c in range(n_mp):
        out_ref[:, c * chunk : (c + 1) * chunk] = jnp.dot(
            place, state[LAYERS, c].reshape(rows, chunk), preferred_element_type=f32
        ).astype(bf16)
    for wait in unsent:
        wait()


def fused(
    hidden_in, norm_gain, w_query, w_keyval, w_out, cache_slots, lengths, positions, slot_order
):
    n_dp = lax.axis_size("dp")
    n_mp = lax.axis_size("mp")
    rows, width = hidden_in.shape
    query_cols = w_query.shape[1]
    keyval_cols = w_keyval.shape[1]
    owned, key_heads, cache_rows, head_dim = (
        cache_slots.shape[1],
        cache_slots.shape[3],
        cache_slots.shape[4],
        cache_slots.shape[5],
    )
    group = query_cols // head_dim
    packed = owned * group
    band = rows // n_dp
    chunk = width // n_mp
    half = n_mp // 2
    index_row = np.arange(head_dim) % (head_dim // 2)
    frequency = np.exp(index_row * (-2.0 * math.log(rope_base) / head_dim))
    frequency = jnp.asarray(frequency[None].astype(np.float32))
    sizes = (n_dp, n_mp, rows, width, query_cols, keyval_cols, owned, key_heads, head_dim)
    vmem = pl.BlockSpec(memory_space=pltpu.VMEM)
    anywhere = pl.BlockSpec(memory_space=pl.ANY)
    f32, bf16 = jnp.float32, jnp.bfloat16
    dma = pltpu.SemaphoreType.DMA
    return pl.pallas_call(
        functools.partial(fused_kernel, sizes),
        out_shape=jax.ShapeDtypeStruct((rows, width), bf16),
        in_specs=[anywhere] * 11,
        out_specs=vmem,
        scratch_shapes=[
            pltpu.SMEM((rows,), jnp.int32),
            pltpu.SMEM((rows,), jnp.int32),
            pltpu.SMEM((rows,), jnp.int32),
            pltpu.VMEM((1, rows), jnp.int32),
            pltpu.VMEM((1, head_dim), f32),
            pltpu.VMEM((rows, width), bf16),
            pltpu.VMEM((width // 128, 128), bf16),
            pltpu.VMEM(w_query.shape, bf16),
            pltpu.VMEM(w_keyval.shape, bf16),
            pltpu.VMEM((n_mp, query_cols, chunk), bf16),
            pltpu.VMEM((half, query_cols, chunk), bf16),
            pltpu.VMEM(cache_slots.shape, bf16),
            pltpu.VMEM((LAYERS + 1, n_mp, 2, rows // 2, chunk), bf16),
            pltpu.VMEM((rows, width), bf16),
            pltpu.VMEM((LAYERS, n_dp, n_mp, owned, 128), f32),
            pltpu.VMEM((LAYERS, n_dp - 1, owned, 128), f32),
            pltpu.VMEM((rows, query_cols + keyval_cols), f32),
            pltpu.VMEM((rows, 128), f32),
            pltpu.VMEM((n_mp, chunk // 128, 1, 128), f32),
            pltpu.VMEM((LAYERS, n_dp, band, keyval_cols), LINK),
            pltpu.VMEM((LAYERS, n_dp - 1, band, keyval_cols), LINK),
            pltpu.VMEM((LAYERS, n_mp, owned, keyval_cols), f32),
            pltpu.VMEM((LAYERS, n_mp, owned, keyval_cols), f32),
            pltpu.VMEM((owned, 2, key_heads, 1, head_dim), f32),
            pltpu.VMEM((rows, group, head_dim), f32),
            pltpu.VMEM((LAYERS, n_dp * n_mp, packed, head_dim), LINK),
            pltpu.VMEM((LAYERS, n_dp * n_mp, packed, head_dim), LINK),
            pltpu.VMEM((LAYERS, n_mp, packed, head_dim), bf16),
            pltpu.VMEM((LAYERS, n_dp * n_mp, packed, head_dim), bf16),
            pltpu.VMEM((rows // 2, group, head_dim), f32),
            pltpu.VMEM((LAYERS, 2, rows // 2, query_cols), bf16),
            pltpu.VMEM((LAYERS, 2, rows // 2, query_cols), bf16),
            pltpu.VMEM((half, rows // 2, chunk), f32),
            pltpu.VMEM((LAYERS, half, rows // 2, chunk), LINK),
            pltpu.VMEM((LAYERS, half, rows // 2, chunk), LINK),
            pltpu.VMEM((LAYERS, half, rows // 2, chunk), LINK),
            pltpu.VMEM((LAYERS, half, rows // 2, chunk), LINK),
            pltpu.VMEM((LAYERS, half, half, rows // 2, chunk), LINK),
            dma((60,)),
        ],
        compiler_params=pltpu.CompilerParams(
            collective_id=0, has_side_effects=True, vmem_limit_bytes=56 << 20
        ),
    )(
        slot_order,
        lengths,
        positions,
        slot_order.reshape(1, rows),
        frequency,
        hidden_in,
        norm_gain.reshape(width // 128, 128),
        w_query,
        w_keyval,
        w_out,
        cache_slots,
    )


def dispatch(
    hidden_in, norm_gain, w_query, w_keyval, w_out, cache_slots, lengths, positions, slot_order
):
    n_mp = lax.axis_size("mp")
    key_heads = cache_slots.shape[3]
    head_dim = cache_slots.shape[5]
    fits = (
        key_heads == n_mp
        and n_mp == 8
        and lax.axis_size("dp") == 4
        and cache_slots.shape[1] * (w_query.shape[1] // head_dim) % 16 == 0
        and (w_query.shape[1] // head_dim) == 8
        and w_keyval.shape[1] % head_dim == 0
        and w_query.shape[1] % w_keyval.shape[1] == 0
        and hidden_in.shape[1] % (128 * n_mp) == 0
        and hidden_in.shape[0] % (16 * lax.axis_size("dp")) == 0
    )
    chosen = fused if fits else shards
    return chosen(
        hidden_in, norm_gain, w_query, w_keyval, w_out, cache_slots, lengths, positions, slot_order
    )


def solution(mesh):
    placed = (
        P(None, "dp"),
        P("dp"),
        P("dp", "mp"),
        P("dp", "mp"),
        P("mp", "dp"),
        P(None, ("dp", "mp"), None, None, None, None),
        P(),
        P(),
        P(),
    )
    return jax.shard_map(
        dispatch, mesh=mesh, in_specs=placed, out_specs=P(None, "dp"), check_vma=False
    )
```

```python
import functools
import math

import jax
import jax.numpy as jnp
import numpy as np
from jax import lax
from jax.experimental import pallas as pl
from jax.experimental.pallas import tpu as pltpu
from jax.sharding import PartitionSpec as P

LAYERS = 2


norm_eps = 1e-05
rope_base = 500000.0


def rotate(values, at_positions):
    half_dim = values.shape[-1] // 2
    index_row = jnp.arange(half_dim, dtype=jnp.float32)
    frequency = jnp.exp(index_row * (-2.0 * math.log(rope_base) / values.shape[-1]))
    angles = at_positions.astype(jnp.float32)[:, None, None] * frequency
    cosines = jnp.cos(angles)
    sine_rows = jnp.sin(angles)
    first_half = values[..., :half_dim]
    second_half = values[..., half_dim:]
    return jnp.concatenate(
        [
            first_half * cosines - second_half * sine_rows,
            second_half * cosines + first_half * sine_rows,
        ],
        axis=-1,
    )


def attend(queries, fresh_keys, fresh_values, key_rows, values, slot_lengths):
    score_scale = 1.0 / math.sqrt(queries.shape[-1])
    scores = (
        jnp.einsum("rkgd,rktd->rkgt", queries, key_rows, preferred_element_type=jnp.float32)
        * score_scale
    )
    own_score = (
        jnp.einsum("rkgd,rkd->rkg", queries, fresh_keys, preferred_element_type=jnp.float32)
        * score_scale
    )
    positions_row = lax.broadcasted_iota(jnp.int32, (1, 1, 1, key_rows.shape[2]), 3)
    valid_keys = positions_row < slot_lengths[:, None, None, None]
    scores = jnp.where(valid_keys, scores, -jnp.inf)
    highest = jnp.maximum(jnp.max(scores, axis=-1), own_score)
    weights = jnp.exp(scores - highest[..., None])
    own_weight = jnp.exp(own_score - highest)
    denominator = jnp.sum(weights, axis=-1) + own_weight
    rounded = weights.astype(jnp.bfloat16)
    own_rounded = lax.optimization_barrier(own_weight.astype(jnp.bfloat16)).astype(jnp.float32)
    summed = jnp.einsum("rkgt,rktd->rkgd", rounded, values, preferred_element_type=jnp.float32)
    summed = summed + own_rounded[..., None] * fresh_values.astype(jnp.float32)[:, :, None, :]
    return (summed / denominator[..., None]).astype(jnp.bfloat16)


def shards(
    hidden_in, norm_gain, w_query, w_keyval, w_out, cache_slots, lengths, positions, slot_order
):
    total_rows = hidden_in.shape[0]
    data_count = lax.axis_size("dp")
    model_count = lax.axis_size("mp")
    owned_rows = cache_slots.shape[1]
    key_heads = cache_slots.shape[3]
    head_dim = cache_slots.shape[5]
    query_cols = w_query.shape[1]
    head_count = query_cols * model_count // head_dim
    group_size = head_count // key_heads
    model_width = hidden_in.shape[1] * data_count
    half_width = key_heads * head_dim
    inverse = (
        jnp.zeros((total_rows,), jnp.int32)
        .at[slot_order]
        .set(jnp.arange(total_rows, dtype=jnp.int32))
    )
    device_index = lax.axis_index("dp") * model_count + lax.axis_index("mp")
    slot_lengths = lax.dynamic_slice_in_dim(
        jnp.take(lengths, slot_order), device_index * owned_rows, owned_rows
    )
    slot_positions = lax.dynamic_slice_in_dim(
        jnp.take(positions, slot_order), device_index * owned_rows, owned_rows
    )
    gain_float = norm_gain.astype(jnp.float32)
    current = jnp.take(hidden_in, slot_order, axis=0)
    for layer_index in range(LAYERS):
        floats = current.astype(jnp.float32)
        squares = jnp.sum(floats * floats, axis=1)
        scaled = (floats * gain_float).astype(jnp.bfloat16)
        partial_value = jnp.concatenate(
            [
                jnp.dot(scaled, w_query, preferred_element_type=jnp.float32),
                jnp.dot(scaled, w_keyval, preferred_element_type=jnp.float32),
            ],
            axis=1,
        )
        summed = lax.psum_scatter(partial_value, "dp", scatter_dimension=0, tiled=True)
        square_sum = lax.psum_scatter(squares, "dp", scatter_dimension=0, tiled=True)
        inverse_rms = lax.rsqrt(square_sum / model_width + norm_eps)
        projected = summed * inverse_rms[:, None]
        arrived = lax.all_to_all(projected, "mp", split_axis=0, concat_axis=1, tiled=True)
        arrived = arrived.reshape(owned_rows, model_count, projected.shape[1])
        query_part = arrived[:, :, :query_cols].reshape(owned_rows, head_count, head_dim)
        keyval_part = arrived[:, :, query_cols:].reshape(owned_rows, 2 * half_width)
        queries = (
            rotate(query_part, slot_positions)
            .astype(jnp.bfloat16)
            .reshape(owned_rows, key_heads, group_size, head_dim)
        )
        fresh_keys = rotate(
            keyval_part[:, :half_width].reshape(owned_rows, key_heads, head_dim), slot_positions
        ).astype(jnp.bfloat16)
        fresh_values = (
            keyval_part[:, half_width:]
            .reshape(owned_rows, key_heads, head_dim)
            .astype(jnp.bfloat16)
        )
        layer_cache = cache_slots[layer_index]
        attended = attend(
            queries, fresh_keys, fresh_values, layer_cache[:, 0], layer_cache[:, 1], slot_lengths
        )
        attended = attended.reshape(owned_rows, head_count * head_dim)
        returned = lax.all_to_all(attended, "mp", split_axis=1, concat_axis=0, tiled=True)
        partial_out = jnp.dot(
            lax.all_gather(returned, "dp", axis=0, tiled=True),
            w_out,
            preferred_element_type=jnp.float32,
        )
        totals = lax.psum(partial_out, "mp")
        current = (floats + totals).astype(jnp.bfloat16)
    return jnp.take(current, inverse, axis=0)


LINK = jnp.bfloat16


def flipped(at, mask, bits):
    turned_at = 0
    for b in range(bits):
        bit = (at // (1 << b)) % 2
        if (mask >> b) & 1:
            bit = 1 - bit
        turned_at = turned_at + bit * (1 << b)
    return turned_at


def fused_kernel(
    sizes,
    slot_hbm,
    length_hbm,
    position_hbm,
    slot_row_hbm,
    frequency_hbm,
    hidden_hbm,
    gain_hbm,
    wq_hbm,
    wkv_hbm,
    wo_hbm,
    cache_hbm,
    out_ref,
    slot_s,
    length_s,
    position_s,
    slot_row,
    frequency_ref,
    hidden_ref,
    gain_ref,
    wq,
    wkv,
    wo,
    wo_other,
    cache,
    state,
    scaled,
    square_send,
    square_recv,
    sums,
    square_sum_buf,
    gain_rows,
    kv_send,
    kv_recv,
    row_send,
    row_recv,
    fresh_buf,
    stage,
    q_send,
    q_recv,
    att_send,
    gathered,
    att_stage,
    left_send,
    left_recv,
    out_acc,
    direct_all,
    out_buf,
    sems,
):
    n_dp, n_mp, rows, width, query_cols, keyval_cols, owned, key_heads, head_dim = sizes
    band = rows // n_dp
    chunk = width // n_mp
    group = query_cols // head_dim
    packed = owned * group
    half = n_mp // 2
    side = rows // 2
    d_bits, m_bits = n_dp.bit_length() - 1, n_mp.bit_length() - 1
    f32, bf16 = jnp.float32, jnp.bfloat16
    d = lax.axis_index("dp")
    m = lax.axis_index("mp")
    model_width = width * n_dp
    core = lax.rem(m, 2)
    sibling = m + 1 - 2 * core
    score_scale = 1.0 / math.sqrt(head_dim)
    others = [
        (kd, km) for kd in reversed(range(n_dp)) for km in reversed(range(n_mp)) if kd or km
    ]
    place_of = {
        (kd, km): {"dp": flipped(d, kd, d_bits), "mp": flipped(m, km, m_bits)}
        for kd, km in others
    }

    taken = []

    def fresh_sem():
        taken.append(0)
        return sems.at[len(taken) - 1]

    shallow = width // 4
    small = [
        pltpu.make_async_copy(src, dst, fresh_sem())
        for src, dst in (
            [
                (slot_row_hbm, slot_row),
                (hidden_hbm, hidden_ref),
                (gain_hbm, gain_ref),
                (slot_hbm, slot_s),
                (length_hbm, length_s),
                (position_hbm, position_s),
                (frequency_hbm, frequency_ref),
            ]
        )
    ]
    wkv_load = pltpu.make_async_copy(wkv_hbm, wkv, fresh_sem())
    wq_loads = [
        pltpu.make_async_copy(
            wq_hbm.at[pl.ds(k * shallow, shallow)],
            wq.at[pl.ds(k * shallow, shallow)],
            fresh_sem(),
        )
        for k in range(4)
    ]
    cache_loads = [
        pltpu.make_async_copy(cache_hbm.at[layer], cache.at[layer], fresh_sem())
        for layer in range(LAYERS)
    ]
    wo_sem = fresh_sem()
    wo_loads = [
        pltpu.make_async_copy(wo_hbm.at[:, pl.ds(j * chunk, chunk)], wo.at[j], wo_sem)
        for j in range(n_mp)
    ]
    wo_arrival = pltpu.make_async_copy(wo, wo, wo_sem)
    loads = [cache_loads[0]] + wo_loads + cache_loads[1:]
    for one in small[:3]:
        one.start()
    for one in [wkv_load] + wq_loads:
        one.start()

    barrier = pltpu.get_barrier_semaphore()
    for pair in others:
        pl.semaphore_signal(
            barrier, inc=1, device_id=place_of[pair], device_id_type=pl.DeviceIdType.MESH
        )
    for one in small[3:]:
        one.start()

    for one in small[:3]:
        one.wait()
    sublanes = lax.broadcasted_iota(jnp.int32, (rows, rows), 0)
    place = jnp.where(slot_row[...] == sublanes, 1.0, 0.0).astype(bf16)
    gains = gain_ref[...].astype(f32)
    for c in range(n_mp):
        state[0, c] = (
            lax.dot_general(
                place,
                hidden_ref[:, c * chunk : (c + 1) * chunk],
                (((0,), (0,)), ((), ())),
                preferred_element_type=f32,
            )
            .astype(bf16)
            .reshape(2, side, chunk)
        )

    unsent = []

    def remote(src, dst, ssem, rsem, where):
        copy = pltpu.make_async_remote_copy(
            src_ref=src,
            dst_ref=dst,
            send_sem=ssem,
            recv_sem=rsem,
            device_id=where,
            device_id_type=pl.DeviceIdType.MESH,
        )
        copy.start()
        return copy

    def single(src, dst, where):
        copy = remote(src, dst, fresh_sem(), fresh_sem(), where)
        unsent.append(copy.wait_send)
        return copy

    def whole(ref, sem):
        return pltpu.make_async_copy(ref, ref, sem).wait

    def gather_chunks(layer, places, fresh_start):
        squares = square_sum_buf[...]
        pieces = []
        for c in places:
            floats = state[layer, c].reshape(rows, chunk).astype(f32)
            for t in range(chunk // 128):
                piece = floats[:, t * 128 : (t + 1) * 128]
                pieces.append((piece * gain_rows[c, t]).astype(bf16))
                squares = squares + piece * piece
        square_sum_buf[...] = squares
        depth = len(places) * chunk
        start = places[0] * chunk
        if not isinstance(start, int):
            start = pl.multiple_of(start, chunk)
        left = jnp.concatenate(pieces, axis=1)
        wide = 256
        for b in range(-1, query_cols // wide):
            if b < 0:
                weights = wkv[pl.ds(start, depth), :]
                at = query_cols
                span = keyval_cols
            else:
                weights = wq[pl.ds(start, depth), b * wide : (b + 1) * wide]
                at = b * wide
                span = wide
            product = jnp.dot(left, weights, preferred_element_type=f32)
            if fresh_start:
                sums[:, at : at + span] = product
            else:
                sums[:, at : at + span] += product

    def prepare_rows(layer):
        square_row = jnp.broadcast_to(
            jnp.sum(square_sum_buf[...], axis=1, keepdims=True), (rows, 128)
        )
        product = sums[:, query_cols:].reshape(n_dp, band, keyval_cols)
        kv_send[layer] = product.astype(LINK)
        for i in range(n_dp):
            for j in range(n_mp):
                at = (i * n_mp + j) * owned
                square_send[layer, i, j] = square_row[at : at + owned]

    def prepare_queries(layer):
        for g in range(group):
            stage[:, g, :] = sums[:, g * head_dim : (g + 1) * head_dim]
        q_send[layer] = stage[...].reshape(n_dp * n_mp, packed, head_dim).astype(bf16)

    for c in range(n_mp):
        for t in range(chunk // 128):
            at = c * (chunk // 128) + t
            gain_rows[c, t] = gains[at : at + 1]
    squares = jnp.zeros((rows, 128), f32)
    for c in range(n_mp):
        floats = state[0, c].reshape(rows, chunk).astype(f32)
        for t in range(chunk // 128):
            piece = floats[:, t * 128 : (t + 1) * 128]
            at = c * (chunk // 128) + t
            scaled[:, at * 128 : (at + 1) * 128] = (piece * gain_rows[c, t]).astype(bf16)
            squares = squares + piece * piece
    square_sum_buf[...] = squares
    wkv_load.wait()
    sums[:, query_cols:] = jnp.dot(scaled[...], wkv[...], preferred_element_type=f32)
    prepare_rows(0)
    turns = []
    pl.semaphore_wait(barrier, len(others))

    swap_out, swap_in, out_sem = fresh_sem(), fresh_sem(), fresh_sem()

    def deliver(c):
        out_buf[c] = jnp.dot(
            place, state[LAYERS, c].reshape(rows, chunk), preferred_element_type=f32
        ).astype(bf16)
        pltpu.make_async_copy(
            out_buf.at[c],
            out_ref.at[:, pl.ds(pl.multiple_of(c * chunk, chunk), chunk)],
            out_sem,
        ).start()

    layer_base = len(taken)
    for layer in range(LAYERS):
        kv_out, kv_in, sq_out, sq_in = fresh_sem(), fresh_sem(), fresh_sem(), fresh_sem()
        for kd in reversed(range(1, n_dp)):
            to = flipped(d, kd, d_bits)
            remote(
                kv_send.at[layer, to], kv_recv.at[layer, kd - 1], kv_out, kv_in, {"dp": to}
            )
        for kd in reversed(range(1, n_dp)):
            to = flipped(d, kd, d_bits)
            remote(
                square_send.at[layer, to, m],
                square_recv.at[layer, kd - 1],
                sq_out,
                sq_in,
                {"dp": to},
            )
        unsent.append(whole(kv_recv.at[layer], kv_out))
        unsent.append(whole(square_recv.at[layer], sq_out))
        if layer == 0:
            for k, one in enumerate(wq_loads):
                one.wait()
                if k == 3:
                    for late in loads:
                        late.start()
                left = scaled[:, k * shallow : (k + 1) * shallow]
                for b in range(query_cols // 256):
                    product = jnp.dot(
                        left,
                        wq[k * shallow : (k + 1) * shallow, b * 256 : (b + 1) * 256],
                        preferred_element_type=f32,
                    )
                    if k == 0:
                        sums[:, b * 256 : (b + 1) * 256] = product
                    else:
                        sums[:, b * 256 : (b + 1) * 256] += product
            prepare_queries(0)
        part = key_heads // 2
        mine = d * n_mp + m
        q_out, q_in = fresh_sem(), [fresh_sem(), fresh_sem()]
        for kd, km in others:
            where = place_of[kd, km]
            remote(
                q_send.at[layer, where["dp"] * n_mp + where["mp"]],
                q_recv.at[layer, mine],
                q_out,
                q_in[km // part],
                where,
            )
        unsent.append(whole(q_recv.at[layer, pl.ds(0, len(others))], q_out))
        q_recv[layer, mine] = q_send[layer, mine]
        if layer == 0:
            for one in small[3:]:
                one.wait()
            for r in range(owned):
                slot = slot_s[(d * n_mp + m) * owned + r]
                at = jnp.full((group, head_dim), position_s[slot], jnp.int32).astype(f32)
                angles = at * frequency_ref[...]
                lane = lax.broadcasted_iota(jnp.int32, (group, head_dim), 1)
                sines = jnp.sin(angles)
                turns.append(
                    (
                        jnp.cos(angles),
                        jnp.where(lane < head_dim // 2, -sines, sines),
                        length_s[slot],
                    )
                )
        whole(kv_recv.at[layer], kv_in)()
        total = sums[pl.ds(pl.multiple_of(d * band, band), band), query_cols:]
        for kd in range(1, n_dp):
            total = total + kv_recv[layer, kd - 1].astype(f32)
        for j in range(n_mp):
            row_send[layer, j] = total[j * owned : (j + 1) * owned]
        row_out, row_in = fresh_sem(), fresh_sem()
        for km in reversed(range(1, n_mp)):
            to = flipped(m, km, m_bits)
            remote(row_send.at[layer, to], row_recv.at[layer, m], row_out, row_in, {"mp": to})
        unsent.append(whole(row_recv.at[layer, pl.ds(0, n_mp - 1)], row_out))
        row_recv[layer, m] = row_send[layer, m]
        if layer == 0:
            wo_arrival.wait()
            for q in range(half):
                remote(
                    wo.at[(1 - core) * half + q],
                    wo_other.at[q],
                    swap_out,
                    swap_in,
                    {"mp": sibling},
                )
            unsent.append(whole(wo_other, swap_out))
        whole(square_recv.at[layer], sq_in)()
        square_sum = square_send[layer, d, m]
        for kd in range(1, n_dp):
            square_sum = square_sum + square_recv[layer, kd - 1]
        inverse_rms = lax.rsqrt(square_sum / model_width + norm_eps)

        def turned(x, r):
            cosines, sines, _ = turns[r]
            return x * cosines + pltpu.roll(x, head_dim // 2, 1) * sines

        cache_loads[layer].wait()
        per = keyval_cols // head_dim
        key_sources = key_heads // per
        first_base = (m // part) * part
        bases = [first_base, part - first_base]
        rests = {}
        for step, base in enumerate(bases):
            count = n_dp * part - (1 if step == 0 else 0)
            whole(q_recv.at[layer, pl.ds(0, count)], q_in[step])()
            raw = q_recv[layer, pl.ds(base, part)].astype(f32)
            for i in range(1, n_dp):
                raw = raw + q_recv[layer, pl.ds(i * n_mp + base, part)].astype(f32)
            raw = raw.reshape(part, owned, group, head_dim)
            for r in range(owned):
                asked = jnp.concatenate(
                    [turned(raw[j, r] * inverse_rms[r : r + 1], r)[None] for j in range(part)],
                    axis=0,
                ).astype(bf16)
                score = (
                    lax.dot_general(
                        asked,
                        cache[layer, r, 0, pl.ds(base, part)],
                        (((2,), (2,)), ((0,), (0,))),
                        preferred_element_type=f32,
                    )
                    * score_scale
                )
                at = lax.broadcasted_iota(jnp.int32, score.shape, 2)
                score = jnp.where(at < turns[r][2], score, -jnp.inf)
                peak = jnp.max(score, axis=2, keepdims=True)
                weights = jnp.exp(score - peak)
                summed = lax.dot_general(
                    weights.astype(bf16),
                    cache[layer, r, 1, pl.ds(base, part)],
                    (((2,), (1,)), ((0,), (0,))),
                    preferred_element_type=f32,
                )
                rests[step, r] = (
                    asked.astype(f32),
                    peak,
                    jnp.sum(weights, axis=2, keepdims=True),
                    summed,
                )
        whole(row_recv.at[layer, pl.ds(0, n_mp - 1)], row_in)()
        for r in range(owned):
            for t in range(per):
                fresh = (
                    row_recv[layer, :, r, t * head_dim : (t + 1) * head_dim]
                    * inverse_rms[r : r + 1]
                )
                keys_fresh = turned(fresh, r)
                for source in range(n_mp):
                    kind = source // key_sources
                    head = (source % key_sources) * per + t
                    row = keys_fresh if kind == 0 else fresh
                    fresh_buf[r, kind, head] = row[source : source + 1]
        at_out, at_in = fresh_sem(), [fresh_sem(), fresh_sem()]
        for step, base in enumerate(bases):
            results = []
            for r in range(owned):
                asked, peak, denominator, summed = rests[step, r]
                fresh_keys = fresh_buf[r, 0, pl.ds(base, part)].astype(bf16).astype(f32)
                fresh_values = fresh_buf[r, 1, pl.ds(base, part)].astype(bf16).astype(f32)
                own_score = jnp.sum(asked * fresh_keys, axis=2, keepdims=True) * score_scale
                highest = jnp.maximum(peak, own_score)
                shrink = jnp.exp(peak - highest)
                own_weight = jnp.exp(own_score - highest)
                own_rounded = own_weight.astype(bf16).astype(f32)
                results.append(
                    (summed * shrink + own_rounded * fresh_values)
                    / (denominator * shrink + own_weight)
                )
            att_send[layer, pl.ds(base, part)] = jnp.concatenate(results, axis=1).astype(bf16)
            for kd, km in sorted(others, key=lambda one: (1, 0, 3, 2).index(one[0])):
                if km // part == step:
                    where = place_of[kd, km]
                    remote(
                        att_send.at[layer, where["mp"]],
                        gathered.at[layer, mine],
                        at_out,
                        at_in[kd // 2],
                        where,
                    )
        unsent.append(whole(gathered.at[layer, pl.ds(0, len(others))], at_out))
        gathered[layer, mine] = att_send[layer, m]
        chip = m // 2
        sides = [d // 2, 1 - d // 2]
        sources = n_dp * n_mp // 2
        direct_in = []
        di_out, st_out = fresh_sem(), fresh_sem()
        unsent.append(whole(direct_all.at[layer, :, :, pl.ds(0, half - 1)], di_out))
        unsent.append(whole(state.at[layer + 1, pl.ds(0, half)], st_out))
        for h, at_side in enumerate(sides):
            whole(gathered.at[layer, pl.ds(0, sources - 1 + h)], at_in[h])()
            att_stage[...] = (
                gathered[layer, pl.ds(at_side * sources, sources)]
                .astype(f32)
                .reshape(side, group, head_dim)
            )
            left = jnp.concatenate(
                [att_stage[:, g, :].astype(bf16) for g in range(group)], axis=1
            )
            left_send[layer, h] = left
            left_copy = single(left_send.at[layer, h], left_recv.at[layer, h], {"mp": sibling})
            for q in range(half):
                out_acc[q] = jnp.dot(left, wo[core * half + q], preferred_element_type=f32)
            if layer == 0 and h == 0:
                whole(wo_other, swap_in)()
            left_copy.wait_recv()
            other_left = left_recv[layer, h]
            for q in range(half):
                product = jnp.dot(other_left, wo_other[q], preferred_element_type=f32)
                chip_sum = (product + out_acc[q]).astype(LINK)
                direct_all[layer, h, q, chip] = chip_sum
                di_in = fresh_sem()
                for k in (3, 1, 2):
                    remote(
                        direct_all.at[layer, h, q, chip],
                        direct_all.at[layer, h, q, chip],
                        di_out,
                        di_in,
                        {"mp": flipped(m, 2 * k, m_bits)},
                    )
                direct_in.append(whole(direct_all.at[layer, h, q, pl.ds(0, half - 1)], di_in))
        st_in = [fresh_sem() for _ in range(half)]
        if layer + 1 < LAYERS:
            square_sum_buf[...] = jnp.zeros((rows, 128), f32)
        for h, at_side in enumerate(sides):
            for q in range(half):
                at = core * half + q
                direct_in[h * half + q]()
                total = direct_all[layer, h, q, 0].astype(f32)
                for c in range(1, n_mp // 2):
                    total = total + direct_all[layer, h, q, c].astype(f32)
                state[layer + 1, at, at_side] = (
                    state[layer, at, at_side].astype(f32) + total
                ).astype(bf16)
                remote(
                    state.at[layer + 1, at, at_side],
                    state.at[layer + 1, at, at_side],
                    st_out,
                    st_in[q],
                    {"mp": sibling},
                )
        if layer + 1 < LAYERS:
            for q in range(1, half, 2):
                at = core * half + q
                gather_chunks(layer + 1, [at - 1, at], q == 1)
        else:
            for q in range(half):
                deliver(core * half + q)
        for q in range(half):
            at = (1 - core) * half + q
            whole(state.at[layer + 1, at], st_in[q])()
            if layer + 1 == LAYERS:
                deliver(at)
            if layer + 1 < LAYERS and q % 2 == 1:
                gather_chunks(layer + 1, [at - 1, at], False)
        if layer + 1 < LAYERS:
            prepare_rows(layer + 1)
            prepare_queries(layer + 1)
            for wait in unsent:
                wait()
            unsent.clear()
            del taken[layer_base:]
    unsent.append(whole(out_buf, out_sem))
    for wait in unsent:
        wait()


def fused(
    hidden_in, norm_gain, w_query, w_keyval, w_out, cache_slots, lengths, positions, slot_order
):
    n_dp = lax.axis_size("dp")
    n_mp = lax.axis_size("mp")
    rows, width = hidden_in.shape
    query_cols = w_query.shape[1]
    keyval_cols = w_keyval.shape[1]
    owned, key_heads, cache_rows, head_dim = (
        cache_slots.shape[1],
        cache_slots.shape[3],
        cache_slots.shape[4],
        cache_slots.shape[5],
    )
    group = query_cols // head_dim
    packed = owned * group
    band = rows // n_dp
    chunk = width // n_mp
    half = n_mp // 2
    index_row = np.arange(head_dim) % (head_dim // 2)
    frequency = np.exp(index_row * (-2.0 * math.log(rope_base) / head_dim))
    frequency = jnp.asarray(frequency[None].astype(np.float32))
    sizes = (n_dp, n_mp, rows, width, query_cols, keyval_cols, owned, key_heads, head_dim)
    anywhere = pl.BlockSpec(memory_space=pl.ANY)
    f32, bf16 = jnp.float32, jnp.bfloat16
    dma = pltpu.SemaphoreType.DMA
    return pl.pallas_call(
        functools.partial(fused_kernel, sizes),
        out_shape=jax.ShapeDtypeStruct((rows, width), bf16),
        in_specs=[anywhere] * 11,
        out_specs=anywhere,
        scratch_shapes=[
            pltpu.SMEM((rows,), jnp.int32),
            pltpu.SMEM((rows,), jnp.int32),
            pltpu.SMEM((rows,), jnp.int32),
            pltpu.VMEM((1, rows), jnp.int32),
            pltpu.VMEM((1, head_dim), f32),
            pltpu.VMEM((rows, width), bf16),
            pltpu.VMEM((width // 128, 128), bf16),
            pltpu.VMEM(w_query.shape, bf16),
            pltpu.VMEM(w_keyval.shape, bf16),
            pltpu.VMEM((n_mp, query_cols, chunk), bf16),
            pltpu.VMEM((half, query_cols, chunk), bf16),
            pltpu.VMEM(cache_slots.shape, bf16),
            pltpu.VMEM((LAYERS + 1, n_mp, 2, rows // 2, chunk), bf16),
            pltpu.VMEM((rows, width), bf16),
            pltpu.VMEM((LAYERS, n_dp, n_mp, owned, 128), f32),
            pltpu.VMEM((LAYERS, n_dp - 1, owned, 128), f32),
            pltpu.VMEM((rows, query_cols + keyval_cols), f32),
            pltpu.VMEM((rows, 128), f32),
            pltpu.VMEM((n_mp, chunk // 128, 1, 128), f32),
            pltpu.VMEM((LAYERS, n_dp, band, keyval_cols), LINK),
            pltpu.VMEM((LAYERS, n_dp - 1, band, keyval_cols), LINK),
            pltpu.VMEM((LAYERS, n_mp, owned, keyval_cols), f32),
            pltpu.VMEM((LAYERS, n_mp, owned, keyval_cols), f32),
            pltpu.VMEM((owned, 2, key_heads, 1, head_dim), f32),
            pltpu.VMEM((rows, group, head_dim), f32),
            pltpu.VMEM((LAYERS, n_dp * n_mp, packed, head_dim), LINK),
            pltpu.VMEM((LAYERS, n_dp * n_mp, packed, head_dim), LINK),
            pltpu.VMEM((LAYERS, n_mp, packed, head_dim), bf16),
            pltpu.VMEM((LAYERS, n_dp * n_mp, packed, head_dim), bf16),
            pltpu.VMEM((rows // 2, group, head_dim), f32),
            pltpu.VMEM((LAYERS, 2, rows // 2, query_cols), bf16),
            pltpu.VMEM((LAYERS, 2, rows // 2, query_cols), bf16),
            pltpu.VMEM((half, rows // 2, chunk), f32),
            pltpu.VMEM((LAYERS, 2, half, half, rows // 2, chunk), LINK),
            pltpu.VMEM((n_mp, rows, chunk), bf16),
            dma((52,)),
        ],
        compiler_params=pltpu.CompilerParams(
            collective_id=0, has_side_effects=True, vmem_limit_bytes=56 << 20
        ),
    )(
        slot_order,
        lengths,
        positions,
        slot_order.reshape(1, rows),
        frequency,
        hidden_in,
        norm_gain.reshape(width // 128, 128),
        w_query,
        w_keyval,
        w_out,
        cache_slots,
    )


def dispatch(
    hidden_in, norm_gain, w_query, w_keyval, w_out, cache_slots, lengths, positions, slot_order
):
    n_mp = lax.axis_size("mp")
    key_heads = cache_slots.shape[3]
    head_dim = cache_slots.shape[5]
    fits = (
        key_heads == n_mp
        and n_mp == 8
        and lax.axis_size("dp") == 4
        and cache_slots.shape[1] * (w_query.shape[1] // head_dim) % 16 == 0
        and (w_query.shape[1] // head_dim) == 8
        and w_keyval.shape[1] % head_dim == 0
        and w_query.shape[1] % w_keyval.shape[1] == 0
        and hidden_in.shape[1] % (128 * n_mp) == 0
        and hidden_in.shape[0] % (16 * lax.axis_size("dp")) == 0
    )
    chosen = fused if fits else shards
    return chosen(
        hidden_in, norm_gain, w_query, w_keyval, w_out, cache_slots, lengths, positions, slot_order
    )


def solution(mesh):
    placed = (
        P(None, "dp"),
        P("dp"),
        P("dp", "mp"),
        P("dp", "mp"),
        P("mp", "dp"),
        P(None, ("dp", "mp"), None, None, None, None),
        P(),
        P(),
        P(),
    )
    return jax.shard_map(
        dispatch, mesh=mesh, in_specs=placed, out_specs=P(None, "dp"), check_vma=False
    )
```
